32 devices in a mesh: group: 2 (over y), seq: 4 (over z), shard: 2 (over x), guide: 2 (over core).
Axes of the slice: x: 2, y: 2, z: 4, core: 2. Of those that a mesh axis runs over, the one named last changes fastest.
Arguments:
- queries: bfloat16 [2, 2, 512, 2560], P('guide', 'group', 'seq', 'shard'), parts along dimension 1, may hold values from -120 to 120
- key_vecs: bfloat16 [2, 2, 512, 2560], P('guide', 'group', 'seq', 'shard'), parts along dimension 1, may hold values from -4 to 4
- value_vecs: bfloat16 [2, 2, 512, 2560], P('guide', 'group', 'seq', 'shard'), parts along dimension 1, may hold values from -24 to 24
- residual: bfloat16 [2, 2, 512, 5120], P('guide', 'group', 'seq', 'shard'), parts along dimension 1, may hold values from -64 to 64
- w_out: bfloat16 [2560, 5120], P('shard', 'guide'), may hold values from -0.125 to 0.125
- attn_gate: float32 [2, 5120], P('group', 'shard'), parts along dimension 0, may hold values from 2 to 4
- norm_shift: float32 [2, 5120], P('group', 'shard'), parts along dimension 0, may hold values from -3 to 3
- norm_scale: float32 [2, 5120], P('group', 'shard'), parts along dimension 0, may hold values from -2.5 to 2.5
- w_head: bfloat16 [5120, 64], P('shard'), may hold values from -0.078125 to 0.078125
- noise: float32 [2, 4, 128, 64], P('group', 'seq', None, 'guide'), parts along dimension 0, may hold values from -6 to 6
- timesteps: int32 [2], P('group'), parts along dimension 0, may hold values from 100 to 980
- frame_owner: int32 [2, 4], P('group'), parts along dimension 0, may hold values from 0 to 3, each once within a row
Outputs:
- sds_grad: float32 [2, 4, 128, 64], P('group', 'seq', None, 'guide'), parts along dimension 0
The draws below stay inside these ranges and needn't reach their ends.
There are 2 independent parts, one for each index of `group`. The reference program is written for one: setup_inputs(seed, part) draws one part's arguments, and reference() takes and returns one part's arrays. A program takes and returns all parts, laid end to end along the dimension named above; an argument that names none is the same for every part. Nothing has to cross between parts.
Inputs may be any that keep to these rules, and one draw needn't show every extreme that they name: `frame_owner`: each row names every owner index once.
All inputs are finite; a program needn't handle non-finite values.
Results may differ from the reference program's by a relative error of at most 0.003.
Values may be sent and summed in bfloat16 or wider, within the bound.
No kernel may reach another device: no remote copies, remote signals or barrier semaphores. Data moves between devices by JAX's collectives and lax.ppermute only.
A program may use at most 128 MiB of HBM per device.

```python
import jax
import jax.numpy as jnp
from jax import lax

D = 5120
HEAD_DIM = 128
HEADS = 20
OUT_CH = 64
TSTEPS = 1
SEG = 512
FRAMES = 4
FR_GRP = 32
FTOK = 128
N_SEQ = 4


def attention_pair(base):
    shape = (2, TSTEPS, SEG, HEADS * HEAD_DIM)
    keys_raw = jnp.clip(jax.random.normal(jax.random.fold_in(base, 103), shape, jnp.float32), -4.0, 4.0)
    query_raw = 1.5 * jnp.clip(jax.random.normal(jax.random.fold_in(base, 104), shape, jnp.float32), -4.0, 4.0)
    return (query_raw, keys_raw)


def draw_queries(key, part):
    return attention_pair(key)[0].astype(jnp.bfloat16)


def draw_key_vecs(key, part):
    return attention_pair(key)[1].astype(jnp.bfloat16)


def draw_residual(key, part):
    shape = (2, TSTEPS, SEG, D)
    position = jnp.arange(D, dtype=jnp.int32).astype(jnp.float32) / D
    spread = 0.4 * jnp.exp(jax.random.uniform(jax.random.fold_in(key, 201), (D,), jnp.float32, 0.0, 2.302585))
    rising = jnp.exp(position * 1.098612)
    entries = jnp.clip(jax.random.normal(jax.random.fold_in(key, 203), shape, jnp.float32), -4.0, 4.0)
    return (entries * spread * rising).astype(jnp.bfloat16)


def steps_of(stream_key, dims, split, least, top_value):
    def one(axis_at, blocks):
        draws = jax.random.uniform(jax.random.fold_in(jax.random.fold_in(stream_key, 6), axis_at), (blocks,), jnp.float32, least / len(split), top_value / len(split))
        return jnp.repeat(jnp.exp(draws), dims[axis_at] // blocks).reshape((-1,) + (1,) * (len(dims) - axis_at - 1))

    level = one(*split[0])
    for cut in split[1:]:
        level = level * one(*cut)
    return level


def scatter_about(rng, shape, deviation, most, cuts=(), kind=jnp.bfloat16):
    gain = steps_of(rng, shape, cuts, -0.22, 0.18) if cuts else 1.0
    values = jax.random.normal(rng, shape, jnp.float32) * deviation * gain
    return jnp.minimum(jnp.maximum(values, -most), most).astype(kind)


def setup_inputs(seed: int = 0, part: int = 0) -> dict:
    arg_keys = jax.random.split(jax.random.key(seed), 13)
    own_keys = jax.random.split(jax.random.fold_in(arg_keys[12], part), 13)
    return {
        "queries": draw_queries(jax.random.fold_in(jax.random.fold_in(arg_keys[12], part), 71), part),
        "key_vecs": draw_key_vecs(jax.random.fold_in(jax.random.fold_in(arg_keys[12], part), 71), part),
        "value_vecs": scatter_about(own_keys[2], (2, TSTEPS, SEG, HEADS * HEAD_DIM), 4.0, 24.0, ((0, 2), (2, 4), (3, 2))),
        "residual": draw_residual(jax.random.fold_in(jax.random.fold_in(arg_keys[12], part), 71), part),
        "w_out": scatter_about(arg_keys[4], (HEADS * HEAD_DIM, D), (HEADS * HEAD_DIM) ** -0.5, 0.125, ((0, 2), (1, 2))),
        "attn_gate": jnp.clip(2.0 + 2.0 * jax.random.uniform(own_keys[5], (TSTEPS, D), jnp.float32) ** steps_of(own_keys[5], (TSTEPS, D), ((1, 2),), -0.2, 0.2), 2.0, 4.0),
        "norm_shift": scatter_about(own_keys[6], (TSTEPS, D), 0.5, 3.0, ((1, 2),), jnp.float32),
        "norm_scale": scatter_about(own_keys[7], (TSTEPS, D), 0.5, 2.5, ((1, 2),), jnp.float32),
        "w_head": scatter_about(arg_keys[8], (D, OUT_CH), D ** -0.5, 0.078125, ((0, 2),)),
        "noise": scatter_about(own_keys[9], (TSTEPS, FRAMES, FTOK, OUT_CH), 1.0, 6.0, ((1, 4), (3, 2)), jnp.float32),
        "timesteps": jax.random.randint(own_keys[10], (TSTEPS,), 100, 981).astype(jnp.int32),
        "frame_owner": jax.vmap(lambda own: jax.random.permutation(own, FRAMES))(jax.random.split(own_keys[11], TSTEPS)).reshape((TSTEPS, FRAMES)).astype(jnp.int32),
    }


beta_low = 0.0001
beta_high = 0.02
guidance_scale = 3.0
norm_epsilon = 1e-06

def plan_weight(timesteps):
    steps_float = timesteps.astype(jnp.float32)
    exponent = (steps_float + 1.0) * beta_low + (beta_high - beta_low) * steps_float * (steps_float + 1.0) / (2.0 * 999.0)
    return 1.0 - jnp.exp(-exponent)

def attend_head(operands):
    query_one, key_one, value_one = operands
    query_float = query_one.astype(jnp.float32)
    key_float = key_one.astype(jnp.float32)
    value_float = value_one.astype(jnp.float32)
    scores = jnp.einsum('qd,kd->qk', query_float, key_float) * HEAD_DIM ** (-0.5)
    highest = lax.optimization_barrier(jnp.max(scores, axis=-1, keepdims=True))
    expo = jnp.exp(scores - highest)
    denominator = lax.optimization_barrier(jnp.sum(expo, axis=-1))
    rounded = expo.astype(jnp.bfloat16).astype(jnp.float32)
    mixed = jnp.einsum('qk,kd->qd', rounded, value_float) / denominator[:, None]
    return mixed.astype(jnp.bfloat16)

def split_heads(array):
    return array.reshape(2 * TSTEPS, SEG, HEADS, HEAD_DIM).transpose(0, 2, 1, 3).reshape(2 * TSTEPS * HEADS, SEG, HEAD_DIM)

def reference(queries, key_vecs, value_vecs, residual, w_out, attn_gate, norm_shift, norm_scale, w_head, noise, timesteps, frame_owner):
    width_heads = HEADS * HEAD_DIM
    stacked = (split_heads(queries), split_heads(key_vecs), split_heads(value_vecs))
    per_head = lax.map(attend_head, stacked)
    attended = per_head.reshape(2 * TSTEPS, HEADS, SEG, HEAD_DIM).transpose(0, 2, 1, 3).reshape(2 * TSTEPS * SEG, width_heads)
    projected = jnp.dot(attended, w_out, preferred_element_type=jnp.float32)
    hidden = residual.astype(jnp.float32) + attn_gate[None, :, None, :] * projected.reshape(2, TSTEPS, SEG, D)
    mean_row = lax.optimization_barrier(jnp.mean(hidden, axis=-1, keepdims=True))
    var_row = lax.optimization_barrier(jnp.mean(hidden * hidden, axis=-1, keepdims=True)) - mean_row * mean_row
    modulated = (hidden - mean_row) * lax.rsqrt(var_row + norm_epsilon) * (1.0 + norm_scale[None, :, None, :]) + norm_shift[None, :, None, :]
    predicted = jnp.dot(modulated.reshape(2 * TSTEPS * SEG, D), w_head.astype(jnp.float32), precision=lax.Precision.HIGHEST).reshape(2, TSTEPS, SEG, OUT_CH)
    guided = predicted[1] + guidance_scale * (predicted[0] - predicted[1])
    framed = guided.reshape(TSTEPS, N_SEQ, N_SEQ, FR_GRP, OUT_CH).transpose(0, 2, 1, 3, 4).reshape(TSTEPS, FRAMES, FTOK, OUT_CH)
    owner_table = (frame_owner[:, :, None] == jnp.arange(FRAMES, dtype=jnp.int32)[None, None, :]).astype(jnp.float32)
    by_owner = jnp.einsum('tfo,tfgc->togc', owner_table, framed, precision=lax.Precision.HIGHEST)
    weight = plan_weight(timesteps)
    return weight[:, None, None, None] * (by_owner - noise)
```

```python
import functools

import jax
import jax.numpy as jnp
from jax import lax
from jax.experimental import pallas as pl
from jax.experimental.pallas import tpu as pltpu
from jax.sharding import PartitionSpec as P

HEAD_DIM = 128
LANES = 128
SUBLANES = 8
beta_low = 0.0001
beta_high = 0.02
guidance_scale = 3.0
norm_epsilon = 1e-06
LOG2E = 1.4426950408889634

F32 = jnp.float32
BF16 = jnp.bfloat16
VMEM_SPEC = pl.BlockSpec(memory_space=pltpu.VMEM)
SMEM_SPEC = pl.BlockSpec(memory_space=pltpu.SMEM)
ANY_SPEC = pl.BlockSpec(memory_space=pl.ANY)


def plan_weight(timesteps):
    steps_float = timesteps.astype(jnp.float32)
    exponent = (steps_float + 1.0) * beta_low + (beta_high - beta_low) * steps_float * (
        steps_float + 1.0
    ) / (2.0 * 999.0)
    return 1.0 - jnp.exp(-exponent)


def attend_all(query_split, keys_all, values_all):
    heads_local = query_split.shape[2]
    keys_split = keys_all.reshape(keys_all.shape[0], keys_all.shape[1], heads_local, HEAD_DIM)
    values_split = values_all.reshape(values_all.shape[0], values_all.shape[1], heads_local, HEAD_DIM)
    scores = jnp.einsum(
        "tqhd,tkhd->tqhk", query_split, keys_split, preferred_element_type=F32
    ) * HEAD_DIM ** (-0.5)
    expo = jnp.exp(scores - jnp.max(scores, axis=-1, keepdims=True))
    total = jnp.sum(expo, axis=-1)
    mixed = jnp.einsum("tqhk,tkhd->tqhd", expo.astype(BF16), values_split, preferred_element_type=F32)
    return (mixed / total[..., None]).astype(BF16)


def general_plan(
    queries, key_vecs, value_vecs, residual, w_out, attn_gate, norm_shift, norm_scale, w_head, noise,
    timesteps, frame_owner,
):
    query_local = queries[0]
    step_count, token_count, width_local = query_local.shape
    heads_local = width_local // HEAD_DIM
    attended = attend_all(
        query_local.reshape(step_count, token_count, heads_local, HEAD_DIM),
        lax.all_gather(key_vecs[0], "seq", axis=1, tiled=True),
        lax.all_gather(value_vecs[0], "seq", axis=1, tiled=True),
    )
    row_count = step_count * token_count
    both_rows = jnp.dot(
        lax.all_gather(attended.reshape(row_count, width_local), "guide", axis=0, tiled=True),
        w_out,
        preferred_element_type=F32,
    )
    half_width = w_out.shape[1]
    swapped = lax.all_to_all(
        both_rows.reshape(2, row_count, half_width), "guide", split_axis=0, concat_axis=2, tiled=True
    )
    projected = swapped.reshape(row_count, 2 * half_width)
    attn_out = lax.psum_scatter(projected, "shard", scatter_dimension=1, tiled=True)
    width_shard = attn_out.shape[1]
    width_model = width_shard * lax.axis_size("shard")
    hidden = residual[0].astype(F32) + attn_gate[:, None, :] * attn_out.reshape(
        step_count, token_count, width_shard
    )
    sum_first, sum_second = lax.psum((jnp.sum(hidden, axis=-1), jnp.sum(hidden * hidden, axis=-1)), "shard")
    mean_row = sum_first / width_model
    var_row = sum_second / width_model - mean_row * mean_row
    inv_std = lax.rsqrt(var_row + norm_epsilon)
    modulated = (hidden - mean_row[..., None]) * inv_std[..., None] * (
        1.0 + norm_scale[:, None, :]
    ) + norm_shift[:, None, :]
    partial_head = jnp.einsum(
        "tqd,dc->tqc", modulated, w_head.astype(F32), precision=lax.Precision.HIGHEST
    )
    predicted = lax.psum(partial_head, "shard")
    seq_count = lax.axis_size("seq")
    frame_group = token_count // seq_count
    frames_view = predicted.reshape(step_count, seq_count, frame_group, predicted.shape[-1])
    owner_table = (
        frame_owner[:, :, None] == jnp.arange(seq_count, dtype=jnp.int32)[None, None, :]
    ).astype(F32)
    by_owner = jnp.einsum("tfo,tfgc->togc", owner_table, frames_view, precision=lax.Precision.HIGHEST)
    arrived = lax.all_to_all(
        lax.all_to_all(by_owner[None], "seq", split_axis=2, concat_axis=3, tiled=True),
        "guide",
        split_axis=4,
        concat_axis=0,
        tiled=True,
    )
    guided = arrived[1] + guidance_scale * (arrived[0] - arrived[1])
    return plan_weight(timesteps)[:, None, None, None] * (guided - noise)


def pack_kernel(parts, half, q_ref, k_ref, v_ref, *out_refs):
    z = lax.axis_index("seq")
    for j in range(parts):
        start = pl.multiple_of(lax.rem(z + j, parts) * half, LANES)
        out_refs[j][0] = k_ref[:, pl.ds(start, half)]
        out_refs[j][1] = v_ref[:, pl.ds(start, half)]
        out_refs[parts + j][...] = q_ref[:, pl.ds(start, half)]


def attend_kernel(parts, *refs):
    q_refs = refs[:parts]
    kv_refs = refs[parts : 3 * parts]
    o_refs = refs[3 * parts :]
    rows = q_refs[0].shape[0]
    for i in range(q_refs[0].shape[1] // HEAD_DIM):
        cols = slice(i * HEAD_DIM, (i + 1) * HEAD_DIM)
        q = jnp.concatenate([r[:, cols] for r in q_refs], axis=0)
        k = jnp.concatenate([r[0, :, cols] for r in kv_refs], axis=0)
        v = jnp.concatenate([r[1, :, cols] for r in kv_refs], axis=0)
        scores = lax.dot_general(q, k, (((1,), (1,)), ((), ())), preferred_element_type=F32)
        scores = scores * (HEAD_DIM ** (-0.5) * LOG2E)
        expo = jnp.exp2(scores - jnp.max(scores, axis=1, keepdims=True))
        total = jnp.sum(expo, axis=1, keepdims=True)
        mixed = jnp.dot(expo.astype(BF16), v, preferred_element_type=F32) / total
        for j in range(parts):
            o_refs[j][:, cols] = mixed[j * rows : (j + 1) * rows].astype(BF16)


def load_weights(parts, half, chunk, take_own, own_ref, other_ref, w_scr, sems):
    z = lax.axis_index("seq")
    copies = []
    for t in range(w_scr.shape[0]):
        for j in range(parts):
            start = pl.multiple_of(lax.rem(z + j, parts) * half, LANES)
            src = (pl.ds(start, half), pl.ds(t * chunk, chunk))
            dst = w_scr.at[t, pl.ds(j * half, half), :]
            copies.append((t, src, dst, sems.at[t, j]))

    @pl.when(take_own)
    def _():
        for _, src, dst, sem in copies:
            pltpu.make_async_copy(own_ref.at[src], dst, sem).start()

    @pl.when(jnp.logical_not(take_own))
    def _():
        for _, src, dst, sem in copies:
            pltpu.make_async_copy(other_ref.at[src], dst, sem).start()

    def wait(t):
        for tt, src, dst, sem in copies:
            if tt == t:
                pltpu.make_async_copy(own_ref.at[src], dst, sem).wait()

    return wait


def project(parts, half, o_refs, w_scr, t):
    total = None
    for j in range(parts):
        term = jnp.dot(o_refs[j][...], w_scr[t, j * half : (j + 1) * half, :], preferred_element_type=F32)
        total = term if total is None else total + term
    return total


def send_kernel(parts, half, chunk, first, count, *refs):
    o_refs = refs[:parts]
    own_ref, other_ref, out_ref, w_scr, sems = refs[parts:]
    take_own = lax.axis_index("guide") != lax.axis_index("shard")
    wait = load_weights(
        parts, half, chunk, take_own,
        own_ref.at[:, pl.ds(first, count)], other_ref.at[:, pl.ds(first, count)], w_scr, sems,
    )
    for t in range(w_scr.shape[0]):
        wait(t)
        out_ref[:, t * chunk : (t + 1) * chunk] = project(parts, half, o_refs, w_scr, t).astype(BF16)


def keep_kernel(parts, half, chunk, *refs):
    o_refs = refs[:parts]
    own_ref, other_ref, res_ref, gate_ref, out_ref, w_scr, sems = refs[parts:]
    take_own = lax.axis_index("guide") == lax.axis_index("shard")
    wait = load_weights(parts, half, chunk, take_own, own_ref, other_ref, w_scr, sems)
    for t in range(w_scr.shape[0]):
        cols = slice(t * chunk, (t + 1) * chunk)
        wait(t)
        out_ref[:, cols] = res_ref[:, cols].astype(F32) + gate_ref[:, cols] * project(
            parts, half, o_refs, w_scr, t
        )


def split_dot(head_t, rows):
    dims = (((1,), (1,)), ((), ()))
    high = rows.astype(BF16)
    low = (rows - high.astype(F32)).astype(BF16)
    return lax.dot_general(head_t, high, dims, preferred_element_type=F32) + lax.dot_general(
        head_t, low, dims, preferred_element_type=F32
    )


def head_rows_kernel(scale_ref, shift_ref, head_ref, out_ref):
    width = scale_ref.shape[1]
    which = lax.broadcasted_iota(jnp.int32, (LANES, width), 0)
    rows = jnp.where(which == 0, 1.0 + scale_ref[...], shift_ref[...])
    high = rows.astype(BF16)
    rest = rows - high.astype(F32)
    mid = rest.astype(BF16)
    low = (rest - mid.astype(F32)).astype(BF16)
    dims = (((1,), (1,)), ((), ()))
    total = None
    for part in (high, mid, low):
        term = lax.dot_general(head_ref[...], part, dims, preferred_element_type=F32)
        total = term if total is None else total + term
    out_ref[...] = total


def head_kernel(first, last, chunk, *refs):
    hid_ref, got_ref, gate_ref, scale_ref, head_ref = refs[:5]
    if first:
        out_refs = refs[5:]
    else:
        prev_refs, out_refs = refs[5:8], refs[8:]
    channels = head_ref.shape[0]
    rows = hid_ref.shape[0]
    acc_one = jnp.zeros((rows, LANES), F32) if first else prev_refs[1][...]
    acc_two = jnp.zeros((rows, LANES), F32) if first else prev_refs[2][...]
    acc_head = jnp.zeros((channels, rows), F32) if first else prev_refs[0][...]
    for t in range(hid_ref.shape[1] // chunk):
        cols = slice(t * chunk, (t + 1) * chunk)
        hidden = hid_ref[:, cols] + gate_ref[:, cols] * got_ref[:, cols].astype(F32)
        for s in range(chunk // LANES):
            piece = hidden[:, s * LANES : (s + 1) * LANES]
            acc_one = acc_one + piece
            acc_two = acc_two + piece * piece
        acc_head = acc_head + split_dot(head_ref[:, cols], hidden * (1.0 + scale_ref[:, cols]))
    if last:
        out_ref = out_refs[0]
        out_ref[0:channels, :] = acc_head
        sum_one = jnp.sum(acc_one.T, axis=0, keepdims=True)
        sum_two = jnp.sum(acc_two.T, axis=0, keepdims=True)
        row = lax.broadcasted_iota(jnp.int32, (SUBLANES, rows), 0)
        out_ref[channels : channels + SUBLANES, :] = jnp.where(row == 0, sum_one, sum_two)
    else:
        out_refs[0][...] = acc_head
        out_refs[1][...] = acc_one
        out_refs[2][...] = acc_two


def norm_kernel(width_model, own_ref, got_ref, rows_own_ref, rows_got_ref, keep_ref, send_ref, eps_scr):
    channels = rows_own_ref.shape[0]
    half_channels = channels // 2
    guide = lax.axis_index("guide")
    head = own_ref[0:channels, :] + got_ref[0:channels, :]
    stats = own_ref[channels : channels + SUBLANES, :] + got_ref[channels : channels + SUBLANES, :]
    mean = stats[0:1] / width_model
    var = stats[1:2] / width_model - mean * mean
    inv_std = lax.rsqrt(var + norm_epsilon)
    scaled = rows_own_ref[:, 0:1] + rows_got_ref[:, 0:1]
    shifted = rows_own_ref[:, 1:2] + rows_got_ref[:, 1:2]
    eps_scr[...] = (head - mean * scaled) * inv_std + shifted
    keep_ref[...] = eps_scr[pl.ds(pl.multiple_of(guide * half_channels, SUBLANES), half_channels), :]
    send_ref[...] = eps_scr[pl.ds(pl.multiple_of((1 - guide) * half_channels, SUBLANES), half_channels), :]


def frame_kernel(seq_count, group, owner_ref, keep_ref, got_ref, *out_refs):
    z = lax.axis_index("seq")
    first = lax.axis_index("guide") == 0
    mine, other = keep_ref[...], got_ref[...]
    eps_cond = jnp.where(first, mine, other)
    eps_free = jnp.where(first, other, mine)
    guided = eps_free + guidance_scale * (eps_cond - eps_free)
    fold = LANES // group
    rows = guided.shape[0] // fold
    lane = lax.broadcasted_iota(jnp.int32, (rows, LANES), 1) // group
    for k in range(seq_count):
        target = lax.rem(z + k, seq_count)
        frame = jnp.int32(0)
        for f in range(seq_count):
            frame = jnp.where(owner_ref[0, f] == target, f, frame)
        packed = jnp.zeros((rows, LANES), F32)
        for j in range(fold):
            shift = lax.rem((j - frame) * group + LANES, LANES)
            rolled = pltpu.roll(guided[j * rows : (j + 1) * rows], shift, axis=1)
            packed = jnp.where(lane == j, rolled, packed)
        out_refs[k][...] = packed


def final_kernel(seq_count, group, steps_ref, noise_ref, *refs):
    piece_refs, out_ref = refs[:seq_count], refs[seq_count]
    z = lax.axis_index("seq")
    fold = LANES // group
    rows = piece_refs[0].shape[0]
    lane = lax.broadcasted_iota(jnp.int32, (rows, LANES), 1) // group
    blocks = []
    for j in range(fold):
        block = jnp.zeros((rows, LANES), F32)
        for k in range(seq_count):
            source = lax.rem(z - k + seq_count, seq_count)
            shift = lax.rem((source - j) * group + LANES, LANES)
            block = jnp.where(lane == source, pltpu.roll(piece_refs[k][...], shift, axis=1), block)
        blocks.append(block)
    pad = jnp.zeros((LANES - rows * fold, LANES), F32)
    framed = jnp.concatenate(blocks + [pad], axis=0).T[:, 0 : rows * fold]
    step = jnp.full((1, 1), steps_ref[0], jnp.int32)
    out_ref[...] = plan_weight(step) * (framed - noise_ref[...])


def call(kernel, outs, args, specs=None, scratch=(), flops=0, moved=0):
    shapes = [jax.ShapeDtypeStruct(s, d) for s, d in outs]
    return pl.pallas_call(
        kernel,
        out_shape=shapes,
        in_specs=specs or [VMEM_SPEC] * len(args),
        out_specs=[VMEM_SPEC] * len(outs),
        scratch_shapes=list(scratch),
        cost_estimate=pl.CostEstimate(flops=flops, bytes_accessed=moved, transcendentals=0),
    )(*args)


def fast_plan(
    queries, key_vecs, value_vecs, residual, w_out, attn_gate, norm_shift, norm_scale, w_head, noise,
    timesteps, frame_owner,
):
    seq_count = lax.axis_size("seq")
    parts = seq_count // 2
    rows, width_local = queries.shape[2:]
    half = width_local // parts
    width_shard = residual.shape[3]
    channels = w_head.shape[1]
    group = rows // seq_count
    width_model = float(width_shard * lax.axis_size("shard"))
    both = [(0, 1), (1, 0)]

    other_w = lax.ppermute(w_out, "guide", both)

    packed = call(
        functools.partial(pack_kernel, parts, half),
        [((2, rows, half), BF16)] * parts + [((rows, half), BF16)] * parts,
        [queries[0, 0], key_vecs[0, 0], value_vecs[0, 0]],
        moved=12 * rows * width_local,
    )
    there = [
        [
            (z * 2 + c, (parts * c + (z + j) % parts) * 2 + z // parts)
            for z in range(seq_count)
            for c in range(2)
        ]
        for j in range(parts)
    ]
    back = [[(b, a) for a, b in pairs] for pairs in there]
    axes = ("seq", "guide")
    kv_own = [lax.ppermute(packed[j], axes, there[j]) for j in range(parts)]
    q_own = [lax.ppermute(packed[parts + j], axes, there[j]) for j in range(parts)]
    kv_other = [lax.ppermute(block, "guide", both) for block in kv_own]

    head_t = w_head.T
    rows_own = call(
        head_rows_kernel, [((channels, LANES), F32)], [norm_scale, norm_shift, head_t],
        moved=4 * width_shard * LANES,
    )[0]
    rows_got = lax.ppermute(rows_own, "shard", both)

    mixed = call(
        functools.partial(attend_kernel, parts),
        [((rows, half), BF16)] * parts,
        q_own + kv_own + kv_other,
        flops=8 * rows * parts * rows * parts * half,
        moved=2 * rows * half * parts * 6,
    )
    mixed = [lax.ppermute(mixed[j], axes, back[j]) for j in range(parts)]

    chunk = 256
    pieces = 2
    width_piece = width_shard // pieces
    tiles = width_piece // chunk
    got = []
    for i in range(pieces):
        partial = call(
            functools.partial(send_kernel, parts, half, chunk, i * width_piece, width_piece),
            [((rows, width_piece), BF16)],
            mixed + [w_out, other_w],
            [VMEM_SPEC] * parts + [ANY_SPEC] * 2,
            [
                pltpu.VMEM((tiles, width_local, chunk), BF16),
                pltpu.SemaphoreType.DMA((tiles, parts)),
            ],
            flops=2 * rows * width_local * width_piece,
            moved=2 * width_local * width_piece,
        )[0]
        got.append(lax.ppermute(partial, "shard", both))
    hidden = call(
        functools.partial(keep_kernel, parts, half, chunk),
        [((rows, width_shard), F32)],
        mixed + [w_out, other_w, residual[0, 0], attn_gate],
        [VMEM_SPEC] * parts + [ANY_SPEC] * 2 + [VMEM_SPEC] * 2,
        [
            pltpu.VMEM((tiles * pieces, width_local, chunk), BF16),
            pltpu.SemaphoreType.DMA((tiles * pieces, parts)),
        ],
        flops=2 * rows * width_local * width_shard,
        moved=2 * width_local * width_shard,
    )[0]
    state = []
    for i in range(pieces):
        first, last = i == 0, i == pieces - 1
        cols = slice(i * width_piece, (i + 1) * width_piece)
        state = call(
            functools.partial(head_kernel, first, last, chunk),
            [((channels + SUBLANES, rows), F32)]
            if last
            else [((channels, rows), F32), ((rows, LANES), F32), ((rows, LANES), F32)],
            [hidden[:, cols], got[i], attn_gate[:, cols], norm_scale[:, cols], head_t[:, cols]] + list(state),
            flops=4 * rows * channels * width_piece,
            moved=6 * rows * width_piece,
        )
    sums = state[0]
    sums_got = lax.ppermute(sums, "shard", both)
    keep, send = call(
        functools.partial(norm_kernel, width_model),
        [((channels // 2, rows), F32)] * 2,
        [sums, sums_got, rows_own, rows_got],
        scratch=[pltpu.VMEM((channels, rows), F32)],
    )
    eps_got = lax.ppermute(send, "guide", both)
    fold = LANES // group
    frames = call(
        functools.partial(frame_kernel, seq_count, group),
        [((channels // 2 // fold, LANES), F32)] * seq_count,
        [frame_owner, keep, eps_got],
        [SMEM_SPEC, VMEM_SPEC, VMEM_SPEC],
    )
    arrived = [frames[0]] + [
        lax.ppermute(frames[k], "seq", [(z, (z + k) % seq_count) for z in range(seq_count)])
        for k in range(1, seq_count)
    ]
    out = call(
        functools.partial(final_kernel, seq_count, group),
        [((rows, channels // 2), F32)],
        [timesteps, noise[0, 0]] + arrived,
        [SMEM_SPEC] + [VMEM_SPEC] * (seq_count + 1),
    )[0]
    return out[None, None]


def fast_fits(sizes, queries, residual, w_out, w_head):
    seq_count = sizes["seq"]
    step_count, rows, width_local = queries.shape[1:]
    channels = w_head.shape[1]
    if sizes["guide"] != 2 or sizes["shard"] != 2 or seq_count % 2 or step_count != 1 or rows != LANES:
        return False
    if width_local % (seq_count // 2 * HEAD_DIM) or residual.shape[3] % (4 * LANES):
        return False
    if w_out.shape[1] != residual.shape[3] or channels % (2 * SUBLANES):
        return False
    group = rows // seq_count
    if rows % seq_count or LANES % group:
        return False
    fold = LANES // group
    return channels // 2 % (fold * SUBLANES) == 0


def solution(mesh):
    sizes = dict(mesh.shape)

    def on_device(queries, key_vecs, value_vecs, residual, w_out, attn_gate, norm_shift, norm_scale, w_head, *rest):
        fits = fast_fits(sizes, queries, residual, w_out, w_head)
        plan = fast_plan if fits else general_plan
        return plan(
            queries, key_vecs, value_vecs, residual, w_out, attn_gate, norm_shift, norm_scale, w_head, *rest
        )

    return jax.shard_map(
        on_device,
        mesh=mesh,
        in_specs=(
            P("guide", "group", "seq", "shard"),
            P("guide", "group", "seq", "shard"),
            P("guide", "group", "seq", "shard"),
            P("guide", "group", "seq", "shard"),
            P("shard", "guide"),
            P("group", "shard"),
            P("group", "shard"),
            P("group", "shard"),
            P("shard", None),
            P("group", "seq", None, "guide"),
            P("group"),
            P("group", None),
        ),
        out_specs=P("group", "seq", None, "guide"),
        check_vma=False,
    )
```

```python
import functools

import jax
import jax.numpy as jnp
from jax import lax
from jax.experimental import pallas as pl
from jax.experimental.pallas import tpu as pltpu
from jax.sharding import PartitionSpec as P

HEAD_DIM = 128
LANES = 128
SUBLANES = 8
beta_low = 0.0001
beta_high = 0.02
guidance_scale = 3.0
norm_epsilon = 1e-06
LOG2E = 1.4426950408889634


F32 = jnp.float32
BF16 = jnp.bfloat16
VMEM_SPEC = pl.BlockSpec(memory_space=pltpu.VMEM)
SMEM_SPEC = pl.BlockSpec(memory_space=pltpu.SMEM)
ANY_SPEC = pl.BlockSpec(memory_space=pl.ANY)


def plan_weight(timesteps):
    steps_float = timesteps.astype(jnp.float32)
    exponent = (steps_float + 1.0) * beta_low + (beta_high - beta_low) * steps_float * (
        steps_float + 1.0
    ) / (2.0 * 999.0)
    return 1.0 - jnp.exp(-exponent)


def attend_all(query_split, keys_all, values_all):
    heads_local = query_split.shape[2]
    keys_split = keys_all.reshape(keys_all.shape[0], keys_all.shape[1], heads_local, HEAD_DIM)
    values_split = values_all.reshape(values_all.shape[0], values_all.shape[1], heads_local, HEAD_DIM)
    scores = jnp.einsum(
        "tqhd,tkhd->tqhk", query_split, keys_split, preferred_element_type=F32
    ) * HEAD_DIM ** (-0.5)
    expo = jnp.exp(scores - jnp.max(scores, axis=-1, keepdims=True))
    total = jnp.sum(expo, axis=-1)
    mixed = jnp.einsum("tqhk,tkhd->tqhd", expo.astype(BF16), values_split, preferred_element_type=F32)
    return (mixed / total[..., None]).astype(BF16)


def general_plan(
    queries, key_vecs, value_vecs, residual, w_out, attn_gate, norm_shift, norm_scale, w_head, noise,
    timesteps, frame_owner,
):
    query_local = queries[0]
    step_count, token_count, width_local = query_local.shape
    heads_local = width_local // HEAD_DIM
    attended = attend_all(
        query_local.reshape(step_count, token_count, heads_local, HEAD_DIM),
        lax.all_gather(key_vecs[0], "seq", axis=1, tiled=True),
        lax.all_gather(value_vecs[0], "seq", axis=1, tiled=True),
    )
    row_count = step_count * token_count
    both_rows = jnp.dot(
        lax.all_gather(attended.reshape(row_count, width_local), "guide", axis=0, tiled=True),
        w_out,
        preferred_element_type=F32,
    )
    half_width = w_out.shape[1]
    swapped = lax.all_to_all(
        both_rows.reshape(2, row_count, half_width), "guide", split_axis=0, concat_axis=2, tiled=True
    )
    projected = swapped.reshape(row_count, 2 * half_width)
    attn_out = lax.psum_scatter(projected, "shard", scatter_dimension=1, tiled=True)
    width_shard = attn_out.shape[1]
    width_model = width_shard * lax.axis_size("shard")
    hidden = residual[0].astype(F32) + attn_gate[:, None, :] * attn_out.reshape(
        step_count, token_count, width_shard
    )
    sum_first, sum_second = lax.psum((jnp.sum(hidden, axis=-1), jnp.sum(hidden * hidden, axis=-1)), "shard")
    mean_row = sum_first / width_model
    var_row = sum_second / width_model - mean_row * mean_row
    inv_std = lax.rsqrt(var_row + norm_epsilon)
    modulated = (hidden - mean_row[..., None]) * inv_std[..., None] * (
        1.0 + norm_scale[:, None, :]
    ) + norm_shift[:, None, :]
    partial_head = jnp.einsum(
        "tqd,dc->tqc", modulated, w_head.astype(F32), precision=lax.Precision.HIGHEST
    )
    predicted = lax.psum(partial_head, "shard")
    seq_count = lax.axis_size("seq")
    frame_group = token_count // seq_count
    frames_view = predicted.reshape(step_count, seq_count, frame_group, predicted.shape[-1])
    owner_table = (
        frame_owner[:, :, None] == jnp.arange(seq_count, dtype=jnp.int32)[None, None, :]
    ).astype(F32)
    by_owner = jnp.einsum("tfo,tfgc->togc", owner_table, frames_view, precision=lax.Precision.HIGHEST)
    arrived = lax.all_to_all(
        lax.all_to_all(by_owner[None], "seq", split_axis=2, concat_axis=3, tiled=True),
        "guide",
        split_axis=4,
        concat_axis=0,
        tiled=True,
    )
    guided = arrived[1] + guidance_scale * (arrived[0] - arrived[1])
    return plan_weight(timesteps)[:, None, None, None] * (guided - noise)


def pack_kernel(parts, half, q_ref, k_ref, v_ref, *out_refs):
    z = lax.axis_index("seq")
    for j in range(parts):
        start = pl.multiple_of(lax.rem(z + j, parts) * half, LANES)
        out_refs[j][0] = k_ref[:, pl.ds(start, half)]
        out_refs[j][1] = v_ref[:, pl.ds(start, half)]
        out_refs[parts + j][...] = q_ref[:, pl.ds(start, half)]


def attend_kernel(parts, *refs):
    q_refs = refs[:parts]
    kv_refs = refs[parts : 3 * parts]
    o_refs = refs[3 * parts :]
    rows = q_refs[0].shape[0]
    for i in range(q_refs[0].shape[1] // HEAD_DIM):
        cols = slice(i * HEAD_DIM, (i + 1) * HEAD_DIM)
        q = jnp.concatenate([r[:, cols] for r in q_refs], axis=0)
        k = jnp.concatenate([r[0, :, cols] for r in kv_refs], axis=0)
        v = jnp.concatenate([r[1, :, cols] for r in kv_refs], axis=0)
        scores = lax.dot_general(q, k, (((1,), (1,)), ((), ())), preferred_element_type=F32)
        scores = scores * (HEAD_DIM ** (-0.5) * LOG2E)
        expo = jnp.exp2(scores - jnp.max(scores, axis=1, keepdims=True))
        total = jnp.sum(expo, axis=1, keepdims=True)
        mixed = jnp.dot(expo.astype(BF16), v, preferred_element_type=F32) / total
        for j in range(parts):
            o_refs[j][:, cols] = mixed[j * rows : (j + 1) * rows].astype(BF16)


def project(parts, half, o_refs, w_ref, cols):
    z = lax.axis_index("seq")
    total = None
    for j in range(parts):
        start = pl.multiple_of(lax.rem(z + j, parts) * half, LANES)
        term = jnp.dot(o_refs[j][...], w_ref[pl.ds(start, half), cols], preferred_element_type=F32)
        total = term if total is None else total + term
    return total


def send_kernel(parts, half, chunk, first, *refs):
    o_refs = refs[:parts]
    near_ref, far_ref, out_ref = refs[parts:]
    guide = lax.axis_index("guide")
    for value, w_ref in ((1, near_ref), (0, far_ref)):

        @pl.when(guide == value)
        def _():
            for t in range(out_ref.shape[1] // chunk):
                cols = slice(first + t * chunk, first + (t + 1) * chunk)
                out_ref[:, t * chunk : (t + 1) * chunk] = project(parts, half, o_refs, w_ref, cols).astype(BF16)


def keep_kernel(parts, half, chunk, *refs):
    o_refs = refs[:parts]
    near_ref, far_ref, res_ref, gate_ref, out_ref = refs[parts:]
    guide = lax.axis_index("guide")
    for value, w_ref in ((0, near_ref), (1, far_ref)):

        @pl.when(guide == value)
        def _():
            for t in range(out_ref.shape[1] // chunk):
                cols = slice(t * chunk, (t + 1) * chunk)
                out_ref[:, cols] = res_ref[:, cols].astype(F32) + gate_ref[:, cols] * project(
                    parts, half, o_refs, w_ref, cols
                )


def split_dot(head_t, rows):
    dims = (((1,), (1,)), ((), ()))
    high = rows.astype(BF16)
    low = (rows - high.astype(F32)).astype(BF16)
    return lax.dot_general(head_t, high, dims, preferred_element_type=F32) + lax.dot_general(
        head_t, low, dims, preferred_element_type=F32
    )


def head_rows_kernel(scale_ref, shift_ref, head_ref, out_ref):
    width = scale_ref.shape[1]
    which = lax.broadcasted_iota(jnp.int32, (LANES, width), 0)
    rows = jnp.where(which == 0, 1.0 + scale_ref[...], shift_ref[...])
    high = rows.astype(BF16)
    rest = rows - high.astype(F32)
    mid = rest.astype(BF16)
    low = (rest - mid.astype(F32)).astype(BF16)
    dims = (((1,), (1,)), ((), ()))
    total = None
    for part in (high, mid, low):
        term = lax.dot_general(head_ref[...], part, dims, preferred_element_type=F32)
        total = term if total is None else total + term
    out_ref[...] = total


def head_kernel(first, last, chunk, start, *refs):
    hid_ref, got_ref, gate_ref, scale_ref, head_ref = refs[:5]
    if first:
        out_refs = refs[5:]
    else:
        prev_refs, out_refs = refs[5:8], refs[8:]
    channels = head_ref.shape[0]
    rows = hid_ref.shape[0]
    acc_one = jnp.zeros((rows, LANES), F32) if first else prev_refs[1][...]
    acc_two = jnp.zeros((rows, LANES), F32) if first else prev_refs[2][...]
    acc_head = jnp.zeros((channels, rows), F32) if first else prev_refs[0][...]
    for t in range(got_ref.shape[1] // chunk):
        cols = slice(start + t * chunk, start + (t + 1) * chunk)
        arrived = got_ref[:, t * chunk : (t + 1) * chunk].astype(F32)
        hidden = hid_ref[:, cols] + gate_ref[:, cols] * arrived
        for s in range(chunk // LANES):
            piece = hidden[:, s * LANES : (s + 1) * LANES]
            acc_one = acc_one + piece
            acc_two = acc_two + piece * piece
        acc_head = acc_head + split_dot(head_ref[:, cols], hidden * (1.0 + scale_ref[:, cols]))
    if last:
        out_ref = out_refs[0]
        out_ref[0:channels, :] = acc_head
        sum_one = jnp.sum(acc_one.T, axis=0, keepdims=True)
        sum_two = jnp.sum(acc_two.T, axis=0, keepdims=True)
        row = lax.broadcasted_iota(jnp.int32, (SUBLANES, rows), 0)
        out_ref[channels : channels + SUBLANES, :] = jnp.where(row == 0, sum_one, sum_two)
    else:
        out_refs[0][...] = acc_head
        out_refs[1][...] = acc_one
        out_refs[2][...] = acc_two


def norm_kernel(width_model, own_ref, got_ref, rows_own_ref, rows_got_ref, keep_ref, send_ref, eps_scr):
    channels = rows_own_ref.shape[0]
    half_channels = channels // 2
    guide = lax.axis_index("guide")
    head = own_ref[0:channels, :] + got_ref[0:channels, :]
    stats = own_ref[channels : channels + SUBLANES, :] + got_ref[channels : channels + SUBLANES, :]
    mean = stats[0:1] / width_model
    var = stats[1:2] / width_model - mean * mean
    inv_std = lax.rsqrt(var + norm_epsilon)
    scaled = rows_own_ref[:, 0:1] + rows_got_ref[:, 0:1]
    shifted = rows_own_ref[:, 1:2] + rows_got_ref[:, 1:2]
    eps_scr[...] = (head - mean * scaled) * inv_std + shifted
    keep_ref[...] = eps_scr[pl.ds(pl.multiple_of(guide * half_channels, SUBLANES), half_channels), :]
    send_ref[...] = eps_scr[pl.ds(pl.multiple_of((1 - guide) * half_channels, SUBLANES), half_channels), :]


def frame_kernel(seq_count, group, owner_ref, keep_ref, got_ref, *out_refs):
    z = lax.axis_index("seq")
    first = lax.axis_index("guide") == 0
    mine, other = keep_ref[...], got_ref[...]
    eps_cond = jnp.where(first, mine, other)
    eps_free = jnp.where(first, other, mine)
    guided = eps_free + guidance_scale * (eps_cond - eps_free)
    fold = LANES // group
    rows = guided.shape[0] // fold
    lane = lax.broadcasted_iota(jnp.int32, (rows, LANES), 1) // group
    for k in range(seq_count):
        target = lax.rem(z + k, seq_count)
        frame = jnp.int32(0)
        for f in range(seq_count):
            frame = jnp.where(owner_ref[0, f] == target, f, frame)
        packed = jnp.zeros((rows, LANES), F32)
        for j in range(fold):
            shift = lax.rem((j - frame) * group + LANES, LANES)
            rolled = pltpu.roll(guided[j * rows : (j + 1) * rows], shift, axis=1)
            packed = jnp.where(lane == j, rolled, packed)
        out_refs[k][...] = packed


def final_kernel(seq_count, group, steps_ref, noise_ref, *refs):
    piece_refs, out_ref = refs[:seq_count], refs[seq_count]
    z = lax.axis_index("seq")
    fold = LANES // group
    rows = piece_refs[0].shape[0]
    lane = lax.broadcasted_iota(jnp.int32, (rows, LANES), 1) // group
    blocks = []
    for j in range(fold):
        block = jnp.zeros((rows, LANES), F32)
        for k in range(seq_count):
            source = lax.rem(z - k + seq_count, seq_count)
            shift = lax.rem((source - j) * group + LANES, LANES)
            block = jnp.where(lane == source, pltpu.roll(piece_refs[k][...], shift, axis=1), block)
        blocks.append(block)
    framed = jnp.concatenate(blocks, axis=0)
    step = jnp.full((1, 1), steps_ref[0], jnp.int32)
    out_ref[...] = plan_weight(step) * (framed - noise_ref[...])


def call(kernel, outs, args, specs=None, scratch=(), flops=0, moved=0, grant=16):
    shapes = [jax.ShapeDtypeStruct(s, d) for s, d in outs]
    return pl.pallas_call(
        kernel,
        out_shape=shapes,
        in_specs=specs or [VMEM_SPEC] * len(args),
        out_specs=[VMEM_SPEC] * len(outs),
        scratch_shapes=list(scratch),
        compiler_params=pltpu.CompilerParams(vmem_limit_bytes=grant << 20),
        cost_estimate=pl.CostEstimate(flops=flops, bytes_accessed=moved, transcendentals=0),
    )(*args)


def fast_plan(
    queries, key_vecs, value_vecs, residual, w_out, attn_gate, norm_shift, norm_scale, w_head, noise,
    timesteps, frame_owner,
):
    seq_count = lax.axis_size("seq")
    parts = seq_count // 2
    rows, width_local = queries.shape[2:]
    half = width_local // parts
    width_shard = residual.shape[3]
    channels = w_head.shape[1]
    group = rows // seq_count
    width_model = float(width_shard * lax.axis_size("shard"))
    both = [(0, 1), (1, 0)]
    axes = ("seq", "guide")

    crossed = [(x * 2 + c, x * 2 + (c + x) % 2) for x in range(2) for c in range(2)]
    straight = [(x * 2 + c, x * 2 + (c + x + 1) % 2) for x in range(2) for c in range(2)]

    packed = call(
        functools.partial(pack_kernel, parts, half),
        [((2, rows, half), BF16)] * parts + [((rows, half), BF16)] * parts,
        [queries[0, 0], key_vecs[0, 0], value_vecs[0, 0]],
        moved=12 * rows * width_local,
    )
    there = [
        [
            (z * 2 + c, (parts * c + (z + j) % parts) * 2 + z // parts)
            for z in range(seq_count)
            for c in range(2)
        ]
        for j in range(parts)
    ]
    back = [[(b, a) for a, b in pairs] for pairs in there]
    kv_own = [lax.ppermute(packed[j], axes, there[j]) for j in range(parts)]
    q_own = [lax.ppermute(packed[parts + j], axes, there[j]) for j in range(parts)]
    near_w = lax.ppermute(w_out, ("shard", "guide"), crossed)
    far_w = lax.ppermute(w_out, ("shard", "guide"), straight)
    kv_other = [lax.ppermute(block, "guide", both) for block in kv_own]

    head_t = w_head.T
    rows_own = call(
        head_rows_kernel, [((channels, LANES), F32)], [norm_scale, norm_shift, head_t],
        moved=4 * width_shard * LANES,
    )[0]
    rows_got = lax.ppermute(rows_own, "shard", both)
    *q_own, rows_own = lax.optimization_barrier((*q_own, rows_own))

    mixed = call(
        functools.partial(attend_kernel, parts),
        [((rows, half), BF16)] * parts,
        q_own + kv_own + kv_other,
        flops=8 * rows * parts * rows * parts * half,
        moved=2 * rows * half * parts * 6,
    )
    *mixed, rows_got, near_w, far_w = lax.optimization_barrier((*mixed, rows_got, near_w, far_w))
    mixed = [lax.ppermute(mixed[j], axes, back[j]) for j in range(parts)]

    chunk = 128
    pieces = 2
    width_piece = width_shard // pieces
    got = []
    for i in range(pieces):
        partial = call(
            functools.partial(send_kernel, parts, half, chunk, i * width_piece),
            [((rows, width_piece), BF16)],
            mixed + [near_w, far_w],
            flops=2 * rows * width_local * width_piece,
            moved=2 * width_local * width_piece,
        )[0]
        got.append(lax.ppermute(partial, "shard", both))
    hidden = call(
        functools.partial(keep_kernel, parts, half, chunk),
        [((rows, width_shard), F32)],
        mixed + [near_w, far_w, residual[0, 0], attn_gate],
        flops=2 * rows * width_local * width_shard,
        moved=2 * width_local * width_shard,
    )[0]
    state = []
    for i in range(pieces):
        first, last = i == 0, i == pieces - 1
        state = call(
            functools.partial(head_kernel, first, last, chunk, i * width_piece),
            [((channels + SUBLANES, rows), F32)]
            if last
            else [((channels, rows), F32), ((rows, LANES), F32), ((rows, LANES), F32)],
            [hidden, got[i], attn_gate, norm_scale, head_t] + list(state),
            flops=4 * rows * channels * width_piece,
            moved=6 * rows * width_piece,
        )
    sums = state[0]
    sums_got = lax.ppermute(sums, "shard", both)
    keep, send = call(
        functools.partial(norm_kernel, width_model),
        [((channels // 2, rows), F32)] * 2,
        [sums, sums_got, rows_own, rows_got],
        scratch=[pltpu.VMEM((channels, rows), F32)],
    )
    eps_got = lax.ppermute(send, "guide", both)
    fold = LANES // group
    frames = call(
        functools.partial(frame_kernel, seq_count, group),
        [((channels // 2 // fold, LANES), F32)] * seq_count,
        [frame_owner, keep, eps_got],
        [SMEM_SPEC, VMEM_SPEC, VMEM_SPEC],
    )
    arrived = [frames[0]] + [
        lax.ppermute(frames[k], "seq", [(z, (z + k) % seq_count) for z in range(seq_count)])
        for k in range(1, seq_count)
    ]
    out = call(
        functools.partial(final_kernel, seq_count, group),
        [((channels // 2, rows), F32)],
        [timesteps, noise[0, 0].T] + arrived,
        [SMEM_SPEC] + [VMEM_SPEC] * (seq_count + 1),
    )[0]
    return out.T[None, None]


def fast_fits(sizes, queries, residual, w_out, w_head):
    seq_count = sizes["seq"]
    step_count, rows, width_local = queries.shape[1:]
    channels = w_head.shape[1]
    if sizes["guide"] != 2 or sizes["shard"] != 2 or seq_count % 2 or step_count != 1 or rows != LANES:
        return False
    if width_local % (seq_count // 2 * HEAD_DIM) or residual.shape[3] % (4 * LANES):
        return False
    if w_out.shape[1] != residual.shape[3] or channels % (2 * SUBLANES):
        return False
    group = rows // seq_count
    if rows % seq_count or LANES % group:
        return False
    fold = LANES // group
    return channels // 2 % (fold * SUBLANES) == 0


def solution(mesh):
    sizes = dict(mesh.shape)

    def on_device(queries, key_vecs, value_vecs, residual, w_out, attn_gate, norm_shift, norm_scale, w_head, *rest):
        fits = fast_fits(sizes, queries, residual, w_out, w_head)
        plan = fast_plan if fits else general_plan
        return plan(
            queries, key_vecs, value_vecs, residual, w_out, attn_gate, norm_shift, norm_scale, w_head, *rest
        )

    return jax.shard_map(
        on_device,
        mesh=mesh,
        in_specs=(
            P("guide", "group", "seq", "shard"),
            P("guide", "group", "seq", "shard"),
            P("guide", "group", "seq", "shard"),
            P("guide", "group", "seq", "shard"),
            P("shard", "guide"),
            P("group", "shard"),
            P("group", "shard"),
            P("group", "shard"),
            P("shard", None),
            P("group", "seq", None, "guide"),
            P("group"),
            P("group", None),
        ),
        out_specs=P("group", "seq", None, "guide"),
        check_vma=False,
    )
```

```python
import functools

import jax
import jax.numpy as jnp
from jax import lax
from jax.experimental import pallas as pl
from jax.experimental.pallas import tpu as pltpu
from jax.sharding import PartitionSpec as P


HEAD_DIM = 128
LANES = 128
SUBLANES = 8
beta_low = 0.0001
beta_high = 0.02
guidance_scale = 3.0
norm_epsilon = 1e-06
LOG2E = 1.4426950408889634


F32 = jnp.float32
BF16 = jnp.bfloat16
VMEM_SPEC = pl.BlockSpec(memory_space=pltpu.VMEM)
SMEM_SPEC = pl.BlockSpec(memory_space=pltpu.SMEM)
HBM_SPEC = pl.BlockSpec(memory_space=pltpu.HBM)


def plan_weight(timesteps):
    steps_float = timesteps.astype(jnp.float32)
    exponent = (steps_float + 1.0) * beta_low + (beta_high - beta_low) * steps_float * (
        steps_float + 1.0
    ) / (2.0 * 999.0)
    return 1.0 - jnp.exp(-exponent)


def attend_all(query_split, keys_all, values_all):
    heads_local = query_split.shape[2]
    keys_split = keys_all.reshape(keys_all.shape[0], keys_all.shape[1], heads_local, HEAD_DIM)
    values_split = values_all.reshape(values_all.shape[0], values_all.shape[1], heads_local, HEAD_DIM)
    scores = jnp.einsum(
        "tqhd,tkhd->tqhk", query_split, keys_split, preferred_element_type=F32
    ) * HEAD_DIM ** (-0.5)
    expo = jnp.exp(scores - jnp.max(scores, axis=-1, keepdims=True))
    total = jnp.sum(expo, axis=-1)
    mixed = jnp.einsum("tqhk,tkhd->tqhd", expo.astype(BF16), values_split, preferred_element_type=F32)
    return (mixed / total[..., None]).astype(BF16)


def general_plan(
    queries, key_vecs, value_vecs, residual, w_out, attn_gate, norm_shift, norm_scale, w_head, noise,
    timesteps, frame_owner,
):
    query_local = queries[0]
    step_count, token_count, width_local = query_local.shape
    heads_local = width_local // HEAD_DIM
    attended = attend_all(
        query_local.reshape(step_count, token_count, heads_local, HEAD_DIM),
        lax.all_gather(key_vecs[0], "seq", axis=1, tiled=True),
        lax.all_gather(value_vecs[0], "seq", axis=1, tiled=True),
    )
    row_count = step_count * token_count
    both_rows = jnp.dot(
        lax.all_gather(attended.reshape(row_count, width_local), "guide", axis=0, tiled=True),
        w_out,
        preferred_element_type=F32,
    )
    half_width = w_out.shape[1]
    swapped = lax.all_to_all(
        both_rows.reshape(2, row_count, half_width), "guide", split_axis=0, concat_axis=2, tiled=True
    )
    projected = swapped.reshape(row_count, 2 * half_width)
    attn_out = lax.psum_scatter(projected, "shard", scatter_dimension=1, tiled=True)
    width_shard = attn_out.shape[1]
    width_model = width_shard * lax.axis_size("shard")
    hidden = residual[0].astype(F32) + attn_gate[:, None, :] * attn_out.reshape(
        step_count, token_count, width_shard
    )
    sum_first, sum_second = lax.psum((jnp.sum(hidden, axis=-1), jnp.sum(hidden * hidden, axis=-1)), "shard")
    mean_row = sum_first / width_model
    var_row = sum_second / width_model - mean_row * mean_row
    inv_std = lax.rsqrt(var_row + norm_epsilon)
    modulated = (hidden - mean_row[..., None]) * inv_std[..., None] * (
        1.0 + norm_scale[:, None, :]
    ) + norm_shift[:, None, :]
    partial_head = jnp.einsum(
        "tqd,dc->tqc", modulated, w_head.astype(F32), precision=lax.Precision.HIGHEST
    )
    predicted = lax.psum(partial_head, "shard")
    seq_count = lax.axis_size("seq")
    frame_group = token_count // seq_count
    frames_view = predicted.reshape(step_count, seq_count, frame_group, predicted.shape[-1])
    owner_table = (
        frame_owner[:, :, None] == jnp.arange(seq_count, dtype=jnp.int32)[None, None, :]
    ).astype(F32)
    by_owner = jnp.einsum("tfo,tfgc->togc", owner_table, frames_view, precision=lax.Precision.HIGHEST)
    arrived = lax.all_to_all(
        lax.all_to_all(by_owner[None], "seq", split_axis=2, concat_axis=3, tiled=True),
        "guide",
        split_axis=4,
        concat_axis=0,
        tiled=True,
    )
    guided = arrived[1] + guidance_scale * (arrived[0] - arrived[1])
    return plan_weight(timesteps)[:, None, None, None] * (guided - noise)


def pack_kernel(parts, half, *refs):
    q_ref, k_ref, v_ref = refs[:3]
    out_refs, sems = refs[3:-1], refs[-1]
    z = lax.axis_index("seq")
    copies = []
    for j in range(parts):
        cols = pl.ds(pl.multiple_of(lax.rem(z + j, parts) * half, LANES), half)
        copies.append(pltpu.make_async_copy(k_ref.at[:, cols], out_refs[j].at[0], sems.at[3 * j]))
        copies.append(pltpu.make_async_copy(v_ref.at[:, cols], out_refs[j].at[1], sems.at[3 * j + 1]))
        copies.append(pltpu.make_async_copy(q_ref.at[:, cols], out_refs[parts + j], sems.at[3 * j + 2]))
    for copy in copies:
        copy.start()
    for copy in copies:
        copy.wait()


def attend_kernel(parts, *refs):
    q_refs = refs[:parts]
    kv_refs = refs[parts : 3 * parts]
    o_refs = refs[3 * parts :]
    rows = q_refs[0].shape[0]
    for i in range(q_refs[0].shape[1] // HEAD_DIM):
        cols = slice(i * HEAD_DIM, (i + 1) * HEAD_DIM)
        q = jnp.concatenate([r[:, cols] for r in q_refs], axis=0)
        k = jnp.concatenate([r[0, :, cols] for r in kv_refs], axis=0)
        v = jnp.concatenate([r[1, :, cols] for r in kv_refs], axis=0)
        scores = lax.dot_general(q, k, (((1,), (1,)), ((), ())), preferred_element_type=F32)
        scores = scores * (HEAD_DIM ** (-0.5) * LOG2E)
        expo = jnp.exp2(scores - jnp.max(scores, axis=1, keepdims=True))
        total = jnp.sum(expo, axis=1, keepdims=True)
        mixed = jnp.dot(expo.astype(BF16), v, preferred_element_type=F32) / total
        for j in range(parts):
            o_refs[j][:, cols] = mixed[j * rows : (j + 1) * rows].astype(BF16)


def project(parts, half, o_refs, w_ref, cols):
    z = lax.axis_index("seq")
    total = None
    for j in range(parts):
        start = pl.multiple_of(lax.rem(z + j, parts) * half, LANES)
        term = jnp.dot(o_refs[j][...], w_ref[pl.ds(start, half), cols], preferred_element_type=F32)
        total = term if total is None else total + term
    return total


def send_kernel(parts, half, chunk, first, *refs):
    o_refs = refs[:parts]
    near_ref, far_ref, out_ref = refs[parts:]
    guide = lax.axis_index("guide")
    for value, w_ref in ((1, near_ref), (0, far_ref)):

        @pl.when(guide == value)
        def _():
            for t in range(out_ref.shape[1] // chunk):
                cols = slice(first + t * chunk, first + (t + 1) * chunk)
                out_ref[:, t * chunk : (t + 1) * chunk] = project(parts, half, o_refs, w_ref, cols).astype(BF16)


def keep_kernel(parts, half, chunk, *refs):
    o_refs = refs[:parts]
    near_ref, far_ref, res_ref, gate_ref, out_ref = refs[parts:]
    guide = lax.axis_index("guide")
    for value, w_ref in ((0, near_ref), (1, far_ref)):

        @pl.when(guide == value)
        def _():
            for t in range(out_ref.shape[1] // chunk):
                cols = slice(t * chunk, (t + 1) * chunk)
                out_ref[:, cols] = res_ref[:, cols].astype(F32) + gate_ref[:, cols] * project(
                    parts, half, o_refs, w_ref, cols
                )


def split_dot(head_t, rows):
    dims = (((1,), (1,)), ((), ()))
    high = rows.astype(BF16)
    low = (rows - high.astype(F32)).astype(BF16)
    return lax.dot_general(head_t, high, dims, preferred_element_type=F32) + lax.dot_general(
        head_t, low, dims, preferred_element_type=F32
    )


def head_rows_kernel(scale_ref, shift_ref, head_ref, out_ref):
    width = scale_ref.shape[1]
    which = lax.broadcasted_iota(jnp.int32, (LANES, width), 0)
    rows = jnp.where(which == 0, 1.0 + scale_ref[...], shift_ref[...])
    high = rows.astype(BF16)
    rest = rows - high.astype(F32)
    mid = rest.astype(BF16)
    low = (rest - mid.astype(F32)).astype(BF16)
    dims = (((1,), (1,)), ((), ()))
    total = None
    for part in (high, mid, low):
        term = lax.dot_general(head_ref[...], part, dims, preferred_element_type=F32)
        total = term if total is None else total + term
    out_ref[...] = total


def head_kernel(first, last, chunk, start, *refs):
    hid_ref, got_ref, gate_ref, scale_ref, head_ref = refs[:5]
    if first:
        out_refs = refs[5:]
    else:
        prev_refs, out_refs = refs[5:8], refs[8:]
    channels = head_ref.shape[0]
    rows = hid_ref.shape[0]
    acc_one = jnp.zeros((rows, LANES), F32) if first else prev_refs[1][...]
    acc_two = jnp.zeros((rows, LANES), F32) if first else prev_refs[2][...]
    acc_head = jnp.zeros((channels, rows), F32) if first else prev_refs[0][...]
    for t in range(got_ref.shape[1] // chunk):
        cols = slice(start + t * chunk, start + (t + 1) * chunk)
        arrived = got_ref[:, t * chunk : (t + 1) * chunk].astype(F32)
        hidden = hid_ref[:, cols] + gate_ref[:, cols] * arrived
        for s in range(chunk // LANES):
            piece = hidden[:, s * LANES : (s + 1) * LANES]
            acc_one = acc_one + piece
            acc_two = acc_two + piece * piece
        acc_head = acc_head + split_dot(head_ref[:, cols], hidden * (1.0 + scale_ref[:, cols]))
    if last:
        out_ref = out_refs[0]
        out_ref[0:channels, :] = acc_head
        sum_one = jnp.sum(acc_one.T, axis=0, keepdims=True)
        sum_two = jnp.sum(acc_two.T, axis=0, keepdims=True)
        row = lax.broadcasted_iota(jnp.int32, (SUBLANES, rows), 0)
        out_ref[channels : channels + SUBLANES, :] = jnp.where(row == 0, sum_one, sum_two)
    else:
        out_refs[0][...] = acc_head
        out_refs[1][...] = acc_one
        out_refs[2][...] = acc_two


def norm_kernel(width_model, own_ref, got_ref, rows_own_ref, rows_got_ref, keep_ref, send_ref, eps_scr):
    channels = rows_own_ref.shape[0]
    half_channels = channels // 2
    guide = lax.axis_index("guide")
    head = own_ref[0:channels, :] + got_ref[0:channels, :]
    stats = own_ref[channels : channels + SUBLANES, :] + got_ref[channels : channels + SUBLANES, :]
    mean = stats[0:1] / width_model
    var = stats[1:2] / width_model - mean * mean
    inv_std = lax.rsqrt(var + norm_epsilon)
    scaled = rows_own_ref[:, 0:1] + rows_got_ref[:, 0:1]
    shifted = rows_own_ref[:, 1:2] + rows_got_ref[:, 1:2]
    eps_scr[...] = (head - mean * scaled) * inv_std + shifted
    keep_ref[...] = eps_scr[pl.ds(pl.multiple_of(guide * half_channels, SUBLANES), half_channels), :]
    send_ref[...] = eps_scr[pl.ds(pl.multiple_of((1 - guide) * half_channels, SUBLANES), half_channels), :]


def frame_kernel(seq_count, group, owner_ref, keep_ref, got_ref, *out_refs):
    z = lax.axis_index("seq")
    first = lax.axis_index("guide") == 0
    mine, other = keep_ref[...], got_ref[...]
    eps_cond = jnp.where(first, mine, other)
    eps_free = jnp.where(first, other, mine)
    guided = eps_free + guidance_scale * (eps_cond - eps_free)
    fold = LANES // group
    rows = guided.shape[0] // fold
    lane = lax.broadcasted_iota(jnp.int32, (rows, LANES), 1) // group
    for k in range(seq_count):
        target = lax.rem(z + k, seq_count)
        frame = jnp.int32(0)
        for f in range(seq_count):
            frame = jnp.where(owner_ref[0, f] == target, f, frame)
        packed = jnp.zeros((rows, LANES), F32)
        for j in range(fold):
            shift = lax.rem((j - frame) * group + LANES, LANES)
            rolled = pltpu.roll(guided[j * rows : (j + 1) * rows], shift, axis=1)
            packed = jnp.where(lane == j, rolled, packed)
        out_refs[k][...] = packed


def final_kernel(seq_count, group, steps_ref, noise_ref, *refs):
    piece_refs, out_ref = refs[:seq_count], refs[seq_count]
    z = lax.axis_index("seq")
    fold = LANES // group
    rows = piece_refs[0].shape[0]
    lane = lax.broadcasted_iota(jnp.int32, (rows, LANES), 1) // group
    blocks = []
    for j in range(fold):
        block = jnp.zeros((rows, LANES), F32)
        for k in range(seq_count):
            source = lax.rem(z - k + seq_count, seq_count)
            shift = lax.rem((source - j) * group + LANES, LANES)
            block = jnp.where(lane == source, pltpu.roll(piece_refs[k][...], shift, axis=1), block)
        blocks.append(block)
    framed = jnp.concatenate(blocks, axis=0)
    step = jnp.full((1, 1), steps_ref[0], jnp.int32)
    out_ref[...] = plan_weight(step) * (framed - noise_ref[...])


def call(kernel, outs, args, specs=None, scratch=(), flops=0, moved=0, grant=16):
    shapes = [jax.ShapeDtypeStruct(s, d) for s, d in outs]
    return pl.pallas_call(
        kernel,
        out_shape=shapes,
        in_specs=specs or [VMEM_SPEC] * len(args),
        out_specs=[VMEM_SPEC] * len(outs),
        scratch_shapes=list(scratch),
        compiler_params=pltpu.CompilerParams(vmem_limit_bytes=grant << 20),
        cost_estimate=pl.CostEstimate(flops=flops, bytes_accessed=moved, transcendentals=0),
    )(*args)


def fast_plan(
    queries, key_vecs, value_vecs, residual, w_out, attn_gate, norm_shift, norm_scale, w_head, noise,
    timesteps, frame_owner,
):
    seq_count = lax.axis_size("seq")
    parts = seq_count // 2
    rows, width_local = queries.shape[2:]
    half = width_local // parts
    width_shard = residual.shape[3]
    channels = w_head.shape[1]
    group = rows // seq_count
    width_model = float(width_shard * lax.axis_size("shard"))
    both = [(0, 1), (1, 0)]
    axes = ("seq", "guide")

    crossed = [(x * 2 + c, x * 2 + (c + x) % 2) for x in range(2) for c in range(2)]
    straight = [(x * 2 + c, x * 2 + (c + x + 1) % 2) for x in range(2) for c in range(2)]

    packed = call(
        functools.partial(pack_kernel, parts, half),
        [((2, rows, half), BF16)] * parts + [((rows, half), BF16)] * parts,
        [
            pltpu.with_memory_space_constraint(array[0, 0], pltpu.HBM)
            for array in (queries, key_vecs, value_vecs)
        ],
        [HBM_SPEC] * 3,
        [pltpu.SemaphoreType.DMA((3 * parts,))],
        moved=12 * rows * width_local,
    )
    there = [
        [
            (z * 2 + c, (parts * c + (z + j) % parts) * 2 + z // parts)
            for z in range(seq_count)
            for c in range(2)
        ]
        for j in range(parts)
    ]
    back = [[(b, a) for a, b in pairs] for pairs in there]
    kv_own = [lax.ppermute(packed[j], axes, there[j]) for j in range(parts)]
    q_own = [lax.ppermute(packed[parts + j], axes, there[j]) for j in range(parts)]
    near_w = lax.ppermute(w_out, ("shard", "guide"), crossed)
    far_w = lax.ppermute(w_out, ("shard", "guide"), straight)
    kv_other = [lax.ppermute(block, "guide", both) for block in kv_own]

    head_t = w_head.T
    rows_own = call(
        head_rows_kernel, [((channels, LANES), F32)], [norm_scale, norm_shift, head_t],
        moved=4 * width_shard * LANES,
    )[0]
    rows_got = lax.ppermute(rows_own, "shard", both)
    *q_own, rows_own = lax.optimization_barrier((*q_own, rows_own))

    mixed = call(
        functools.partial(attend_kernel, parts),
        [((rows, half), BF16)] * parts,
        q_own + kv_own + kv_other,
        flops=8 * rows * parts * rows * parts * half,
        moved=2 * rows * half * parts * 6,
    )
    *mixed, rows_got, near_w, far_w = lax.optimization_barrier((*mixed, rows_got, near_w, far_w))
    mixed = [lax.ppermute(mixed[j], axes, back[j]) for j in range(parts)]

    chunk = 128
    pieces = 2
    width_piece = width_shard // pieces
    got = []
    for i in range(pieces):
        partial = call(
            functools.partial(send_kernel, parts, half, chunk, i * width_piece),
            [((rows, width_piece), BF16)],
            mixed + [near_w, far_w],
            flops=2 * rows * width_local * width_piece,
            moved=2 * width_local * width_piece,
        )[0]
        got.append(lax.ppermute(partial, "shard", both))
    hidden = call(
        functools.partial(keep_kernel, parts, half, chunk),
        [((rows, width_shard), F32)],
        mixed + [near_w, far_w, residual[0, 0], attn_gate],
        flops=2 * rows * width_local * width_shard,
        moved=2 * width_local * width_shard,
    )[0]
    state = []
    for i in range(pieces):
        first, last = i == 0, i == pieces - 1
        state = call(
            functools.partial(head_kernel, first, last, chunk, i * width_piece),
            [((channels + SUBLANES, rows), F32)]
            if last
            else [((channels, rows), F32), ((rows, LANES), F32), ((rows, LANES), F32)],
            [hidden, got[i], attn_gate, norm_scale, head_t] + list(state),
            flops=4 * rows * channels * width_piece,
            moved=6 * rows * width_piece,
        )
    sums = state[0]
    sums_got = lax.ppermute(sums, "shard", both)
    keep, send = call(
        functools.partial(norm_kernel, width_model),
        [((channels // 2, rows), F32)] * 2,
        [sums, sums_got, rows_own, rows_got],
        scratch=[pltpu.VMEM((channels, rows), F32)],
    )
    eps_got = lax.ppermute(send, "guide", both)
    fold = LANES // group
    frames = call(
        functools.partial(frame_kernel, seq_count, group),
        [((channels // 2 // fold, LANES), F32)] * seq_count,
        [frame_owner, keep, eps_got],
        [SMEM_SPEC, VMEM_SPEC, VMEM_SPEC],
    )
    arrived = [frames[0]] + [
        lax.ppermute(frames[k], "seq", [(z, (z + k) % seq_count) for z in range(seq_count)])
        for k in range(1, seq_count)
    ]
    out = call(
        functools.partial(final_kernel, seq_count, group),
        [((channels // 2, rows), F32)],
        [timesteps, noise[0, 0].T] + arrived,
        [SMEM_SPEC] + [VMEM_SPEC] * (seq_count + 1),
    )[0]
    return out.T[None, None]


def fast_fits(sizes, queries, residual, w_out, w_head):
    seq_count = sizes["seq"]
    step_count, rows, width_local = queries.shape[1:]
    channels = w_head.shape[1]
    if sizes["guide"] != 2 or sizes["shard"] != 2 or seq_count % 2 or step_count != 1 or rows != LANES:
        return False
    if width_local % (seq_count // 2 * HEAD_DIM) or residual.shape[3] % (4 * LANES):
        return False
    if w_out.shape[1] != residual.shape[3] or channels % (2 * SUBLANES):
        return False
    group = rows // seq_count
    if rows % seq_count or LANES % group:
        return False
    fold = LANES // group
    return channels // 2 % (fold * SUBLANES) == 0


def solution(mesh):
    sizes = dict(mesh.shape)

    def on_device(queries, key_vecs, value_vecs, residual, w_out, attn_gate, norm_shift, norm_scale, w_head, *rest):
        fits = fast_fits(sizes, queries, residual, w_out, w_head)
        plan = fast_plan if fits else general_plan
        return plan(queries, key_vecs, value_vecs, residual, w_out, attn_gate, norm_shift, norm_scale, w_head, *rest)

    return jax.shard_map(
        on_device,
        mesh=mesh,
        in_specs=(
            P("guide", "group", "seq", "shard"),
            P("guide", "group", "seq", "shard"),
            P("guide", "group", "seq", "shard"),
            P("guide", "group", "seq", "shard"),
            P("shard", "guide"),
            P("group", "shard"),
            P("group", "shard"),
            P("group", "shard"),
            P("shard", None),
            P("group", "seq", None, "guide"),
            P("group"),
            P("group", None),
        ),
        out_specs=P("group", "seq", None, "guide"),
        check_vma=False,
    )
```

```python
import functools

import jax
import jax.numpy as jnp
from jax import lax
from jax.experimental import pallas as pl
from jax.experimental.pallas import tpu as pltpu
from jax.sharding import PartitionSpec as P


HEAD_DIM = 128
LANES = 128
SUBLANES = 8
beta_low = 0.0001
beta_high = 0.02
guidance_scale = 3.0
norm_epsilon = 1e-06
LOG2E = 1.4426950408889634


F32 = jnp.float32
BF16 = jnp.bfloat16
VMEM_SPEC = pl.BlockSpec(memory_space=pltpu.VMEM)
SMEM_SPEC = pl.BlockSpec(memory_space=pltpu.SMEM)
HBM_SPEC = pl.BlockSpec(memory_space=pltpu.HBM)


def plan_weight(timesteps):
    steps_float = timesteps.astype(jnp.float32)
    exponent = (steps_float + 1.0) * beta_low + (beta_high - beta_low) * steps_float * (
        steps_float + 1.0
    ) / (2.0 * 999.0)
    return 1.0 - jnp.exp(-exponent)


def attend_all(query_split, keys_all, values_all):
    heads_local = query_split.shape[2]
    keys_split = keys_all.reshape(keys_all.shape[0], keys_all.shape[1], heads_local, HEAD_DIM)
    values_split = values_all.reshape(values_all.shape[0], values_all.shape[1], heads_local, HEAD_DIM)
    scores = jnp.einsum(
        "tqhd,tkhd->tqhk", query_split, keys_split, preferred_element_type=F32
    ) * HEAD_DIM ** (-0.5)
    expo = jnp.exp(scores - jnp.max(scores, axis=-1, keepdims=True))
    total = jnp.sum(expo, axis=-1)
    mixed = jnp.einsum("tqhk,tkhd->tqhd", expo.astype(BF16), values_split, preferred_element_type=F32)
    return (mixed / total[..., None]).astype(BF16)


def general_plan(
    queries, key_vecs, value_vecs, residual, w_out, attn_gate, norm_shift, norm_scale, w_head, noise,
    timesteps, frame_owner,
):
    query_local = queries[0]
    step_count, token_count, width_local = query_local.shape
    heads_local = width_local // HEAD_DIM
    attended = attend_all(
        query_local.reshape(step_count, token_count, heads_local, HEAD_DIM),
        lax.all_gather(key_vecs[0], "seq", axis=1, tiled=True),
        lax.all_gather(value_vecs[0], "seq", axis=1, tiled=True),
    )
    row_count = step_count * token_count
    both_rows = jnp.dot(
        lax.all_gather(attended.reshape(row_count, width_local), "guide", axis=0, tiled=True),
        w_out,
        preferred_element_type=F32,
    )
    half_width = w_out.shape[1]
    swapped = lax.all_to_all(
        both_rows.reshape(2, row_count, half_width), "guide", split_axis=0, concat_axis=2, tiled=True
    )
    projected = swapped.reshape(row_count, 2 * half_width)
    attn_out = lax.psum_scatter(projected, "shard", scatter_dimension=1, tiled=True)
    width_shard = attn_out.shape[1]
    width_model = width_shard * lax.axis_size("shard")
    hidden = residual[0].astype(F32) + attn_gate[:, None, :] * attn_out.reshape(
        step_count, token_count, width_shard
    )
    sum_first, sum_second = lax.psum((jnp.sum(hidden, axis=-1), jnp.sum(hidden * hidden, axis=-1)), "shard")
    mean_row = sum_first / width_model
    var_row = sum_second / width_model - mean_row * mean_row
    inv_std = lax.rsqrt(var_row + norm_epsilon)
    modulated = (hidden - mean_row[..., None]) * inv_std[..., None] * (
        1.0 + norm_scale[:, None, :]
    ) + norm_shift[:, None, :]
    partial_head = jnp.einsum(
        "tqd,dc->tqc", modulated, w_head.astype(F32), precision=lax.Precision.HIGHEST
    )
    predicted = lax.psum(partial_head, "shard")
    seq_count = lax.axis_size("seq")
    frame_group = token_count // seq_count
    frames_view = predicted.reshape(step_count, seq_count, frame_group, predicted.shape[-1])
    owner_table = (
        frame_owner[:, :, None] == jnp.arange(seq_count, dtype=jnp.int32)[None, None, :]
    ).astype(F32)
    by_owner = jnp.einsum("tfo,tfgc->togc", owner_table, frames_view, precision=lax.Precision.HIGHEST)
    arrived = lax.all_to_all(
        lax.all_to_all(by_owner[None], "seq", split_axis=2, concat_axis=3, tiled=True),
        "guide",
        split_axis=4,
        concat_axis=0,
        tiled=True,
    )
    guided = arrived[1] + guidance_scale * (arrived[0] - arrived[1])
    return plan_weight(timesteps)[:, None, None, None] * (guided - noise)


def pack_kernel(parts, half, *refs):
    q_ref, k_ref, v_ref = refs[:3]
    out_refs, sems = refs[3:-1], refs[-1]
    z = lax.axis_index("seq")
    copies = []
    for j in range(parts):
        cols = pl.ds(pl.multiple_of(lax.rem(z + j, parts) * half, LANES), half)
        copies.append(pltpu.make_async_copy(k_ref.at[:, cols], out_refs[j].at[0], sems.at[3 * j]))
        copies.append(pltpu.make_async_copy(v_ref.at[:, cols], out_refs[j].at[1], sems.at[3 * j + 1]))
        copies.append(pltpu.make_async_copy(q_ref.at[:, cols], out_refs[parts + j], sems.at[3 * j + 2]))
    for copy in copies:
        copy.start()
    for copy in copies:
        copy.wait()


def is_near(parts):
    return lax.axis_index("seq") // parts == lax.axis_index("guide")


def attend_kernel(parts, near_ref, far_ref, *refs):
    kv_refs, out_ref = refs[: 2 * parts], refs[2 * parts]
    near = is_near(parts)
    for i in range(near_ref.shape[1] // HEAD_DIM):
        cols = slice(i * HEAD_DIM, (i + 1) * HEAD_DIM)
        q = jnp.where(near, near_ref[:, cols], far_ref[:, cols])
        k = jnp.concatenate([r[0, :, cols] for r in kv_refs], axis=0)
        v = jnp.concatenate([r[1, :, cols] for r in kv_refs], axis=0)
        scores = lax.dot_general(q, k, (((1,), (1,)), ((), ())), preferred_element_type=F32)
        scores = scores * (HEAD_DIM ** (-0.5) * LOG2E)
        expo = jnp.exp2(scores - jnp.max(scores, axis=1, keepdims=True))
        total = jnp.sum(expo, axis=1, keepdims=True)
        mixed = jnp.dot(expo.astype(BF16), v, preferred_element_type=F32) / total
        out_ref[:, cols] = mixed.astype(BF16)


def attended_rows(parts, o_refs):
    near = is_near(parts)
    return [jnp.where(near, o_refs[j][...], o_refs[parts + j][...]) for j in range(parts)]


def project(parts, half, attended, w_ref, cols):
    z = lax.axis_index("seq")
    total = None
    for j in range(parts):
        start = pl.multiple_of(lax.rem(z + j, parts) * half, LANES)
        term = jnp.dot(attended[j], w_ref[pl.ds(start, half), cols], preferred_element_type=F32)
        total = term if total is None else total + term
    return total


def send_kernel(parts, half, chunk, first, *refs):
    near_ref, far_ref, out_ref = refs[2 * parts :]
    attended = attended_rows(parts, refs[: 2 * parts])
    guide = lax.axis_index("guide")
    for value, w_ref in ((1, near_ref), (0, far_ref)):

        @pl.when(guide == value)
        def _():
            for t in range(out_ref.shape[1] // chunk):
                cols = slice(first + t * chunk, first + (t + 1) * chunk)
                out_ref[:, t * chunk : (t + 1) * chunk] = project(parts, half, attended, w_ref, cols).astype(BF16)


def keep_kernel(parts, half, chunk, *refs):
    near_ref, far_ref, res_ref, gate_ref, out_ref = refs[2 * parts :]
    attended = attended_rows(parts, refs[: 2 * parts])
    guide = lax.axis_index("guide")
    for value, w_ref in ((0, near_ref), (1, far_ref)):

        @pl.when(guide == value)
        def _():
            for t in range(out_ref.shape[1] // chunk):
                cols = slice(t * chunk, (t + 1) * chunk)
                out_ref[:, cols] = res_ref[:, cols].astype(F32) + gate_ref[:, cols] * project(
                    parts, half, attended, w_ref, cols
                )


def split_dot(head_t, rows):
    dims = (((1,), (1,)), ((), ()))
    high = rows.astype(BF16)
    low = (rows - high.astype(F32)).astype(BF16)
    return lax.dot_general(head_t, high, dims, preferred_element_type=F32) + lax.dot_general(
        head_t, low, dims, preferred_element_type=F32
    )


def head_rows_kernel(scale_ref, shift_ref, head_ref, out_ref):
    width = scale_ref.shape[1]
    which = lax.broadcasted_iota(jnp.int32, (LANES, width), 0)
    rows = jnp.where(which == 0, 1.0 + scale_ref[...], shift_ref[...])
    high = rows.astype(BF16)
    rest = rows - high.astype(F32)
    mid = rest.astype(BF16)
    low = (rest - mid.astype(F32)).astype(BF16)
    dims = (((1,), (1,)), ((), ()))
    total = None
    for part in (high, mid, low):
        term = lax.dot_general(head_ref[...], part, dims, preferred_element_type=F32)
        total = term if total is None else total + term
    out_ref[...] = total


def head_kernel(first, last, chunk, start, *refs):
    hid_ref, got_ref, gate_ref, scale_ref, head_ref = refs[:5]
    if first:
        out_refs = refs[5:]
    else:
        prev_refs, out_refs = refs[5:8], refs[8:]
    channels = head_ref.shape[0]
    rows = hid_ref.shape[0]
    acc_one = jnp.zeros((rows, LANES), F32) if first else prev_refs[1][...]
    acc_two = jnp.zeros((rows, LANES), F32) if first else prev_refs[2][...]
    acc_head = jnp.zeros((channels, rows), F32) if first else prev_refs[0][...]
    for t in range(got_ref.shape[1] // chunk):
        cols = slice(start + t * chunk, start + (t + 1) * chunk)
        arrived = got_ref[:, t * chunk : (t + 1) * chunk].astype(F32)
        hidden = hid_ref[:, cols] + gate_ref[:, cols] * arrived
        for s in range(chunk // LANES):
            piece = hidden[:, s * LANES : (s + 1) * LANES]
            acc_one = acc_one + piece
            acc_two = acc_two + piece * piece
        acc_head = acc_head + split_dot(head_ref[:, cols], hidden * (1.0 + scale_ref[:, cols]))
    if last:
        out_ref = out_refs[0]
        out_ref[0:channels, :] = acc_head
        sum_one = jnp.sum(acc_one.T, axis=0, keepdims=True)
        sum_two = jnp.sum(acc_two.T, axis=0, keepdims=True)
        row = lax.broadcasted_iota(jnp.int32, (SUBLANES, rows), 0)
        out_ref[channels : channels + SUBLANES, :] = jnp.where(row == 0, sum_one, sum_two)
    else:
        out_refs[0][...] = acc_head
        out_refs[1][...] = acc_one
        out_refs[2][...] = acc_two


def norm_kernel(width_model, own_ref, got_ref, rows_own_ref, rows_got_ref, keep_ref, send_ref, eps_scr):
    channels = rows_own_ref.shape[0]
    half_channels = channels // 2
    guide = lax.axis_index("guide")
    head = own_ref[0:channels, :] + got_ref[0:channels, :]
    stats = own_ref[channels : channels + SUBLANES, :] + got_ref[channels : channels + SUBLANES, :]
    mean = stats[0:1] / width_model
    var = stats[1:2] / width_model - mean * mean
    inv_std = lax.rsqrt(var + norm_epsilon)
    scaled = rows_own_ref[:, 0:1] + rows_got_ref[:, 0:1]
    shifted = rows_own_ref[:, 1:2] + rows_got_ref[:, 1:2]
    eps_scr[...] = (head - mean * scaled) * inv_std + shifted
    keep_ref[...] = eps_scr[pl.ds(pl.multiple_of(guide * half_channels, SUBLANES), half_channels), :]
    send_ref[...] = eps_scr[pl.ds(pl.multiple_of((1 - guide) * half_channels, SUBLANES), half_channels), :]


def frame_kernel(seq_count, group, owner_ref, keep_ref, got_ref, *out_refs):
    z = lax.axis_index("seq")
    first = lax.axis_index("guide") == 0
    mine, other = keep_ref[...], got_ref[...]
    eps_cond = jnp.where(first, mine, other)
    eps_free = jnp.where(first, other, mine)
    guided = eps_free + guidance_scale * (eps_cond - eps_free)
    fold = LANES // group
    rows = guided.shape[0] // fold
    lane = lax.broadcasted_iota(jnp.int32, (rows, LANES), 1) // group
    for k in range(seq_count):
        target = lax.rem(z + k, seq_count)
        frame = jnp.int32(0)
        for f in range(seq_count):
            frame = jnp.where(owner_ref[0, f] == target, f, frame)
        packed = jnp.zeros((rows, LANES), F32)
        for j in range(fold):
            shift = lax.rem((j - frame) * group + LANES, LANES)
            rolled = pltpu.roll(guided[j * rows : (j + 1) * rows], shift, axis=1)
            packed = jnp.where(lane == j, rolled, packed)
        out_refs[k][...] = packed


def final_kernel(seq_count, group, steps_ref, noise_ref, *refs):
    piece_refs, out_ref = refs[:seq_count], refs[seq_count]
    z = lax.axis_index("seq")
    fold = LANES // group
    rows = piece_refs[0].shape[0]
    lane = lax.broadcasted_iota(jnp.int32, (rows, LANES), 1) // group
    blocks = []
    for j in range(fold):
        block = jnp.zeros((rows, LANES), F32)
        for k in range(seq_count):
            source = lax.rem(z - k + seq_count, seq_count)
            shift = lax.rem((source - j) * group + LANES, LANES)
            block = jnp.where(lane == source, pltpu.roll(piece_refs[k][...], shift, axis=1), block)
        blocks.append(block)
    framed = jnp.concatenate(blocks, axis=0)
    step = jnp.full((1, 1), steps_ref[0], jnp.int32)
    out_ref[...] = plan_weight(step) * (framed - noise_ref[...])


def call(kernel, outs, args, specs=None, scratch=(), flops=0, moved=0, grant=16):
    shapes = [jax.ShapeDtypeStruct(s, d) for s, d in outs]
    return pl.pallas_call(
        kernel,
        out_shape=shapes,
        in_specs=specs or [VMEM_SPEC] * len(args),
        out_specs=[VMEM_SPEC] * len(outs),
        scratch_shapes=list(scratch),
        compiler_params=pltpu.CompilerParams(vmem_limit_bytes=grant << 20),
        cost_estimate=pl.CostEstimate(flops=flops, bytes_accessed=moved, transcendentals=0),
    )(*args)


def fast_plan(
    queries, key_vecs, value_vecs, residual, w_out, attn_gate, norm_shift, norm_scale, w_head, noise,
    timesteps, frame_owner,
):
    seq_count = lax.axis_size("seq")
    parts = seq_count // 2
    rows, width_local = queries.shape[2:]
    half = width_local // parts
    width_shard = residual.shape[3]
    channels = w_head.shape[1]
    group = rows // seq_count
    width_model = float(width_shard * lax.axis_size("shard"))
    both = [(0, 1), (1, 0)]
    axes = ("seq", "guide")

    crossed = [(x * 2 + c, x * 2 + (c + x) % 2) for x in range(2) for c in range(2)]
    straight = [(x * 2 + c, x * 2 + (c + x + 1) % 2) for x in range(2) for c in range(2)]

    packed = call(
        functools.partial(pack_kernel, parts, half),
        [((2, rows, half), BF16)] * parts + [((rows, half), BF16)] * parts,
        [
            pltpu.with_memory_space_constraint(array[0, 0], pltpu.HBM)
            for array in (queries, key_vecs, value_vecs)
        ],
        [HBM_SPEC] * 3,
        [pltpu.SemaphoreType.DMA((3 * parts,))],
        moved=12 * rows * width_local,
    )
    there = [
        [
            (z * 2 + c, (parts * c + (z + j) % parts) * 2 + z // parts)
            for z in range(seq_count)
            for c in range(2)
        ]
        for j in range(parts)
    ]
    close = [[(a, b) for a, b in pairs if a // 2 // parts == a % 2] for pairs in there]
    apart = [[(a, b) for a, b in pairs if a // 2 // parts != a % 2] for pairs in there]
    q_near, q_far, kv_own, kv_other = [packed[parts]], [], [], []
    for j in range(1, parts):
        q_near.append(lax.ppermute(packed[parts + j], axes, close[j]))
    near_w = lax.ppermute(w_out, ("shard", "guide"), crossed)
    far_w = lax.ppermute(w_out, ("shard", "guide"), straight)
    for j in range(parts):
        kv_own.append(lax.ppermute(packed[j], axes, there[j]))
        kv_other.append(lax.ppermute(kv_own[j], "guide", both))
        q_far.append(lax.ppermute(packed[parts + j], axes, apart[j]))

    head_t = w_head.T
    rows_own = call(
        head_rows_kernel, [((channels, LANES), F32)], [norm_scale, norm_shift, head_t],
        moved=4 * width_shard * LANES,
    )[0]
    rows_got = lax.ppermute(rows_own, "shard", both)
    q_near[0], rows_own = lax.optimization_barrier((q_near[0], rows_own))

    o_near, o_far = [], []
    for j in range(parts):
        block = call(
            functools.partial(attend_kernel, parts),
            [((rows, half), BF16)],
            [q_near[j], q_far[j]] + kv_own + kv_other,
            flops=8 * rows * rows * parts * half,
            moved=2 * rows * half * parts * 5,
        )[0]
        o_far.append(lax.ppermute(block, axes, [(b, a) for a, b in apart[j]]))
        o_near.append(block if j == 0 else lax.ppermute(block, axes, [(b, a) for a, b in close[j]]))
    mixed = o_near + o_far

    chunk = 128
    pieces = 2
    width_piece = width_shard // pieces
    got = []
    for i in range(pieces):
        partial = call(
            functools.partial(send_kernel, parts, half, chunk, i * width_piece),
            [((rows, width_piece), BF16)],
            mixed + [near_w, far_w],
            flops=2 * rows * width_local * width_piece,
            moved=2 * width_local * width_piece,
        )[0]
        got.append(lax.ppermute(partial, "shard", both))
    hidden = call(
        functools.partial(keep_kernel, parts, half, chunk),
        [((rows, width_shard), F32)],
        mixed + [near_w, far_w, residual[0, 0], attn_gate],
        flops=2 * rows * width_local * width_shard,
        moved=2 * width_local * width_shard,
    )[0]
    state = []
    for i in range(pieces):
        first, last = i == 0, i == pieces - 1
        state = call(
            functools.partial(head_kernel, first, last, chunk, i * width_piece),
            [((channels + SUBLANES, rows), F32)]
            if last
            else [((channels, rows), F32), ((rows, LANES), F32), ((rows, LANES), F32)],
            [hidden, got[i], attn_gate, norm_scale, head_t] + list(state),
            flops=4 * rows * channels * width_piece,
            moved=6 * rows * width_piece,
        )
    sums = state[0]
    sums_got = lax.ppermute(sums, "shard", both)
    keep, send = call(
        functools.partial(norm_kernel, width_model),
        [((channels // 2, rows), F32)] * 2,
        [sums, sums_got, rows_own, rows_got],
        scratch=[pltpu.VMEM((channels, rows), F32)],
    )
    eps_got = lax.ppermute(send, "guide", both)
    fold = LANES // group
    frames = call(
        functools.partial(frame_kernel, seq_count, group),
        [((channels // 2 // fold, LANES), F32)] * seq_count,
        [frame_owner, keep, eps_got],
        [SMEM_SPEC, VMEM_SPEC, VMEM_SPEC],
    )
    arrived = [frames[0]] + [
        lax.ppermute(frames[k], "seq", [(z, (z + k) % seq_count) for z in range(seq_count)])
        for k in range(1, seq_count)
    ]
    out = call(
        functools.partial(final_kernel, seq_count, group),
        [((channels // 2, rows), F32)],
        [timesteps, noise[0, 0].T] + arrived,
        [SMEM_SPEC] + [VMEM_SPEC] * (seq_count + 1),
    )[0]
    return out.T[None, None]


def fast_fits(sizes, queries, residual, w_out, w_head):
    seq_count = sizes["seq"]
    step_count, rows, width_local = queries.shape[1:]
    channels = w_head.shape[1]
    if sizes["guide"] != 2 or sizes["shard"] != 2 or seq_count % 2 or step_count != 1 or rows != LANES:
        return False
    if width_local % (seq_count // 2 * HEAD_DIM) or residual.shape[3] % (4 * LANES):
        return False
    if w_out.shape[1] != residual.shape[3] or channels % (2 * SUBLANES):
        return False
    group = rows // seq_count
    if rows % seq_count or LANES % group:
        return False
    fold = LANES // group
    return channels // 2 % (fold * SUBLANES) == 0


def solution(mesh):
    sizes = dict(mesh.shape)

    def on_device(queries, key_vecs, value_vecs, residual, w_out, attn_gate, norm_shift, norm_scale, w_head, *rest):
        fits = fast_fits(sizes, queries, residual, w_out, w_head)
        plan = fast_plan if fits else general_plan
        return plan(queries, key_vecs, value_vecs, residual, w_out, attn_gate, norm_shift, norm_scale, w_head, *rest)

    return jax.shard_map(
        on_device,
        mesh=mesh,
        in_specs=(
            P("guide", "group", "seq", "shard"),
            P("guide", "group", "seq", "shard"),
            P("guide", "group", "seq", "shard"),
            P("guide", "group", "seq", "shard"),
            P("shard", "guide"),
            P("group", "shard"),
            P("group", "shard"),
            P("group", "shard"),
            P("shard", None),
            P("group", "seq", None, "guide"),
            P("group"),
            P("group", None),
        ),
        out_specs=P("group", "seq", None, "guide"),
        check_vma=False,
    )
```

```python
import functools

import jax
import jax.numpy as jnp
from jax import lax
from jax.experimental import pallas as pl
from jax.experimental.pallas import tpu as pltpu
from jax.sharding import PartitionSpec as P


HEAD_DIM = 128
LANES = 128
SUBLANES = 8
beta_low = 0.0001
beta_high = 0.02
guidance_scale = 3.0
norm_epsilon = 1e-06
LOG2E = 1.4426950408889634


F32 = jnp.float32
BF16 = jnp.bfloat16
VMEM_SPEC = pl.BlockSpec(memory_space=pltpu.VMEM)
SMEM_SPEC = pl.BlockSpec(memory_space=pltpu.SMEM)
HBM_SPEC = pl.BlockSpec(memory_space=pltpu.HBM)


def plan_weight(timesteps):
    steps_float = timesteps.astype(jnp.float32)
    exponent = (steps_float + 1.0) * beta_low + (beta_high - beta_low) * steps_float * (
        steps_float + 1.0
    ) / (2.0 * 999.0)
    return 1.0 - jnp.exp(-exponent)


def attend_all(query_split, keys_all, values_all):
    heads_local = query_split.shape[2]
    keys_split = keys_all.reshape(keys_all.shape[0], keys_all.shape[1], heads_local, HEAD_DIM)
    values_split = values_all.reshape(values_all.shape[0], values_all.shape[1], heads_local, HEAD_DIM)
    scores = jnp.einsum(
        "tqhd,tkhd->tqhk", query_split, keys_split, preferred_element_type=F32
    ) * HEAD_DIM ** (-0.5)
    expo = jnp.exp(scores - jnp.max(scores, axis=-1, keepdims=True))
    total = jnp.sum(expo, axis=-1)
    mixed = jnp.einsum("tqhk,tkhd->tqhd", expo.astype(BF16), values_split, preferred_element_type=F32)
    return (mixed / total[..., None]).astype(BF16)


def general_plan(
    queries, key_vecs, value_vecs, residual, w_out, attn_gate, norm_shift, norm_scale, w_head, noise,
    timesteps, frame_owner,
):
    query_local = queries[0]
    step_count, token_count, width_local = query_local.shape
    heads_local = width_local // HEAD_DIM
    attended = attend_all(
        query_local.reshape(step_count, token_count, heads_local, HEAD_DIM),
        lax.all_gather(key_vecs[0], "seq", axis=1, tiled=True),
        lax.all_gather(value_vecs[0], "seq", axis=1, tiled=True),
    )
    row_count = step_count * token_count
    both_rows = jnp.dot(
        lax.all_gather(attended.reshape(row_count, width_local), "guide", axis=0, tiled=True),
        w_out,
        preferred_element_type=F32,
    )
    half_width = w_out.shape[1]
    swapped = lax.all_to_all(
        both_rows.reshape(2, row_count, half_width), "guide", split_axis=0, concat_axis=2, tiled=True
    )
    projected = swapped.reshape(row_count, 2 * half_width)
    attn_out = lax.psum_scatter(projected, "shard", scatter_dimension=1, tiled=True)
    width_shard = attn_out.shape[1]
    width_model = width_shard * lax.axis_size("shard")
    hidden = residual[0].astype(F32) + attn_gate[:, None, :] * attn_out.reshape(
        step_count, token_count, width_shard
    )
    sum_first, sum_second = lax.psum((jnp.sum(hidden, axis=-1), jnp.sum(hidden * hidden, axis=-1)), "shard")
    mean_row = sum_first / width_model
    var_row = sum_second / width_model - mean_row * mean_row
    inv_std = lax.rsqrt(var_row + norm_epsilon)
    modulated = (hidden - mean_row[..., None]) * inv_std[..., None] * (
        1.0 + norm_scale[:, None, :]
    ) + norm_shift[:, None, :]
    partial_head = jnp.einsum(
        "tqd,dc->tqc", modulated, w_head.astype(F32), precision=lax.Precision.HIGHEST
    )
    predicted = lax.psum(partial_head, "shard")
    seq_count = lax.axis_size("seq")
    frame_group = token_count // seq_count
    frames_view = predicted.reshape(step_count, seq_count, frame_group, predicted.shape[-1])
    owner_table = (
        frame_owner[:, :, None] == jnp.arange(seq_count, dtype=jnp.int32)[None, None, :]
    ).astype(F32)
    by_owner = jnp.einsum("tfo,tfgc->togc", owner_table, frames_view, precision=lax.Precision.HIGHEST)
    arrived = lax.all_to_all(
        lax.all_to_all(by_owner[None], "seq", split_axis=2, concat_axis=3, tiled=True),
        "guide",
        split_axis=4,
        concat_axis=0,
        tiled=True,
    )
    guided = arrived[1] + guidance_scale * (arrived[0] - arrived[1])
    return plan_weight(timesteps)[:, None, None, None] * (guided - noise)


def pack_kernel(parts, half, *refs):
    q_ref, k_ref, v_ref = refs[:3]
    pair_refs, own_ref, full_refs, sems = refs[3 : 3 + parts], refs[3 + parts], refs[4 + parts : -1], refs[-1]
    z = lax.axis_index("seq")
    copies = []

    def copy(source, cols, target):
        copies.append(pltpu.make_async_copy(source.at[:, cols], target, sems.at[len(copies)]))
        copies[-1].start()

    for j in range(parts):
        cols = pl.ds(pl.multiple_of(lax.rem(z + j, parts) * half, LANES), half)
        copy(k_ref, cols, pair_refs[j].at[0])
        copy(v_ref, cols, pair_refs[j].at[1])
        if j == 0:
            copy(q_ref, cols, own_ref)
        else:
            for i, source in enumerate((k_ref, v_ref, q_ref)):
                copy(source, cols, full_refs[j - 1].at[i])
    for started in copies:
        started.wait()


def attend_kernel(parts, *refs):
    own_q_ref, own_kv_ref = refs[:2]
    near_refs = refs[2 : 1 + parts]
    far_refs = [refs[1 + parts + i * parts : 1 + parts + (i + 1) * parts] for i in range(2)]
    out_refs = refs[1 + 3 * parts :]
    rows = own_q_ref.shape[0]
    first = lax.axis_index("guide") == 0
    for i in range(own_q_ref.shape[1] // HEAD_DIM):
        cols = slice(i * HEAD_DIM, (i + 1) * HEAD_DIM)

        def gather(which):
            blocks = [own_kv_ref[which, :, cols]] + [r[which, :, cols] for r in near_refs]
            for a, b in zip(*far_refs):
                blocks.append(jnp.where(first, a[which, :, cols], b[which, :, cols]))
            return jnp.concatenate(blocks, axis=0)

        q = jnp.concatenate([own_q_ref[:, cols]] + [r[2, :, cols] for r in near_refs], axis=0)
        scores = lax.dot_general(q, gather(0), (((1,), (1,)), ((), ())), preferred_element_type=F32)
        scores = scores * (HEAD_DIM ** (-0.5) * LOG2E)
        expo = jnp.exp2(scores - jnp.max(scores, axis=1, keepdims=True))
        total = jnp.sum(expo, axis=1, keepdims=True)
        mixed = jnp.dot(expo.astype(BF16), gather(1), preferred_element_type=F32) / total
        for j in range(parts):
            out_refs[j][:, cols] = mixed[j * rows : (j + 1) * rows].astype(BF16)


def project(parts, half, attended, w_ref, cols):
    z = lax.axis_index("seq")
    total = None
    for j in range(parts):
        start = pl.multiple_of(lax.rem(z + j, parts) * half, LANES)
        term = jnp.dot(attended[j], w_ref[pl.ds(start, half), cols], preferred_element_type=F32)
        total = term if total is None else total + term
    return total


def send_kernel(parts, half, chunk, first, *refs):
    near_ref, far_ref, out_ref = refs[parts:]
    attended = [r[...] for r in refs[:parts]]
    guide = lax.axis_index("guide")
    for value, w_ref in ((1, near_ref), (0, far_ref)):

        @pl.when(guide == value)
        def _():
            for t in range(out_ref.shape[1] // chunk):
                cols = slice(first + t * chunk, first + (t + 1) * chunk)
                out_ref[:, t * chunk : (t + 1) * chunk] = project(parts, half, attended, w_ref, cols).astype(BF16)


def keep_kernel(parts, half, chunk, *refs):
    near_ref, far_ref, res_ref, gate_ref, out_ref = refs[parts:]
    attended = [r[...] for r in refs[:parts]]
    guide = lax.axis_index("guide")
    for value, w_ref in ((0, near_ref), (1, far_ref)):

        @pl.when(guide == value)
        def _():
            for t in range(out_ref.shape[1] // chunk):
                cols = slice(t * chunk, (t + 1) * chunk)
                out_ref[:, cols] = res_ref[:, cols].astype(F32) + gate_ref[:, cols] * project(
                    parts, half, attended, w_ref, cols
                )


def split_dot(head_t, rows):
    dims = (((1,), (1,)), ((), ()))
    high = rows.astype(BF16)
    low = (rows - high.astype(F32)).astype(BF16)
    return lax.dot_general(head_t, high, dims, preferred_element_type=F32) + lax.dot_general(
        head_t, low, dims, preferred_element_type=F32
    )


def head_rows_kernel(scale_ref, shift_ref, head_ref, out_ref):
    width = scale_ref.shape[1]
    which = lax.broadcasted_iota(jnp.int32, (LANES, width), 0)
    rows = jnp.where(which == 0, 1.0 + scale_ref[...], shift_ref[...])
    high = rows.astype(BF16)
    rest = rows - high.astype(F32)
    mid = rest.astype(BF16)
    low = (rest - mid.astype(F32)).astype(BF16)
    dims = (((1,), (1,)), ((), ()))
    total = None
    for part in (high, mid, low):
        term = lax.dot_general(head_ref[...], part, dims, preferred_element_type=F32)
        total = term if total is None else total + term
    out_ref[...] = total


def head_kernel(first, last, chunk, start, *refs):
    hid_ref, got_ref, gate_ref, scale_ref, head_ref = refs[:5]
    if first:
        out_refs = refs[5:]
    else:
        prev_refs, out_refs = refs[5:8], refs[8:]
    channels = head_ref.shape[0]
    rows = hid_ref.shape[0]
    acc_one = jnp.zeros((rows, LANES), F32) if first else prev_refs[1][...]
    acc_two = jnp.zeros((rows, LANES), F32) if first else prev_refs[2][...]
    acc_head = jnp.zeros((channels, rows), F32) if first else prev_refs[0][...]
    for t in range(got_ref.shape[1] // chunk):
        cols = slice(start + t * chunk, start + (t + 1) * chunk)
        arrived = got_ref[:, t * chunk : (t + 1) * chunk].astype(F32)
        hidden = hid_ref[:, cols] + gate_ref[:, cols] * arrived
        for s in range(chunk // LANES):
            piece = hidden[:, s * LANES : (s + 1) * LANES]
            acc_one = acc_one + piece
            acc_two = acc_two + piece * piece
        acc_head = acc_head + split_dot(head_ref[:, cols], hidden * (1.0 + scale_ref[:, cols]))
    if last:
        out_ref = out_refs[0]
        out_ref[0:channels, :] = acc_head
        sum_one = jnp.sum(acc_one.T, axis=0, keepdims=True)
        sum_two = jnp.sum(acc_two.T, axis=0, keepdims=True)
        row = lax.broadcasted_iota(jnp.int32, (SUBLANES, rows), 0)
        out_ref[channels : channels + SUBLANES, :] = jnp.where(row == 0, sum_one, sum_two)
    else:
        out_refs[0][...] = acc_head
        out_refs[1][...] = acc_one
        out_refs[2][...] = acc_two


def norm_kernel(width_model, own_ref, got_ref, rows_own_ref, rows_got_ref, keep_ref, send_ref, eps_scr):
    channels = rows_own_ref.shape[0]
    half_channels = channels // 2
    guide = lax.axis_index("guide")
    head = own_ref[0:channels, :] + got_ref[0:channels, :]
    stats = own_ref[channels : channels + SUBLANES, :] + got_ref[channels : channels + SUBLANES, :]
    mean = stats[0:1] / width_model
    var = stats[1:2] / width_model - mean * mean
    inv_std = lax.rsqrt(var + norm_epsilon)
    scaled = rows_own_ref[:, 0:1] + rows_got_ref[:, 0:1]
    shifted = rows_own_ref[:, 1:2] + rows_got_ref[:, 1:2]
    eps_scr[...] = (head - mean * scaled) * inv_std + shifted
    keep_ref[...] = eps_scr[pl.ds(pl.multiple_of(guide * half_channels, SUBLANES), half_channels), :]
    send_ref[...] = eps_scr[pl.ds(pl.multiple_of((1 - guide) * half_channels, SUBLANES), half_channels), :]


def frame_kernel(seq_count, group, owner_ref, keep_ref, got_ref, *out_refs):
    z = lax.axis_index("seq")
    first = lax.axis_index("guide") == 0
    mine, other = keep_ref[...], got_ref[...]
    eps_cond = jnp.where(first, mine, other)
    eps_free = jnp.where(first, other, mine)
    guided = eps_free + guidance_scale * (eps_cond - eps_free)
    fold = LANES // group
    rows = guided.shape[0] // fold
    lane = lax.broadcasted_iota(jnp.int32, (rows, LANES), 1) // group
    for k in range(seq_count):
        target = z ^ k
        frame = jnp.int32(0)
        for f in range(seq_count):
            frame = jnp.where(owner_ref[0, f] == target, f, frame)
        packed = jnp.zeros((rows, LANES), F32)
        for j in range(fold):
            shift = lax.rem((j - frame) * group + LANES, LANES)
            rolled = pltpu.roll(guided[j * rows : (j + 1) * rows], shift, axis=1)
            packed = jnp.where(lane == j, rolled, packed)
        out_refs[k][...] = packed


def final_kernel(seq_count, group, steps_ref, noise_ref, *refs):
    piece_refs, out_ref = refs[:seq_count], refs[seq_count]
    z = lax.axis_index("seq")
    fold = LANES // group
    rows = piece_refs[0].shape[0]
    lane = lax.broadcasted_iota(jnp.int32, (rows, LANES), 1) // group
    blocks = []
    for j in range(fold):
        block = jnp.zeros((rows, LANES), F32)
        for k in range(seq_count):
            source = z ^ k
            shift = lax.rem((source - j) * group + LANES, LANES)
            block = jnp.where(lane == source, pltpu.roll(piece_refs[k][...], shift, axis=1), block)
        blocks.append(block)
    framed = jnp.concatenate(blocks, axis=0)
    step = jnp.full((1, 1), steps_ref[0], jnp.int32)
    out_ref[...] = plan_weight(step) * (framed - noise_ref[...])


def call(kernel, outs, args, specs=None, scratch=(), flops=0, moved=0, grant=16):
    shapes = [jax.ShapeDtypeStruct(s, d) for s, d in outs]
    return pl.pallas_call(
        kernel,
        out_shape=shapes,
        in_specs=specs or [VMEM_SPEC] * len(args),
        out_specs=[VMEM_SPEC] * len(outs),
        scratch_shapes=list(scratch),
        compiler_params=pltpu.CompilerParams(vmem_limit_bytes=grant << 20),
        cost_estimate=pl.CostEstimate(flops=flops, bytes_accessed=moved, transcendentals=0),
    )(*args)


def fast_plan(
    queries, key_vecs, value_vecs, residual, w_out, attn_gate, norm_shift, norm_scale, w_head, noise,
    timesteps, frame_owner,
):
    seq_count = lax.axis_size("seq")
    parts = seq_count // 2
    rows, width_local = queries.shape[2:]
    half = width_local // parts
    width_shard = residual.shape[3]
    channels = w_head.shape[1]
    group = rows // seq_count
    width_model = float(width_shard * lax.axis_size("shard"))
    both = [(0, 1), (1, 0)]

    crossed = [(x * 2 + c, x * 2 + (c + x) % 2) for x in range(2) for c in range(2)]
    straight = [(x * 2 + c, x * 2 + (c + x + 1) % 2) for x in range(2) for c in range(2)]

    packed = call(
        functools.partial(pack_kernel, parts, half),
        [((2, rows, half), BF16)] * parts + [((rows, half), BF16)] + [((3, rows, half), BF16)] * (parts - 1),
        [
            pltpu.with_memory_space_constraint(array[0, 0], pltpu.HBM)
            for array in (queries, key_vecs, value_vecs)
        ],
        [HBM_SPEC] * 3,
        [pltpu.SemaphoreType.DMA((5 * parts,))],
        moved=12 * rows * width_local,
    )
    kv_sent, q_own, full_sent = packed[:parts], packed[parts], packed[parts + 1 :]

    def to_part(z, j, across):
        return (z // parts + across) % 2 * parts + (z + j) % parts

    def far_pairs(j, core):
        return [(z * 2 + core, to_part(z, j, 1) * 2 + core) for z in range(seq_count)]

    axes = ("seq", "guide")
    near_pairs = [[(z, to_part(z, j, 0)) for z in range(seq_count)] for j in range(parts)]
    far = [[lax.ppermute(kv_sent[j], axes, far_pairs(j, 0)) for j in range(parts)]]
    near = [lax.ppermute(full_sent[j - 1], "seq", near_pairs[j]) for j in range(1, parts)]
    near_w = lax.ppermute(w_out, ("shard", "guide"), crossed)
    far_w = lax.ppermute(w_out, ("shard", "guide"), straight)
    far.append([lax.ppermute(kv_sent[j], axes, far_pairs(j, 1)) for j in range(parts)])

    head_t = w_head.T
    rows_own = call(
        head_rows_kernel, [((channels, LANES), F32)], [norm_scale, norm_shift, head_t],
        moved=4 * width_shard * LANES,
    )[0]
    rows_got = lax.ppermute(rows_own, "shard", both)
    q_own, rows_own = lax.optimization_barrier((q_own, rows_own))

    mixed = call(
        functools.partial(attend_kernel, parts),
        [((rows, half), BF16)] * parts,
        [q_own, kv_sent[0]] + near + far[0] + far[1],
        flops=8 * rows * parts * rows * parts * half,
        moved=2 * rows * half * parts * 6,
    )
    mixed = [mixed[0]] + [lax.ppermute(mixed[j], "seq", [(b, a) for a, b in near_pairs[j]]) for j in range(1, parts)]

    chunk = 128
    pieces = 2
    width_piece = width_shard // pieces
    got = []
    for i in range(pieces):
        partial = call(
            functools.partial(send_kernel, parts, half, chunk, i * width_piece),
            [((rows, width_piece), BF16)],
            mixed + [near_w, far_w],
            flops=2 * rows * width_local * width_piece,
            moved=2 * width_local * width_piece,
        )[0]
        got.append(lax.ppermute(partial, "shard", both))
    hidden = call(
        functools.partial(keep_kernel, parts, half, chunk),
        [((rows, width_shard), F32)],
        mixed + [near_w, far_w, residual[0, 0], attn_gate],
        flops=2 * rows * width_local * width_shard,
        moved=2 * width_local * width_shard,
    )[0]
    state = []
    for i in range(pieces):
        first, last = i == 0, i == pieces - 1
        state = call(
            functools.partial(head_kernel, first, last, chunk, i * width_piece),
            [((channels + SUBLANES, rows), F32)]
            if last
            else [((channels, rows), F32), ((rows, LANES), F32), ((rows, LANES), F32)],
            [hidden, got[i], attn_gate, norm_scale, head_t] + list(state),
            flops=4 * rows * channels * width_piece,
            moved=6 * rows * width_piece,
        )
    sums = state[0]
    sums_got = lax.ppermute(sums, "shard", both)
    keep, send = call(
        functools.partial(norm_kernel, width_model),
        [((channels // 2, rows), F32)] * 2,
        [sums, sums_got, rows_own, rows_got],
        scratch=[pltpu.VMEM((channels, rows), F32)],
    )
    eps_got = lax.ppermute(send, "guide", both)
    fold = LANES // group
    frames = call(
        functools.partial(frame_kernel, seq_count, group),
        [((channels // 2 // fold, LANES), F32)] * seq_count,
        [frame_owner, keep, eps_got],
        [SMEM_SPEC, VMEM_SPEC, VMEM_SPEC],
    )
    arrived = [frames[0]] + [
        lax.ppermute(frames[k], "seq", [(z, z ^ k) for z in range(seq_count)])
        for k in range(1, seq_count)
    ]
    out = call(
        functools.partial(final_kernel, seq_count, group),
        [((channels // 2, rows), F32)],
        [timesteps, noise[0, 0].T] + arrived,
        [SMEM_SPEC] + [VMEM_SPEC] * (seq_count + 1),
    )[0]
    return out.T[None, None]


def fast_fits(sizes, queries, residual, w_out, w_head):
    seq_count = sizes["seq"]
    step_count, rows, width_local = queries.shape[1:]
    channels = w_head.shape[1]
    if seq_count < 2 or sizes["guide"] != 2 or sizes["shard"] != 2 or seq_count & (seq_count - 1) or step_count != 1 or rows != LANES:
        return False
    if width_local % (seq_count // 2 * HEAD_DIM) or residual.shape[3] % (4 * LANES):
        return False
    if w_out.shape[1] != residual.shape[3] or channels % (2 * SUBLANES):
        return False
    group = rows // seq_count
    if rows % seq_count or LANES % group:
        return False
    fold = LANES // group
    return channels // 2 % (fold * SUBLANES) == 0


def solution(mesh):
    sizes = dict(mesh.shape)

    def on_device(queries, key_vecs, value_vecs, residual, w_out, attn_gate, norm_shift, norm_scale, w_head, *rest):
        fits = fast_fits(sizes, queries, residual, w_out, w_head)
        plan = fast_plan if fits else general_plan
        return plan(queries, key_vecs, value_vecs, residual, w_out, attn_gate, norm_shift, norm_scale, w_head, *rest)

    return jax.shard_map(
        on_device,
        mesh=mesh,
        in_specs=(
            P("guide", "group", "seq", "shard"),
            P("guide", "group", "seq", "shard"),
            P("guide", "group", "seq", "shard"),
            P("guide", "group", "seq", "shard"),
            P("shard", "guide"),
            P("group", "shard"),
            P("group", "shard"),
            P("group", "shard"),
            P("shard", None),
            P("group", "seq", None, "guide"),
            P("group"),
            P("group", None),
        ),
        out_specs=P("group", "seq", None, "guide"),
        check_vma=False,
    )
```

```python
import functools

import jax
import jax.numpy as jnp
from jax import lax
from jax.experimental import pallas as pl
from jax.experimental.pallas import tpu as pltpu
from jax.sharding import PartitionSpec as P


HEAD_DIM = 128
LANES = 128
SUBLANES = 8
beta_low = 0.0001
beta_high = 0.02
guidance_scale = 3.0
norm_epsilon = 1e-06
LOG2E = 1.4426950408889634


F32 = jnp.float32
BF16 = jnp.bfloat16
VMEM_SPEC = pl.BlockSpec(memory_space=pltpu.VMEM)
SMEM_SPEC = pl.BlockSpec(memory_space=pltpu.SMEM)
HBM_SPEC = pl.BlockSpec(memory_space=pltpu.HBM)


def plan_weight(timesteps):
    steps_float = timesteps.astype(jnp.float32)
    exponent = (steps_float + 1.0) * beta_low + (beta_high - beta_low) * steps_float * (
        steps_float + 1.0
    ) / (2.0 * 999.0)
    return 1.0 - jnp.exp(-exponent)


def attend_all(query_split, keys_all, values_all):
    heads_local = query_split.shape[2]
    keys_split = keys_all.reshape(keys_all.shape[0], keys_all.shape[1], heads_local, HEAD_DIM)
    values_split = values_all.reshape(values_all.shape[0], values_all.shape[1], heads_local, HEAD_DIM)
    scores = jnp.einsum(
        "tqhd,tkhd->tqhk", query_split, keys_split, preferred_element_type=F32
    ) * HEAD_DIM ** (-0.5)
    expo = jnp.exp(scores - jnp.max(scores, axis=-1, keepdims=True))
    total = jnp.sum(expo, axis=-1)
    mixed = jnp.einsum("tqhk,tkhd->tqhd", expo.astype(BF16), values_split, preferred_element_type=F32)
    return (mixed / total[..., None]).astype(BF16)


def general_plan(
    queries, key_vecs, value_vecs, residual, w_out, attn_gate, norm_shift, norm_scale, w_head, noise,
    timesteps, frame_owner,
):
    query_local = queries[0]
    step_count, token_count, width_local = query_local.shape
    heads_local = width_local // HEAD_DIM
    attended = attend_all(
        query_local.reshape(step_count, token_count, heads_local, HEAD_DIM),
        lax.all_gather(key_vecs[0], "seq", axis=1, tiled=True),
        lax.all_gather(value_vecs[0], "seq", axis=1, tiled=True),
    )
    row_count = step_count * token_count
    both_rows = jnp.dot(
        lax.all_gather(attended.reshape(row_count, width_local), "guide", axis=0, tiled=True),
        w_out,
        preferred_element_type=F32,
    )
    half_width = w_out.shape[1]
    swapped = lax.all_to_all(
        both_rows.reshape(2, row_count, half_width), "guide", split_axis=0, concat_axis=2, tiled=True
    )
    projected = swapped.reshape(row_count, 2 * half_width)
    attn_out = lax.psum_scatter(projected, "shard", scatter_dimension=1, tiled=True)
    width_shard = attn_out.shape[1]
    width_model = width_shard * lax.axis_size("shard")
    hidden = residual[0].astype(F32) + attn_gate[:, None, :] * attn_out.reshape(
        step_count, token_count, width_shard
    )
    sum_first, sum_second = lax.psum((jnp.sum(hidden, axis=-1), jnp.sum(hidden * hidden, axis=-1)), "shard")
    mean_row = sum_first / width_model
    var_row = sum_second / width_model - mean_row * mean_row
    inv_std = lax.rsqrt(var_row + norm_epsilon)
    modulated = (hidden - mean_row[..., None]) * inv_std[..., None] * (
        1.0 + norm_scale[:, None, :]
    ) + norm_shift[:, None, :]
    partial_head = jnp.einsum(
        "tqd,dc->tqc", modulated, w_head.astype(F32), precision=lax.Precision.HIGHEST
    )
    predicted = lax.psum(partial_head, "shard")
    seq_count = lax.axis_size("seq")
    frame_group = token_count // seq_count
    frames_view = predicted.reshape(step_count, seq_count, frame_group, predicted.shape[-1])
    owner_table = (
        frame_owner[:, :, None] == jnp.arange(seq_count, dtype=jnp.int32)[None, None, :]
    ).astype(F32)
    by_owner = jnp.einsum("tfo,tfgc->togc", owner_table, frames_view, precision=lax.Precision.HIGHEST)
    arrived = lax.all_to_all(
        lax.all_to_all(by_owner[None], "seq", split_axis=2, concat_axis=3, tiled=True),
        "guide",
        split_axis=4,
        concat_axis=0,
        tiled=True,
    )
    guided = arrived[1] + guidance_scale * (arrived[0] - arrived[1])
    return plan_weight(timesteps)[:, None, None, None] * (guided - noise)


def pack_kernel(parts, half, count, *refs):
    source_refs, out_refs, sems = refs[:count], refs[count:-1], refs[-1]
    z = lax.axis_index("seq")
    copies = []
    for j in range(parts):
        cols = pl.ds(pl.multiple_of(lax.rem(z + j, parts) * half, LANES), half)
        for i in range(count):
            copies.append(
                pltpu.make_async_copy(source_refs[i].at[:, cols], out_refs[j].at[i], sems.at[j * count + i])
            )
    for copy in copies:
        copy.start()
    for copy in copies:
        copy.wait()


def attend_kernel(parts, *refs):
    q_refs = refs[:parts]
    kv_refs = refs[parts : 3 * parts]
    o_refs = refs[3 * parts :]
    rows = q_refs[0].shape[1]
    for i in range(q_refs[0].shape[2] // HEAD_DIM):
        cols = slice(i * HEAD_DIM, (i + 1) * HEAD_DIM)
        q = jnp.concatenate([r[0, :, cols] for r in q_refs], axis=0)
        k = jnp.concatenate([r[0, :, cols] for r in kv_refs], axis=0)
        v = jnp.concatenate([r[1, :, cols] for r in kv_refs], axis=0)
        scores = lax.dot_general(q, k, (((1,), (1,)), ((), ())), preferred_element_type=F32)
        scores = scores * (HEAD_DIM ** (-0.5) * LOG2E)
        expo = jnp.exp2(scores - jnp.max(scores, axis=1, keepdims=True))
        total = jnp.sum(expo, axis=1, keepdims=True)
        mixed = jnp.dot(expo.astype(BF16), v, preferred_element_type=F32) / total
        for j in range(parts):
            o_refs[j][:, cols] = mixed[j * rows : (j + 1) * rows].astype(BF16)


def project(parts, half, o_refs, w_ref, cols):
    z = lax.axis_index("seq")
    total = None
    for j in range(parts):
        start = pl.multiple_of(lax.rem(z + j, parts) * half, LANES)
        term = jnp.dot(o_refs[j][...], w_ref[pl.ds(start, half), cols], preferred_element_type=F32)
        total = term if total is None else total + term
    return total


def send_kernel(parts, half, chunk, first, *refs):
    o_refs = refs[:parts]
    near_ref, far_ref, out_ref = refs[parts:]
    guide = lax.axis_index("guide")
    for value, w_ref in ((1, near_ref), (0, far_ref)):

        @pl.when(guide == value)
        def _():
            for t in range(out_ref.shape[1] // chunk):
                cols = slice(first + t * chunk, first + (t + 1) * chunk)
                out_ref[:, t * chunk : (t + 1) * chunk] = project(parts, half, o_refs, w_ref, cols).astype(BF16)


def keep_kernel(parts, half, chunk, *refs):
    o_refs = refs[:parts]
    near_ref, far_ref, res_ref, gate_ref, out_ref = refs[parts:]
    guide = lax.axis_index("guide")
    for value, w_ref in ((0, near_ref), (1, far_ref)):

        @pl.when(guide == value)
        def _():
            for t in range(out_ref.shape[1] // chunk):
                cols = slice(t * chunk, (t + 1) * chunk)
                out_ref[:, cols] = res_ref[:, cols].astype(F32) + gate_ref[:, cols] * project(
                    parts, half, o_refs, w_ref, cols
                )


def split_dot(head_t, rows):
    dims = (((1,), (1,)), ((), ()))
    high = rows.astype(BF16)
    low = (rows - high.astype(F32)).astype(BF16)
    return lax.dot_general(head_t, high, dims, preferred_element_type=F32) + lax.dot_general(
        head_t, low, dims, preferred_element_type=F32
    )


def early_kernel(seq_count, scale_ref, shift_ref, head_ref, owner_ref, steps_ref, out_ref, chosen_ref, weight_ref):
    z = lax.axis_index("seq")
    for k in range(seq_count):
        for f in range(seq_count):
            here = jnp.where(owner_ref[0, f] == z ^ k, 1.0, 0.0)
            chosen_ref[k * seq_count + f : k * seq_count + f + 1, :] = jnp.full((1, LANES), here, F32)
    weight_ref[...] = plan_weight(jnp.full((SUBLANES, LANES), steps_ref[0], jnp.int32))
    width = scale_ref.shape[1]
    which = lax.broadcasted_iota(jnp.int32, (LANES, width), 0)
    rows = jnp.where(which == 0, 1.0 + scale_ref[...], shift_ref[...])
    high = rows.astype(BF16)
    rest = rows - high.astype(F32)
    mid = rest.astype(BF16)
    low = (rest - mid.astype(F32)).astype(BF16)
    dims = (((1,), (1,)), ((), ()))
    total = None
    for part in (high, mid, low):
        term = lax.dot_general(head_ref[...], part, dims, preferred_element_type=F32)
        total = term if total is None else total + term
    out_ref[...] = total


def head_kernel(first, last, chunk, start, *refs):
    hid_ref, got_ref, gate_ref, scale_ref, head_ref = refs[:5]
    if first:
        out_refs = refs[5:]
    else:
        prev_refs, out_refs = refs[5:8], refs[8:]
    channels = head_ref.shape[0]
    rows = hid_ref.shape[0]
    acc_one = jnp.zeros((rows, LANES), F32) if first else prev_refs[1][...]
    acc_two = jnp.zeros((rows, LANES), F32) if first else prev_refs[2][...]
    acc_head = jnp.zeros((channels, rows), F32) if first else prev_refs[0][...]
    for t in range(got_ref.shape[1] // chunk):
        cols = slice(start + t * chunk, start + (t + 1) * chunk)
        arrived = got_ref[:, t * chunk : (t + 1) * chunk].astype(F32)
        hidden = hid_ref[:, cols] + gate_ref[:, cols] * arrived
        for s in range(chunk // LANES):
            piece = hidden[:, s * LANES : (s + 1) * LANES]
            acc_one = acc_one + piece
            acc_two = acc_two + piece * piece
        acc_head = acc_head + split_dot(head_ref[:, cols], hidden * (1.0 + scale_ref[:, cols]))
    if last:
        out_ref = out_refs[0]
        out_ref[0:channels, :] = acc_head
        sum_one = jnp.sum(acc_one.T, axis=0, keepdims=True)
        sum_two = jnp.sum(acc_two.T, axis=0, keepdims=True)
        row = lax.broadcasted_iota(jnp.int32, (SUBLANES, rows), 0)
        out_ref[channels : channels + SUBLANES, :] = jnp.where(row == 0, sum_one, sum_two)
    else:
        out_refs[0][...] = acc_head
        out_refs[1][...] = acc_one
        out_refs[2][...] = acc_two


def norm_kernel(width_model, own_ref, got_ref, rows_own_ref, rows_got_ref, keep_ref, send_ref, eps_scr):
    channels = rows_own_ref.shape[0]
    half_channels = channels // 2
    guide = lax.axis_index("guide")
    head = own_ref[0:channels, :] + got_ref[0:channels, :]
    stats = own_ref[channels : channels + SUBLANES, :] + got_ref[channels : channels + SUBLANES, :]
    mean = stats[0:1] / width_model
    var = stats[1:2] / width_model - mean * mean
    inv_std = lax.rsqrt(var + norm_epsilon)
    scaled = rows_own_ref[:, 0:1] + rows_got_ref[:, 0:1]
    shifted = rows_own_ref[:, 1:2] + rows_got_ref[:, 1:2]
    eps_scr[...] = (head - mean * scaled) * inv_std + shifted
    keep_ref[...] = eps_scr[pl.ds(pl.multiple_of(guide * half_channels, SUBLANES), half_channels), :]
    send_ref[...] = eps_scr[pl.ds(pl.multiple_of((1 - guide) * half_channels, SUBLANES), half_channels), :]


def frame_kernel(seq_count, group, chosen_ref, keep_ref, got_ref, *out_refs):
    first = lax.axis_index("guide") == 0
    mine, other = keep_ref[...], got_ref[...]
    eps_cond = jnp.where(first, mine, other)
    eps_free = jnp.where(first, other, mine)
    guided = eps_free + guidance_scale * (eps_cond - eps_free)
    fold = LANES // group
    rows = guided.shape[0] // fold
    lane = lax.broadcasted_iota(jnp.int32, (rows, LANES), 1) // group
    packed = []
    for f in range(seq_count):
        block = jnp.zeros((rows, LANES), F32)
        for j in range(fold):
            piece = guided[j * rows : (j + 1) * rows]
            shift = (j - f) * group % LANES
            block = jnp.where(lane == j, pltpu.roll(piece, shift, axis=1) if shift else piece, block)
        packed.append(block)
    for k in range(seq_count):
        block = packed[0]
        for f in range(1, seq_count):
            block = jnp.where(chosen_ref[k * seq_count + f : k * seq_count + f + 1, :] > 0.5, packed[f], block)
        out_refs[k][...] = block


def final_kernel(seq_count, group, weight_ref, noise_ref, *refs):
    piece_refs, out_ref = refs[:seq_count], refs[seq_count]
    z = lax.axis_index("seq")
    fold = LANES // group
    rows = piece_refs[0].shape[0]
    lane = lax.broadcasted_iota(jnp.int32, (rows, LANES), 1) // group
    for j in range(fold):
        block = jnp.zeros((rows, LANES), F32)
        for k in range(seq_count):
            source = z ^ k
            shift = lax.rem((source - j) * group + LANES, LANES)
            block = jnp.where(lane == source, pltpu.roll(piece_refs[k][...], shift, axis=1), block)
        part = slice(j * rows, (j + 1) * rows)
        out_ref[part, :] = weight_ref[0:1, :] * (block - noise_ref[part, :])


def call(kernel, outs, args, specs=None, scratch=(), flops=0, moved=0, grant=16):
    shapes = [jax.ShapeDtypeStruct(s, d) for s, d in outs]
    return pl.pallas_call(
        kernel,
        out_shape=shapes,
        in_specs=specs or [VMEM_SPEC] * len(args),
        out_specs=[VMEM_SPEC] * len(outs),
        scratch_shapes=list(scratch),
        compiler_params=pltpu.CompilerParams(vmem_limit_bytes=grant << 20),
        cost_estimate=pl.CostEstimate(flops=flops, bytes_accessed=moved, transcendentals=0),
    )(*args)


def fast_plan(
    queries, key_vecs, value_vecs, residual, w_out, attn_gate, norm_shift, norm_scale, w_head, noise,
    timesteps, frame_owner,
):
    seq_count = lax.axis_size("seq")
    parts = seq_count // 2
    rows, width_local = queries.shape[2:]
    half = width_local // parts
    width_shard = residual.shape[3]
    channels = w_head.shape[1]
    group = rows // seq_count
    width_model = float(width_shard * lax.axis_size("shard"))
    both = [(0, 1), (1, 0)]
    axes = ("seq", "guide")

    crossed = [(x * 2 + c, x * 2 + (c + x) % 2) for x in range(2) for c in range(2)]
    straight = [(x * 2 + c, x * 2 + (c + x + 1) % 2) for x in range(2) for c in range(2)]

    def pack(*arrays):
        return call(
            functools.partial(pack_kernel, parts, half, len(arrays)),
            [((len(arrays), rows, half), BF16)] * parts,
            [pltpu.with_memory_space_constraint(array[0, 0], pltpu.HBM) for array in arrays],
            [HBM_SPEC] * len(arrays),
            [pltpu.SemaphoreType.DMA((parts * len(arrays),))],
            moved=4 * len(arrays) * rows * width_local,
        )

    kv_sent = pack(key_vecs, value_vecs)
    there = [
        [
            (z * 2 + c, (parts * c + (z + j) % parts) * 2 + z // parts)
            for z in range(seq_count)
            for c in range(2)
        ]
        for j in range(parts)
    ]
    back = [[(b, a) for a, b in pairs] for pairs in there]
    kv_own = [lax.ppermute(kv_sent[j], axes, there[j]) for j in range(parts)]
    q_sent = pack(queries)
    q_own = [lax.ppermute(q_sent[j], axes, there[j]) for j in range(parts)]
    near_w = lax.ppermute(w_out, ("shard", "guide"), crossed)
    far_w = lax.ppermute(w_out, ("shard", "guide"), straight)
    kv_other = [lax.ppermute(block, "guide", both) for block in kv_own]

    head_t = w_head.T
    rows_own, chosen, weight = call(
        functools.partial(early_kernel, seq_count),
        [((channels, LANES), F32), ((seq_count * seq_count, LANES), F32), ((SUBLANES, LANES), F32)],
        [norm_scale, norm_shift, head_t, frame_owner, timesteps],
        [VMEM_SPEC] * 3 + [SMEM_SPEC] * 2,
        moved=4 * width_shard * LANES,
    )
    rows_got = lax.ppermute(rows_own, "shard", both)
    *q_own, rows_own = lax.optimization_barrier((*q_own, rows_own))

    mixed = call(
        functools.partial(attend_kernel, parts),
        [((rows, half), BF16)] * parts,
        q_own + kv_own + kv_other,
        flops=8 * rows * parts * rows * parts * half,
        moved=2 * rows * half * parts * 6,
    )
    mixed = [lax.ppermute(mixed[j], axes, back[j]) for j in range(parts)]

    chunk = 128
    pieces = 4
    width_piece = width_shard // pieces
    got = []
    for i in range(pieces):
        partial = call(
            functools.partial(send_kernel, parts, half, chunk, i * width_piece),
            [((rows, width_piece), BF16)],
            mixed + [near_w, far_w],
            flops=2 * rows * width_local * width_piece,
            moved=2 * width_local * width_piece,
        )[0]
        got.append(lax.ppermute(partial, "shard", both))
    hidden = call(
        functools.partial(keep_kernel, parts, half, chunk),
        [((rows, width_shard), F32)],
        mixed + [near_w, far_w, residual[0, 0], attn_gate],
        flops=2 * rows * width_local * width_shard,
        moved=2 * width_local * width_shard,
    )[0]
    state = []
    for i in range(pieces):
        first, last = i == 0, i == pieces - 1
        state = call(
            functools.partial(head_kernel, first, last, chunk, i * width_piece),
            [((channels + SUBLANES, rows), F32)]
            if last
            else [((channels, rows), F32), ((rows, LANES), F32), ((rows, LANES), F32)],
            [hidden, got[i], attn_gate, norm_scale, head_t] + list(state),
            flops=4 * rows * channels * width_piece,
            moved=6 * rows * width_piece,
        )
    sums = state[0]
    sums_got = lax.ppermute(sums, "shard", both)
    keep, send = call(
        functools.partial(norm_kernel, width_model),
        [((channels // 2, rows), F32)] * 2,
        [sums, sums_got, rows_own, rows_got],
        scratch=[pltpu.VMEM((channels, rows), F32)],
    )
    eps_got = lax.ppermute(send, "guide", both)
    fold = LANES // group
    frames = call(
        functools.partial(frame_kernel, seq_count, group),
        [((channels // 2 // fold, LANES), F32)] * seq_count,
        [chosen, keep, eps_got],
    )
    arrived = [frames[0]] + [
        lax.ppermute(frames[k], "seq", [(z, z ^ k) for z in range(seq_count)])
        for k in range(1, seq_count)
    ]
    out = call(
        functools.partial(final_kernel, seq_count, group),
        [((channels // 2, rows), F32)],
        [weight, noise[0, 0].T] + arrived,
    )[0]
    return out.T[None, None]


def fast_fits(sizes, queries, residual, w_out, w_head):
    seq_count = sizes["seq"]
    step_count, rows, width_local = queries.shape[1:]
    channels = w_head.shape[1]
    if seq_count < 2 or sizes["guide"] != 2 or sizes["shard"] != 2 or seq_count & (seq_count - 1) or step_count != 1 or rows != LANES:
        return False
    if width_local % (seq_count // 2 * HEAD_DIM) or residual.shape[3] % (4 * LANES):
        return False
    if w_out.shape[1] != residual.shape[3] or channels % (2 * SUBLANES):
        return False
    group = rows // seq_count
    if rows % seq_count or LANES % group:
        return False
    fold = LANES // group
    return channels // 2 % (fold * SUBLANES) == 0


def solution(mesh):
    sizes = dict(mesh.shape)

    def on_device(queries, key_vecs, value_vecs, residual, w_out, attn_gate, norm_shift, norm_scale, w_head, *rest):
        fits = fast_fits(sizes, queries, residual, w_out, w_head)
        plan = fast_plan if fits else general_plan
        return plan(queries, key_vecs, value_vecs, residual, w_out, attn_gate, norm_shift, norm_scale, w_head, *rest)

    return jax.shard_map(
        on_device,
        mesh=mesh,
        in_specs=(
            P("guide", "group", "seq", "shard"),
            P("guide", "group", "seq", "shard"),
            P("guide", "group", "seq", "shard"),
            P("guide", "group", "seq", "shard"),
            P("shard", "guide"),
            P("group", "shard"),
            P("group", "shard"),
            P("group", "shard"),
            P("shard", None),
            P("group", "seq", None, "guide"),
            P("group"),
            P("group", None),
        ),
        out_specs=P("group", "seq", None, "guide"),
        check_vma=False,
    )
```

```python
import functools

import jax
import jax.numpy as jnp
from jax import lax
from jax.experimental import pallas as pl
from jax.experimental.pallas import tpu as pltpu
from jax.sharding import PartitionSpec as P


HEAD_DIM = 128
LANES = 128
SUBLANES = 8
beta_low = 0.0001
beta_high = 0.02
guidance_scale = 3.0
norm_epsilon = 1e-06
LOG2E = 1.4426950408889634


F32 = jnp.float32
BF16 = jnp.bfloat16
VMEM_SPEC = pl.BlockSpec(memory_space=pltpu.VMEM)
SMEM_SPEC = pl.BlockSpec(memory_space=pltpu.SMEM)
HBM_SPEC = pl.BlockSpec(memory_space=pltpu.HBM)


def plan_weight(timesteps):
    steps_float = timesteps.astype(jnp.float32)
    exponent = (steps_float + 1.0) * beta_low + (beta_high - beta_low) * steps_float * (
        steps_float + 1.0
    ) / (2.0 * 999.0)
    return 1.0 - jnp.exp(-exponent)


def attend_all(query_split, keys_all, values_all):
    heads_local = query_split.shape[2]
    keys_split = keys_all.reshape(keys_all.shape[0], keys_all.shape[1], heads_local, HEAD_DIM)
    values_split = values_all.reshape(values_all.shape[0], values_all.shape[1], heads_local, HEAD_DIM)
    scores = jnp.einsum(
        "tqhd,tkhd->tqhk", query_split, keys_split, preferred_element_type=F32
    ) * HEAD_DIM ** (-0.5)
    expo = jnp.exp(scores - jnp.max(scores, axis=-1, keepdims=True))
    total = jnp.sum(expo, axis=-1)
    mixed = jnp.einsum("tqhk,tkhd->tqhd", expo.astype(BF16), values_split, preferred_element_type=F32)
    return (mixed / total[..., None]).astype(BF16)


def general_plan(
    queries, key_vecs, value_vecs, residual, w_out, attn_gate, norm_shift, norm_scale, w_head, noise,
    timesteps, frame_owner,
):
    query_local = queries[0]
    step_count, token_count, width_local = query_local.shape
    heads_local = width_local // HEAD_DIM
    attended = attend_all(
        query_local.reshape(step_count, token_count, heads_local, HEAD_DIM),
        lax.all_gather(key_vecs[0], "seq", axis=1, tiled=True),
        lax.all_gather(value_vecs[0], "seq", axis=1, tiled=True),
    )
    row_count = step_count * token_count
    both_rows = jnp.dot(
        lax.all_gather(attended.reshape(row_count, width_local), "guide", axis=0, tiled=True),
        w_out,
        preferred_element_type=F32,
    )
    half_width = w_out.shape[1]
    swapped = lax.all_to_all(
        both_rows.reshape(2, row_count, half_width), "guide", split_axis=0, concat_axis=2, tiled=True
    )
    projected = swapped.reshape(row_count, 2 * half_width)
    attn_out = lax.psum_scatter(projected, "shard", scatter_dimension=1, tiled=True)
    width_shard = attn_out.shape[1]
    width_model = width_shard * lax.axis_size("shard")
    hidden = residual[0].astype(F32) + attn_gate[:, None, :] * attn_out.reshape(
        step_count, token_count, width_shard
    )
    sum_first, sum_second = lax.psum((jnp.sum(hidden, axis=-1), jnp.sum(hidden * hidden, axis=-1)), "shard")
    mean_row = sum_first / width_model
    var_row = sum_second / width_model - mean_row * mean_row
    inv_std = lax.rsqrt(var_row + norm_epsilon)
    modulated = (hidden - mean_row[..., None]) * inv_std[..., None] * (
        1.0 + norm_scale[:, None, :]
    ) + norm_shift[:, None, :]
    partial_head = jnp.einsum(
        "tqd,dc->tqc", modulated, w_head.astype(F32), precision=lax.Precision.HIGHEST
    )
    predicted = lax.psum(partial_head, "shard")
    seq_count = lax.axis_size("seq")
    frame_group = token_count // seq_count
    frames_view = predicted.reshape(step_count, seq_count, frame_group, predicted.shape[-1])
    owner_table = (
        frame_owner[:, :, None] == jnp.arange(seq_count, dtype=jnp.int32)[None, None, :]
    ).astype(F32)
    by_owner = jnp.einsum("tfo,tfgc->togc", owner_table, frames_view, precision=lax.Precision.HIGHEST)
    arrived = lax.all_to_all(
        lax.all_to_all(by_owner[None], "seq", split_axis=2, concat_axis=3, tiled=True),
        "guide",
        split_axis=4,
        concat_axis=0,
        tiled=True,
    )
    guided = arrived[1] + guidance_scale * (arrived[0] - arrived[1])
    return plan_weight(timesteps)[:, None, None, None] * (guided - noise)


def pack_kernel(parts, half, count, *refs):
    source_refs, out_refs, sems = refs[:count], refs[count:-1], refs[-1]
    z = lax.axis_index("seq")
    copies = []
    for j in range(parts):
        cols = pl.ds(pl.multiple_of(lax.rem(z + j, parts) * half, LANES), half)
        for i in range(count):
            copies.append(
                pltpu.make_async_copy(source_refs[i].at[:, cols], out_refs[j].at[i], sems.at[j * count + i])
            )
    for copy in copies:
        copy.start()
    for copy in copies:
        copy.wait()


def attend_kernel(blocks, q_ref, *refs):
    kv_refs, out_ref, score_scr, total_scr = refs[:blocks], refs[blocks], refs[blocks + 1], refs[blocks + 2]
    heads = q_ref.shape[2] // HEAD_DIM
    rows = kv_refs[0].shape[1]
    for i in range(heads):
        cols = slice(i * HEAD_DIM, (i + 1) * HEAD_DIM)
        q = q_ref[0, :, cols]
        for b in range(blocks):
            scores = lax.dot_general(
                q, kv_refs[b][0, :, cols], (((1,), (1,)), ((), ())), preferred_element_type=F32
            )
            score_scr[i, :, b * rows : (b + 1) * rows] = scores * (HEAD_DIM ** (-0.5) * LOG2E)
    for i in range(heads):
        scores = score_scr[i]
        expo = jnp.exp2(scores - jnp.max(scores, axis=1, keepdims=True))
        score_scr[i] = expo
        total_scr[i] = jnp.broadcast_to(jnp.sum(expo, axis=1, keepdims=True), total_scr.shape[1:])
    for i in range(heads):
        cols = slice(i * HEAD_DIM, (i + 1) * HEAD_DIM)
        values = jnp.concatenate([r[1, :, cols] for r in kv_refs], axis=0)
        mixed = jnp.dot(score_scr[i].astype(BF16), values, preferred_element_type=F32)
        out_ref[:, cols] = (mixed / total_scr[i]).astype(BF16)


def project(parts, half, o_refs, w_ref, cols):
    z = lax.axis_index("seq")
    total = None
    for j in range(parts):
        start = pl.multiple_of(lax.rem(z + j, parts) * half, LANES)
        term = jnp.dot(o_refs[j][...], w_ref[pl.ds(start, half), cols], preferred_element_type=F32)
        total = term if total is None else total + term
    return total


def send_kernel(parts, half, chunk, first, *refs):
    o_refs = refs[:parts]
    near_ref, far_ref, out_ref = refs[parts:]
    guide = lax.axis_index("guide")
    for value, w_ref in ((1, near_ref), (0, far_ref)):

        @pl.when(guide == value)
        def _():
            for t in range(out_ref.shape[1] // chunk):
                cols = slice(first + t * chunk, first + (t + 1) * chunk)
                out_ref[:, t * chunk : (t + 1) * chunk] = project(parts, half, o_refs, w_ref, cols).astype(BF16)


def keep_kernel(parts, half, chunk, *refs):
    o_refs = refs[:parts]
    near_ref, far_ref, res_ref, gate_ref, out_ref = refs[parts:]
    guide = lax.axis_index("guide")
    for value, w_ref in ((0, near_ref), (1, far_ref)):

        @pl.when(guide == value)
        def _():
            for t in range(out_ref.shape[1] // chunk):
                cols = slice(t * chunk, (t + 1) * chunk)
                out_ref[:, cols] = res_ref[:, cols].astype(F32) + gate_ref[:, cols] * project(
                    parts, half, o_refs, w_ref, cols
                )


def split_dot(head_t, rows):
    dims = (((1,), (1,)), ((), ()))
    high = rows.astype(BF16)
    low = (rows - high.astype(F32)).astype(BF16)
    return lax.dot_general(head_t, high, dims, preferred_element_type=F32) + lax.dot_general(
        head_t, low, dims, preferred_element_type=F32
    )


def early_kernel(seq_count, scale_ref, shift_ref, head_ref, owner_ref, steps_ref, out_ref, chosen_ref, weight_ref):
    z = lax.axis_index("seq")
    for k in range(seq_count):
        for f in range(seq_count):
            here = jnp.where(owner_ref[0, f] == z ^ k, 1.0, 0.0)
            chosen_ref[k * seq_count + f : k * seq_count + f + 1, :] = jnp.full((1, LANES), here, F32)
    weight_ref[...] = plan_weight(jnp.full((SUBLANES, LANES), steps_ref[0], jnp.int32))
    width = scale_ref.shape[1]
    which = lax.broadcasted_iota(jnp.int32, (LANES, width), 0)
    rows = jnp.where(which == 0, 1.0 + scale_ref[...], shift_ref[...])
    high = rows.astype(BF16)
    rest = rows - high.astype(F32)
    mid = rest.astype(BF16)
    low = (rest - mid.astype(F32)).astype(BF16)
    dims = (((1,), (1,)), ((), ()))
    total = None
    for part in (high, mid, low):
        term = lax.dot_general(head_ref[...], part, dims, preferred_element_type=F32)
        total = term if total is None else total + term
    out_ref[...] = total


def head_kernel(first, last, chunk, start, *refs):
    hid_ref, got_ref, gate_ref, scale_ref, head_ref = refs[:5]
    if first:
        out_refs = refs[5:]
    else:
        prev_refs, out_refs = refs[5:8], refs[8:]
    channels = head_ref.shape[0]
    rows = hid_ref.shape[0]
    acc_one = jnp.zeros((rows, LANES), F32) if first else prev_refs[1][...]
    acc_two = jnp.zeros((rows, LANES), F32) if first else prev_refs[2][...]
    acc_head = jnp.zeros((channels, rows), F32) if first else prev_refs[0][...]
    for t in range(got_ref.shape[1] // chunk):
        cols = slice(start + t * chunk, start + (t + 1) * chunk)
        arrived = got_ref[:, t * chunk : (t + 1) * chunk].astype(F32)
        hidden = hid_ref[:, cols] + gate_ref[:, cols] * arrived
        for s in range(chunk // LANES):
            piece = hidden[:, s * LANES : (s + 1) * LANES]
            acc_one = acc_one + piece
            acc_two = acc_two + piece * piece
        acc_head = acc_head + split_dot(head_ref[:, cols], hidden * (1.0 + scale_ref[:, cols]))
    if last:
        out_ref = out_refs[0]
        out_ref[0:channels, :] = acc_head
        sum_one = jnp.sum(acc_one.T, axis=0, keepdims=True)
        sum_two = jnp.sum(acc_two.T, axis=0, keepdims=True)
        row = lax.broadcasted_iota(jnp.int32, (SUBLANES, rows), 0)
        out_ref[channels : channels + SUBLANES, :] = jnp.where(row == 0, sum_one, sum_two)
    else:
        out_refs[0][...] = acc_head
        out_refs[1][...] = acc_one
        out_refs[2][...] = acc_two


def norm_kernel(width_model, own_ref, got_ref, rows_own_ref, rows_got_ref, keep_ref, send_ref, eps_scr):
    channels = rows_own_ref.shape[0]
    half_channels = channels // 2
    guide = lax.axis_index("guide")
    head = own_ref[0:channels, :] + got_ref[0:channels, :]
    stats = own_ref[channels : channels + SUBLANES, :] + got_ref[channels : channels + SUBLANES, :]
    mean = stats[0:1] / width_model
    var = stats[1:2] / width_model - mean * mean
    inv_std = lax.rsqrt(var + norm_epsilon)
    scaled = rows_own_ref[:, 0:1] + rows_got_ref[:, 0:1]
    shifted = rows_own_ref[:, 1:2] + rows_got_ref[:, 1:2]
    eps_scr[...] = (head - mean * scaled) * inv_std + shifted
    keep_ref[...] = eps_scr[pl.ds(pl.multiple_of(guide * half_channels, SUBLANES), half_channels), :]
    send_ref[...] = eps_scr[pl.ds(pl.multiple_of((1 - guide) * half_channels, SUBLANES), half_channels), :]


def frame_kernel(seq_count, group, chosen_ref, keep_ref, got_ref, *out_refs):
    first = lax.axis_index("guide") == 0
    mine, other = keep_ref[...], got_ref[...]
    eps_cond = jnp.where(first, mine, other)
    eps_free = jnp.where(first, other, mine)
    guided = eps_free + guidance_scale * (eps_cond - eps_free)
    fold = LANES // group
    rows = guided.shape[0] // fold
    lane = lax.broadcasted_iota(jnp.int32, (rows, LANES), 1) // group
    packed = []
    for f in range(seq_count):
        block = jnp.zeros((rows, LANES), F32)
        for j in range(fold):
            piece = guided[j * rows : (j + 1) * rows]
            shift = (j - f) * group % LANES
            block = jnp.where(lane == j, pltpu.roll(piece, shift, axis=1) if shift else piece, block)
        packed.append(block)
    for k in range(seq_count):
        block = packed[0]
        for f in range(1, seq_count):
            block = jnp.where(chosen_ref[k * seq_count + f : k * seq_count + f + 1, :] > 0.5, packed[f], block)
        out_refs[k][...] = block


def final_kernel(seq_count, group, weight_ref, noise_ref, *refs):
    piece_refs, out_ref = refs[:seq_count], refs[seq_count]
    z = lax.axis_index("seq")
    fold = LANES // group
    rows = piece_refs[0].shape[0]
    lane = lax.broadcasted_iota(jnp.int32, (rows, LANES), 1) // group
    for j in range(fold):
        block = jnp.zeros((rows, LANES), F32)
        for k in range(seq_count):
            source = z ^ k
            shift = lax.rem((source - j) * group + LANES, LANES)
            block = jnp.where(lane == source, pltpu.roll(piece_refs[k][...], shift, axis=1), block)
        part = slice(j * rows, (j + 1) * rows)
        out_ref[part, :] = weight_ref[0:1, :] * (block - noise_ref[part, :])


def call(kernel, outs, args, specs=None, scratch=(), flops=0, moved=0, grant=16):
    shapes = [jax.ShapeDtypeStruct(s, d) for s, d in outs]
    return pl.pallas_call(
        kernel,
        out_shape=shapes,
        in_specs=specs or [VMEM_SPEC] * len(args),
        out_specs=[VMEM_SPEC] * len(outs),
        scratch_shapes=list(scratch),
        compiler_params=pltpu.CompilerParams(vmem_limit_bytes=grant << 20),
        cost_estimate=pl.CostEstimate(flops=flops, bytes_accessed=moved, transcendentals=0),
    )(*args)


def fast_plan(
    queries, key_vecs, value_vecs, residual, w_out, attn_gate, norm_shift, norm_scale, w_head, noise,
    timesteps, frame_owner,
):
    seq_count = lax.axis_size("seq")
    parts = seq_count // 2
    rows, width_local = queries.shape[2:]
    half = width_local // parts
    width_shard = residual.shape[3]
    channels = w_head.shape[1]
    group = rows // seq_count
    width_model = float(width_shard * lax.axis_size("shard"))
    both = [(0, 1), (1, 0)]
    axes = ("seq", "guide")

    crossed = [(x * 2 + c, x * 2 + (c + x) % 2) for x in range(2) for c in range(2)]
    straight = [(x * 2 + c, x * 2 + (c + x + 1) % 2) for x in range(2) for c in range(2)]

    def pack(*arrays):
        return call(
            functools.partial(pack_kernel, parts, half, len(arrays)),
            [((len(arrays), rows, half), BF16)] * parts,
            [pltpu.with_memory_space_constraint(array[0, 0], pltpu.HBM) for array in arrays],
            [HBM_SPEC] * len(arrays),
            [pltpu.SemaphoreType.DMA((parts * len(arrays),))],
            moved=4 * len(arrays) * rows * width_local,
        )

    kv_sent = pack(key_vecs, value_vecs)
    there = [
        [
            (z * 2 + c, (parts * c + (z + j) % parts) * 2 + z // parts)
            for z in range(seq_count)
            for c in range(2)
        ]
        for j in range(parts)
    ]
    back = [[(b, a) for a, b in pairs] for pairs in there]
    kv_own = [lax.ppermute(kv_sent[j], axes, there[j]) for j in range(parts)]
    q_sent = pack(queries)
    q_own = [lax.ppermute(q_sent[j], axes, there[j]) for j in range(parts)]
    near_w = lax.ppermute(w_out, ("shard", "guide"), crossed)
    far_w = lax.ppermute(w_out, ("shard", "guide"), straight)
    kv_other = [lax.ppermute(block, "guide", both) for block in kv_own]

    head_t = w_head.T
    rows_own, chosen, weight = call(
        functools.partial(early_kernel, seq_count),
        [((channels, LANES), F32), ((seq_count * seq_count, LANES), F32), ((SUBLANES, LANES), F32)],
        [norm_scale, norm_shift, head_t, frame_owner, timesteps],
        [VMEM_SPEC] * 3 + [SMEM_SPEC] * 2,
        moved=4 * width_shard * LANES,
    )
    rows_got = lax.ppermute(rows_own, "shard", both)
    q_own[0], rows_own = lax.optimization_barrier((q_own[0], rows_own))

    mixed = []
    for j in range(parts):
        block = call(
            functools.partial(attend_kernel, 2 * parts),
            [((rows, half), BF16)],
            [q_own[j]] + kv_own + kv_other,
            scratch=[
                pltpu.VMEM((half // HEAD_DIM, rows, 2 * parts * rows), F32),
                pltpu.VMEM((half // HEAD_DIM, rows, HEAD_DIM), F32),
            ],
            flops=8 * rows * rows * parts * half,
            moved=2 * rows * half * parts * 5,
        )[0]
        mixed.append(lax.ppermute(block, axes, back[j]))

    chunk = 128
    quarter = width_shard // 4
    pieces = [(0, quarter), (quarter, 2 * quarter), (3 * quarter, quarter)]
    got = []
    for start, width in pieces:
        partial = call(
            functools.partial(send_kernel, parts, half, chunk, start),
            [((rows, width), BF16)],
            mixed + [near_w, far_w],
            flops=2 * rows * width_local * width,
            moved=2 * width_local * width,
        )[0]
        got.append(lax.ppermute(partial, "shard", both))
    hidden = call(
        functools.partial(keep_kernel, parts, half, chunk),
        [((rows, width_shard), F32)],
        mixed + [near_w, far_w, residual[0, 0], attn_gate],
        flops=2 * rows * width_local * width_shard,
        moved=2 * width_local * width_shard,
    )[0]
    state = []
    for i, (start, width) in enumerate(pieces):
        first, last = i == 0, i == len(pieces) - 1
        state = call(
            functools.partial(head_kernel, first, last, chunk, start),
            [((channels + SUBLANES, rows), F32)]
            if last
            else [((channels, rows), F32), ((rows, LANES), F32), ((rows, LANES), F32)],
            [hidden, got[i], attn_gate, norm_scale, head_t] + list(state),
            flops=4 * rows * channels * width,
            moved=6 * rows * width,
        )
    sums = state[0]
    sums_got = lax.ppermute(sums, "shard", both)
    keep, send = call(
        functools.partial(norm_kernel, width_model),
        [((channels // 2, rows), F32)] * 2,
        [sums, sums_got, rows_own, rows_got],
        scratch=[pltpu.VMEM((channels, rows), F32)],
    )
    eps_got = lax.ppermute(send, "guide", both)
    fold = LANES // group
    frames = call(
        functools.partial(frame_kernel, seq_count, group),
        [((channels // 2 // fold, LANES), F32)] * seq_count,
        [chosen, keep, eps_got],
    )
    arrived = [frames[0]] + [
        lax.ppermute(frames[k], "seq", [(z, z ^ k) for z in range(seq_count)])
        for k in range(1, seq_count)
    ]
    out = call(
        functools.partial(final_kernel, seq_count, group),
        [((channels // 2, rows), F32)],
        [weight, noise[0, 0].T] + arrived,
    )[0]
    return out.T[None, None]


def fast_fits(sizes, queries, residual, w_out, w_head):
    seq_count = sizes["seq"]
    step_count, rows, width_local = queries.shape[1:]
    channels = w_head.shape[1]
    if seq_count < 2 or sizes["guide"] != 2 or sizes["shard"] != 2 or seq_count & (seq_count - 1) or step_count != 1 or rows != LANES:
        return False
    if width_local % (seq_count // 2 * HEAD_DIM) or residual.shape[3] % (4 * LANES):
        return False
    if w_out.shape[1] != residual.shape[3] or channels % (2 * SUBLANES):
        return False
    group = rows // seq_count
    if rows % seq_count or LANES % group:
        return False
    fold = LANES // group
    return channels // 2 % (fold * SUBLANES) == 0


def solution(mesh):
    sizes = dict(mesh.shape)

    def on_device(queries, key_vecs, value_vecs, residual, w_out, attn_gate, norm_shift, norm_scale, w_head, *rest):
        fits = fast_fits(sizes, queries, residual, w_out, w_head)
        plan = fast_plan if fits else general_plan
        return plan(queries, key_vecs, value_vecs, residual, w_out, attn_gate, norm_shift, norm_scale, w_head, *rest)

    return jax.shard_map(
        on_device,
        mesh=mesh,
        in_specs=(
            P("guide", "group", "seq", "shard"),
            P("guide", "group", "seq", "shard"),
            P("guide", "group", "seq", "shard"),
            P("guide", "group", "seq", "shard"),
            P("shard", "guide"),
            P("group", "shard"),
            P("group", "shard"),
            P("group", "shard"),
            P("shard", None),
            P("group", "seq", None, "guide"),
            P("group"),
            P("group", None),
        ),
        out_specs=P("group", "seq", None, "guide"),
        check_vma=False,
    )
```

```python
import functools

import jax
import jax.numpy as jnp
from jax import lax
from jax.experimental import pallas as pl
from jax.experimental.pallas import tpu as pltpu
from jax.sharding import PartitionSpec as P


HEAD_DIM = 128
LANES = 128
SUBLANES = 8
beta_low = 0.0001
beta_high = 0.02
guidance_scale = 3.0
norm_epsilon = 1e-06
LOG2E = 1.4426950408889634


F32 = jnp.float32
BF16 = jnp.bfloat16
VMEM_SPEC = pl.BlockSpec(memory_space=pltpu.VMEM)
SMEM_SPEC = pl.BlockSpec(memory_space=pltpu.SMEM)
HBM_SPEC = pl.BlockSpec(memory_space=pltpu.HBM)


def plan_weight(timesteps):
    steps_float = timesteps.astype(jnp.float32)
    exponent = (steps_float + 1.0) * beta_low + (beta_high - beta_low) * steps_float * (
        steps_float + 1.0
    ) / (2.0 * 999.0)
    return 1.0 - jnp.exp(-exponent)


def attend_all(query_split, keys_all, values_all):
    heads_local = query_split.shape[2]
    keys_split = keys_all.reshape(keys_all.shape[0], keys_all.shape[1], heads_local, HEAD_DIM)
    values_split = values_all.reshape(values_all.shape[0], values_all.shape[1], heads_local, HEAD_DIM)
    scores = jnp.einsum(
        "tqhd,tkhd->tqhk", query_split, keys_split, preferred_element_type=F32
    ) * HEAD_DIM ** (-0.5)
    expo = jnp.exp(scores - jnp.max(scores, axis=-1, keepdims=True))
    total = jnp.sum(expo, axis=-1)
    mixed = jnp.einsum("tqhk,tkhd->tqhd", expo.astype(BF16), values_split, preferred_element_type=F32)
    return (mixed / total[..., None]).astype(BF16)


def general_plan(
    queries, key_vecs, value_vecs, residual, w_out, attn_gate, norm_shift, norm_scale, w_head, noise,
    timesteps, frame_owner,
):
    query_local = queries[0]
    step_count, token_count, width_local = query_local.shape
    heads_local = width_local // HEAD_DIM
    attended = attend_all(
        query_local.reshape(step_count, token_count, heads_local, HEAD_DIM),
        lax.all_gather(key_vecs[0], "seq", axis=1, tiled=True),
        lax.all_gather(value_vecs[0], "seq", axis=1, tiled=True),
    )
    row_count = step_count * token_count
    both_rows = jnp.dot(
        lax.all_gather(attended.reshape(row_count, width_local), "guide", axis=0, tiled=True),
        w_out,
        preferred_element_type=F32,
    )
    half_width = w_out.shape[1]
    swapped = lax.all_to_all(
        both_rows.reshape(2, row_count, half_width), "guide", split_axis=0, concat_axis=2, tiled=True
    )
    projected = swapped.reshape(row_count, 2 * half_width)
    attn_out = lax.psum_scatter(projected, "shard", scatter_dimension=1, tiled=True)
    width_shard = attn_out.shape[1]
    width_model = width_shard * lax.axis_size("shard")
    hidden = residual[0].astype(F32) + attn_gate[:, None, :] * attn_out.reshape(
        step_count, token_count, width_shard
    )
    sum_first, sum_second = lax.psum((jnp.sum(hidden, axis=-1), jnp.sum(hidden * hidden, axis=-1)), "shard")
    mean_row = sum_first / width_model
    var_row = sum_second / width_model - mean_row * mean_row
    inv_std = lax.rsqrt(var_row + norm_epsilon)
    modulated = (hidden - mean_row[..., None]) * inv_std[..., None] * (
        1.0 + norm_scale[:, None, :]
    ) + norm_shift[:, None, :]
    partial_head = jnp.einsum(
        "tqd,dc->tqc", modulated, w_head.astype(F32), precision=lax.Precision.HIGHEST
    )
    predicted = lax.psum(partial_head, "shard")
    seq_count = lax.axis_size("seq")
    frame_group = token_count // seq_count
    frames_view = predicted.reshape(step_count, seq_count, frame_group, predicted.shape[-1])
    owner_table = (
        frame_owner[:, :, None] == jnp.arange(seq_count, dtype=jnp.int32)[None, None, :]
    ).astype(F32)
    by_owner = jnp.einsum("tfo,tfgc->togc", owner_table, frames_view, precision=lax.Precision.HIGHEST)
    arrived = lax.all_to_all(
        lax.all_to_all(by_owner[None], "seq", split_axis=2, concat_axis=3, tiled=True),
        "guide",
        split_axis=4,
        concat_axis=0,
        tiled=True,
    )
    guided = arrived[1] + guidance_scale * (arrived[0] - arrived[1])
    return plan_weight(timesteps)[:, None, None, None] * (guided - noise)


def pack_kernel(parts, half, count, *refs):
    source_refs, out_refs, sems = refs[:count], refs[count:-1], refs[-1]
    z = lax.axis_index("seq")
    copies = []
    for j in range(parts):
        cols = pl.ds(pl.multiple_of(lax.rem(z + j, parts) * half, LANES), half)
        for i in range(count):
            copies.append(
                pltpu.make_async_copy(source_refs[i].at[:, cols], out_refs[j].at[i], sems.at[j * count + i])
            )
    for copy in copies:
        copy.start()
    for copy in copies:
        copy.wait()


def attend_kernel(parts, *refs):
    q_refs = refs[:parts]
    kv_refs = refs[parts : 3 * parts]
    o_refs = refs[3 * parts : 4 * parts]
    score_scr, total_scr = refs[4 * parts :]
    heads = q_refs[0].shape[2] // HEAD_DIM
    rows = q_refs[0].shape[1]
    for i in range(heads):
        cols = slice(i * HEAD_DIM, (i + 1) * HEAD_DIM)
        q = jnp.concatenate([r[0, :, cols] for r in q_refs], axis=0)
        for b, kv_ref in enumerate(kv_refs):
            scores = lax.dot_general(q, kv_ref[0, :, cols], (((1,), (1,)), ((), ())), preferred_element_type=F32)
            score_scr[i, :, b * rows : (b + 1) * rows] = scores * (HEAD_DIM ** (-0.5) * LOG2E)
    for i in range(heads):
        scores = score_scr[i]
        expo = jnp.exp2(scores - jnp.max(scores, axis=1, keepdims=True))
        score_scr[i] = expo
        total_scr[i] = jnp.broadcast_to(jnp.sum(expo, axis=1, keepdims=True), total_scr.shape[1:])
    for i in range(heads):
        cols = slice(i * HEAD_DIM, (i + 1) * HEAD_DIM)
        values = jnp.concatenate([r[1, :, cols] for r in kv_refs], axis=0)
        mixed = jnp.dot(score_scr[i].astype(BF16), values, preferred_element_type=F32) / total_scr[i]
        for j in range(parts):
            o_refs[j][:, cols] = mixed[j * rows : (j + 1) * rows].astype(BF16)


def project(parts, half, o_refs, w_ref, cols):
    z = lax.axis_index("seq")
    total = None
    for j in range(parts):
        start = pl.multiple_of(lax.rem(z + j, parts) * half, LANES)
        term = jnp.dot(o_refs[j][...], w_ref[pl.ds(start, half), cols], preferred_element_type=F32)
        total = term if total is None else total + term
    return total


def send_kernel(parts, half, chunk, first, *refs):
    o_refs = refs[:parts]
    near_ref, far_ref, out_ref = refs[parts:]
    guide = lax.axis_index("guide")
    for value, w_ref in ((1, near_ref), (0, far_ref)):

        @pl.when(guide == value)
        def _():
            for t in range(out_ref.shape[1] // chunk):
                cols = slice(first + t * chunk, first + (t + 1) * chunk)
                out_ref[:, t * chunk : (t + 1) * chunk] = project(parts, half, o_refs, w_ref, cols).astype(BF16)


def keep_kernel(parts, half, chunk, *refs):
    o_refs = refs[:parts]
    near_ref, far_ref, gate_ref, out_ref = refs[parts:]
    guide = lax.axis_index("guide")
    for value, w_ref in ((0, near_ref), (1, far_ref)):

        @pl.when(guide == value)
        def _():
            for t in range(out_ref.shape[1] // chunk):
                cols = slice(t * chunk, (t + 1) * chunk)
                out_ref[:, cols] = gate_ref[:, cols] * project(parts, half, o_refs, w_ref, cols)


def split_dot(head_t, rows):
    dims = (((1,), (1,)), ((), ()))
    high = rows.astype(BF16)
    low = (rows - high.astype(F32)).astype(BF16)
    return lax.dot_general(head_t, high, dims, preferred_element_type=F32) + lax.dot_general(
        head_t, low, dims, preferred_element_type=F32
    )


def early_kernel(seq_count, scale_ref, shift_ref, head_ref, owner_ref, steps_ref, out_ref, chosen_ref, weight_ref):
    z = lax.axis_index("seq")
    for k in range(seq_count):
        for f in range(seq_count):
            here = jnp.where(owner_ref[0, f] == z ^ k, 1.0, 0.0)
            chosen_ref[k * seq_count + f : k * seq_count + f + 1, :] = jnp.full((1, LANES), here, F32)
    weight_ref[...] = plan_weight(jnp.full((SUBLANES, LANES), steps_ref[0], jnp.int32))
    width = scale_ref.shape[1]
    which = lax.broadcasted_iota(jnp.int32, (LANES, width), 0)
    rows = jnp.where(which == 0, 1.0 + scale_ref[...], shift_ref[...])
    high = rows.astype(BF16)
    rest = rows - high.astype(F32)
    mid = rest.astype(BF16)
    low = (rest - mid.astype(F32)).astype(BF16)
    dims = (((1,), (1,)), ((), ()))
    total = None
    for part in (high, mid, low):
        term = lax.dot_general(head_ref[...], part, dims, preferred_element_type=F32)
        total = term if total is None else total + term
    out_ref[...] = total


def head_kernel(first, last, chunk, start, *refs):
    res_ref, hid_ref, got_ref, gate_ref, scale_ref, head_ref = refs[:6]
    if first:
        out_refs = refs[6:]
    else:
        prev_refs, out_refs = refs[6:9], refs[9:]
    channels = head_ref.shape[0]
    rows = hid_ref.shape[0]
    acc_one = jnp.zeros((rows, LANES), F32) if first else prev_refs[1][...]
    acc_two = jnp.zeros((rows, LANES), F32) if first else prev_refs[2][...]
    acc_head = jnp.zeros((channels, rows), F32) if first else prev_refs[0][...]
    for t in range(got_ref.shape[1] // chunk):
        cols = slice(start + t * chunk, start + (t + 1) * chunk)
        arrived = got_ref[:, t * chunk : (t + 1) * chunk].astype(F32)
        hidden = res_ref[:, cols].astype(F32) + hid_ref[:, cols] + gate_ref[:, cols] * arrived
        for s in range(chunk // LANES):
            piece = hidden[:, s * LANES : (s + 1) * LANES]
            acc_one = acc_one + piece
            acc_two = acc_two + piece * piece
        acc_head = acc_head + split_dot(head_ref[:, cols], hidden * (1.0 + scale_ref[:, cols]))
    if last:
        out_ref = out_refs[0]
        out_ref[0:channels, :] = acc_head
        sum_one = jnp.sum(acc_one.T, axis=0, keepdims=True)
        sum_two = jnp.sum(acc_two.T, axis=0, keepdims=True)
        row = lax.broadcasted_iota(jnp.int32, (SUBLANES, rows), 0)
        out_ref[channels : channels + SUBLANES, :] = jnp.where(row == 0, sum_one, sum_two)
    else:
        out_refs[0][...] = acc_head
        out_refs[1][...] = acc_one
        out_refs[2][...] = acc_two


def norm_kernel(width_model, own_ref, got_ref, rows_own_ref, rows_got_ref, keep_ref, send_ref, eps_scr):
    channels = rows_own_ref.shape[0]
    half_channels = channels // 2
    guide = lax.axis_index("guide")
    head = own_ref[0:channels, :] + got_ref[0:channels, :]
    stats = own_ref[channels : channels + SUBLANES, :] + got_ref[channels : channels + SUBLANES, :]
    mean = stats[0:1] / width_model
    var = stats[1:2] / width_model - mean * mean
    inv_std = lax.rsqrt(var + norm_epsilon)
    scaled = rows_own_ref[:, 0:1] + rows_got_ref[:, 0:1]
    shifted = rows_own_ref[:, 1:2] + rows_got_ref[:, 1:2]
    eps_scr[...] = (head - mean * scaled) * inv_std + shifted
    keep_ref[...] = eps_scr[pl.ds(pl.multiple_of(guide * half_channels, SUBLANES), half_channels), :]
    send_ref[...] = eps_scr[pl.ds(pl.multiple_of((1 - guide) * half_channels, SUBLANES), half_channels), :]


def frame_kernel(seq_count, group, chosen_ref, keep_ref, got_ref, *out_refs):
    first = lax.axis_index("guide") == 0
    mine, other = keep_ref[...], got_ref[...]
    fold = LANES // group
    rows = mine.shape[0] // fold
    lane = lax.broadcasted_iota(jnp.int32, (rows, LANES), 1) // group
    for sub, block in enumerate((jnp.where(first, mine, other), jnp.where(first, other, mine))):
        packed = []
        for f in range(seq_count):
            frame = jnp.zeros((rows, LANES), F32)
            for j in range(fold):
                piece = block[j * rows : (j + 1) * rows]
                shift = (j - f) * group % LANES
                frame = jnp.where(lane == j, pltpu.roll(piece, shift, axis=1) if shift else piece, frame)
            packed.append(frame)
        for k in range(seq_count):
            frame = packed[0]
            for f in range(1, seq_count):
                frame = jnp.where(chosen_ref[k * seq_count + f : k * seq_count + f + 1, :] > 0.5, packed[f], frame)
            out_refs[k][sub * rows : (sub + 1) * rows, :] = frame


def final_kernel(seq_count, group, weight_ref, noise_ref, *refs):
    piece_refs, out_ref = refs[:seq_count], refs[seq_count]
    z = lax.axis_index("seq")
    parts = seq_count // 2
    fold = LANES // group
    rows = piece_refs[0].shape[0] // 2
    lane = lax.broadcasted_iota(jnp.int32, (rows, LANES), 1) // group
    for j in range(fold):
        eps_cond = jnp.zeros((rows, LANES), F32)
        eps_free = jnp.zeros((rows, LANES), F32)
        for k in range(seq_count):
            source = z ^ k
            branch, position = source // parts, lax.rem(source, parts)
            for sub in range(2):
                block = parts * sub + position
                shift = lax.rem((block - j) * group + LANES, LANES)
                rolled = pltpu.roll(piece_refs[k][sub * rows : (sub + 1) * rows], shift, axis=1)
                eps_cond = jnp.where((lane == block) & (branch == 0), rolled, eps_cond)
                eps_free = jnp.where((lane == block) & (branch == 1), rolled, eps_free)
        part = slice(j * rows, (j + 1) * rows)
        guided = eps_free + guidance_scale * (eps_cond - eps_free)
        out_ref[part, :] = weight_ref[0:1, :] * (guided - noise_ref[part, :])


def call(kernel, outs, args, specs=None, scratch=(), flops=0, moved=0, grant=16):
    shapes = [jax.ShapeDtypeStruct(s, d) for s, d in outs]
    return pl.pallas_call(
        kernel,
        out_shape=shapes,
        in_specs=specs or [VMEM_SPEC] * len(args),
        out_specs=[VMEM_SPEC] * len(outs),
        scratch_shapes=list(scratch),
        compiler_params=pltpu.CompilerParams(vmem_limit_bytes=grant << 20),
        cost_estimate=pl.CostEstimate(flops=flops, bytes_accessed=moved, transcendentals=0),
    )(*args)


def fast_plan(
    queries, key_vecs, value_vecs, residual, w_out, attn_gate, norm_shift, norm_scale, w_head, noise,
    timesteps, frame_owner,
):
    seq_count = lax.axis_size("seq")
    parts = seq_count // 2
    rows, width_local = queries.shape[2:]
    half = width_local // parts
    width_shard = residual.shape[3]
    channels = w_head.shape[1]
    group = rows // seq_count
    width_model = float(width_shard * lax.axis_size("shard"))
    both = [(0, 1), (1, 0)]
    axes = ("seq", "guide")

    crossed = [(x * 2 + c, x * 2 + (c + x) % 2) for x in range(2) for c in range(2)]
    straight = [(x * 2 + c, x * 2 + (c + x + 1) % 2) for x in range(2) for c in range(2)]

    def pack(*arrays):
        return call(
            functools.partial(pack_kernel, parts, half, len(arrays)),
            [((len(arrays), rows, half), BF16)] * parts,
            [pltpu.with_memory_space_constraint(array[0, 0], pltpu.HBM) for array in arrays],
            [HBM_SPEC] * len(arrays),
            [pltpu.SemaphoreType.DMA((parts * len(arrays),))],
            moved=4 * len(arrays) * rows * width_local,
        )

    kv_sent = pack(key_vecs, value_vecs)
    there = [
        [
            (z * 2 + c, (parts * c + (z + j) % parts) * 2 + z // parts)
            for z in range(seq_count)
            for c in range(2)
        ]
        for j in range(parts)
    ]
    inside = [[(z, z // parts * parts + (z - j) % parts) for z in range(seq_count)] for j in range(parts)]
    kv_own = [lax.ppermute(kv_sent[j], axes, there[j]) for j in range(parts)]
    q_sent = pack(queries)
    q_own = [lax.ppermute(q_sent[j], axes, there[j]) for j in range(parts)]
    near_w = lax.ppermute(w_out, ("shard", "guide"), crossed)
    far_w = lax.ppermute(w_out, ("shard", "guide"), straight)
    kv_other = [lax.ppermute(block, "guide", both) for block in kv_own]
    res_here = lax.ppermute(residual[0, 0], axes, there[0])

    head_t = w_head.T
    rows_own, chosen, weight = call(
        functools.partial(early_kernel, seq_count),
        [((channels, LANES), F32), ((seq_count * seq_count, LANES), F32), ((SUBLANES, LANES), F32)],
        [norm_scale, norm_shift, head_t, frame_owner, timesteps],
        [VMEM_SPEC] * 3 + [SMEM_SPEC] * 2,
        moved=4 * width_shard * LANES,
    )
    rows_got = lax.ppermute(rows_own, "shard", both)
    *q_own, rows_own = lax.optimization_barrier((*q_own, rows_own))

    mixed = call(
        functools.partial(attend_kernel, parts),
        [((rows, half), BF16)] * parts,
        q_own + kv_own + kv_other,
        scratch=[
            pltpu.VMEM((half // HEAD_DIM, rows * parts, 2 * parts * rows), F32),
            pltpu.VMEM((half // HEAD_DIM, rows * parts, HEAD_DIM), F32),
        ],
        flops=8 * rows * parts * rows * parts * half,
        moved=2 * rows * half * parts * 6,
    )
    mixed = [mixed[0]] + [lax.ppermute(mixed[j], "seq", inside[j]) for j in range(1, parts)]

    chunk = 128
    pieces = 4
    width_piece = width_shard // pieces
    got = []
    for i in range(pieces):
        partial = call(
            functools.partial(send_kernel, parts, half, chunk, i * width_piece),
            [((rows, width_piece), BF16)],
            mixed + [near_w, far_w],
            flops=2 * rows * width_local * width_piece,
            moved=2 * width_local * width_piece,
        )[0]
        got.append(lax.ppermute(partial, "shard", both))
    hidden = call(
        functools.partial(keep_kernel, parts, half, chunk),
        [((rows, width_shard), F32)],
        mixed + [near_w, far_w, attn_gate],
        flops=2 * rows * width_local * width_shard,
        moved=2 * width_local * width_shard,
    )[0]
    state = []
    for i in range(pieces):
        first, last = i == 0, i == pieces - 1
        state = call(
            functools.partial(head_kernel, first, last, chunk, i * width_piece),
            [((channels + SUBLANES, rows), F32)]
            if last
            else [((channels, rows), F32), ((rows, LANES), F32), ((rows, LANES), F32)],
            [res_here, hidden, got[i], attn_gate, norm_scale, head_t] + list(state),
            flops=4 * rows * channels * width_piece,
            moved=6 * rows * width_piece,
        )
    sums = state[0]
    sums_got = lax.ppermute(sums, "shard", both)
    keep, send = call(
        functools.partial(norm_kernel, width_model),
        [((channels // 2, rows), F32)] * 2,
        [sums, sums_got, rows_own, rows_got],
        scratch=[pltpu.VMEM((channels, rows), F32)],
    )
    eps_got = lax.ppermute(send, "guide", both)
    fold = LANES // group
    frames = call(
        functools.partial(frame_kernel, seq_count, group),
        [((channels // fold, LANES), F32)] * seq_count,
        [chosen, keep, eps_got],
    )
    arrived = [frames[0]] + [
        lax.ppermute(frames[k], "seq", [(z, z ^ k) for z in range(seq_count)])
        for k in range(1, seq_count)
    ]
    out = call(
        functools.partial(final_kernel, seq_count, group),
        [((channels // 2, rows), F32)],
        [weight, noise[0, 0].T] + arrived,
    )[0]
    return out.T[None, None]


def fast_fits(sizes, queries, residual, w_out, w_head):
    seq_count = sizes["seq"]
    step_count, rows, width_local = queries.shape[1:]
    channels = w_head.shape[1]
    if seq_count < 2 or sizes["guide"] != 2 or sizes["shard"] != 2 or seq_count & (seq_count - 1) or step_count != 1 or rows != LANES:
        return False
    if width_local % (seq_count // 2 * HEAD_DIM) or residual.shape[3] % (4 * LANES):
        return False
    if w_out.shape[1] != residual.shape[3] or channels % (2 * SUBLANES):
        return False
    group = rows // seq_count
    if rows % seq_count or LANES % group:
        return False
    fold = LANES // group
    return channels // 2 % (fold * SUBLANES) == 0


def solution(mesh):
    sizes = dict(mesh.shape)

    def on_device(queries, key_vecs, value_vecs, residual, w_out, attn_gate, norm_shift, norm_scale, w_head, *rest):
        fits = fast_fits(sizes, queries, residual, w_out, w_head)
        plan = fast_plan if fits else general_plan
        return plan(queries, key_vecs, value_vecs, residual, w_out, attn_gate, norm_shift, norm_scale, w_head, *rest)

    return jax.shard_map(
        on_device,
        mesh=mesh,
        in_specs=(
            P("guide", "group", "seq", "shard"),
            P("guide", "group", "seq", "shard"),
            P("guide", "group", "seq", "shard"),
            P("guide", "group", "seq", "shard"),
            P("shard", "guide"),
            P("group", "shard"),
            P("group", "shard"),
            P("group", "shard"),
            P("shard", None),
            P("group", "seq", None, "guide"),
            P("group"),
            P("group", None),
        ),
        out_specs=P("group", "seq", None, "guide"),
        check_vma=False,
    )
```

```python
import functools

import jax
import jax.numpy as jnp
from jax import lax
from jax.experimental import pallas as pl
from jax.experimental.pallas import tpu as pltpu
from jax.sharding import PartitionSpec as P


HEAD_DIM = 128
LANES = 128
SUBLANES = 8
beta_low = 0.0001
beta_high = 0.02
guidance_scale = 3.0
norm_epsilon = 1e-06
LOG2E = 1.4426950408889634


F32 = jnp.float32
BF16 = jnp.bfloat16
VMEM_SPEC = pl.BlockSpec(memory_space=pltpu.VMEM)
SMEM_SPEC = pl.BlockSpec(memory_space=pltpu.SMEM)
HBM_SPEC = pl.BlockSpec(memory_space=pltpu.HBM)


def plan_weight(timesteps):
    steps_float = timesteps.astype(jnp.float32)
    exponent = (steps_float + 1.0) * beta_low + (beta_high - beta_low) * steps_float * (
        steps_float + 1.0
    ) / (2.0 * 999.0)
    return 1.0 - jnp.exp(-exponent)


def attend_all(query_split, keys_all, values_all):
    heads_local = query_split.shape[2]
    keys_split = keys_all.reshape(keys_all.shape[0], keys_all.shape[1], heads_local, HEAD_DIM)
    values_split = values_all.reshape(values_all.shape[0], values_all.shape[1], heads_local, HEAD_DIM)
    scores = jnp.einsum(
        "tqhd,tkhd->tqhk", query_split, keys_split, preferred_element_type=F32
    ) * HEAD_DIM ** (-0.5)
    expo = jnp.exp(scores - jnp.max(scores, axis=-1, keepdims=True))
    total = jnp.sum(expo, axis=-1)
    mixed = jnp.einsum("tqhk,tkhd->tqhd", expo.astype(BF16), values_split, preferred_element_type=F32)
    return (mixed / total[..., None]).astype(BF16)


def general_plan(
    queries, key_vecs, value_vecs, residual, w_out, attn_gate, norm_shift, norm_scale, w_head, noise,
    timesteps, frame_owner,
):
    query_local = queries[0]
    step_count, token_count, width_local = query_local.shape
    heads_local = width_local // HEAD_DIM
    attended = attend_all(
        query_local.reshape(step_count, token_count, heads_local, HEAD_DIM),
        lax.all_gather(key_vecs[0], "seq", axis=1, tiled=True),
        lax.all_gather(value_vecs[0], "seq", axis=1, tiled=True),
    )
    row_count = step_count * token_count
    both_rows = jnp.dot(
        lax.all_gather(attended.reshape(row_count, width_local), "guide", axis=0, tiled=True),
        w_out,
        preferred_element_type=F32,
    )
    half_width = w_out.shape[1]
    swapped = lax.all_to_all(
        both_rows.reshape(2, row_count, half_width), "guide", split_axis=0, concat_axis=2, tiled=True
    )
    projected = swapped.reshape(row_count, 2 * half_width)
    attn_out = lax.psum_scatter(projected, "shard", scatter_dimension=1, tiled=True)
    width_shard = attn_out.shape[1]
    width_model = width_shard * lax.axis_size("shard")
    hidden = residual[0].astype(F32) + attn_gate[:, None, :] * attn_out.reshape(
        step_count, token_count, width_shard
    )
    sum_first, sum_second = lax.psum((jnp.sum(hidden, axis=-1), jnp.sum(hidden * hidden, axis=-1)), "shard")
    mean_row = sum_first / width_model
    var_row = sum_second / width_model - mean_row * mean_row
    inv_std = lax.rsqrt(var_row + norm_epsilon)
    modulated = (hidden - mean_row[..., None]) * inv_std[..., None] * (
        1.0 + norm_scale[:, None, :]
    ) + norm_shift[:, None, :]
    partial_head = jnp.einsum(
        "tqd,dc->tqc", modulated, w_head.astype(F32), precision=lax.Precision.HIGHEST
    )
    predicted = lax.psum(partial_head, "shard")
    seq_count = lax.axis_size("seq")
    frame_group = token_count // seq_count
    frames_view = predicted.reshape(step_count, seq_count, frame_group, predicted.shape[-1])
    owner_table = (
        frame_owner[:, :, None] == jnp.arange(seq_count, dtype=jnp.int32)[None, None, :]
    ).astype(F32)
    by_owner = jnp.einsum("tfo,tfgc->togc", owner_table, frames_view, precision=lax.Precision.HIGHEST)
    arrived = lax.all_to_all(
        lax.all_to_all(by_owner[None], "seq", split_axis=2, concat_axis=3, tiled=True),
        "guide",
        split_axis=4,
        concat_axis=0,
        tiled=True,
    )
    guided = arrived[1] + guidance_scale * (arrived[0] - arrived[1])
    return plan_weight(timesteps)[:, None, None, None] * (guided - noise)


def pack_kernel(parts, half, count, *refs):
    source_refs, out_refs, sems = refs[:count], refs[count:-1], refs[-1]
    z = lax.axis_index("seq")
    copies = []
    for j in range(parts):
        cols = pl.ds(pl.multiple_of(lax.rem(z + j, parts) * half, LANES), half)
        for i in range(count):
            copies.append(
                pltpu.make_async_copy(source_refs[i].at[:, cols], out_refs[j].at[i], sems.at[j * count + i])
            )
    for copy in copies:
        copy.start()
    for copy in copies:
        copy.wait()


def attend_kernel(parts, *refs):
    q_refs = refs[:parts]
    kv_refs = refs[parts : 3 * parts]
    o_refs = refs[3 * parts : 4 * parts]
    score_scr, total_scr = refs[4 * parts :]
    heads = q_refs[0].shape[2] // HEAD_DIM
    rows = q_refs[0].shape[1]
    for i in range(heads):
        cols = slice(i * HEAD_DIM, (i + 1) * HEAD_DIM)
        q = jnp.concatenate([r[0, :, cols] for r in q_refs], axis=0)
        for b, kv_ref in enumerate(kv_refs):
            scores = lax.dot_general(q, kv_ref[0, :, cols], (((1,), (1,)), ((), ())), preferred_element_type=F32)
            score_scr[i, :, b * rows : (b + 1) * rows] = scores * (HEAD_DIM ** (-0.5) * LOG2E)
    for i in range(heads):
        scores = score_scr[i]
        expo = jnp.exp2(scores - jnp.max(scores, axis=1, keepdims=True))
        score_scr[i] = expo
        total_scr[i] = jnp.broadcast_to(jnp.sum(expo, axis=1, keepdims=True), total_scr.shape[1:])
    for i in range(heads):
        cols = slice(i * HEAD_DIM, (i + 1) * HEAD_DIM)
        values = jnp.concatenate([r[1, :, cols] for r in kv_refs], axis=0)
        mixed = jnp.dot(score_scr[i].astype(BF16), values, preferred_element_type=F32) / total_scr[i]
        for j in range(parts):
            o_refs[j][:, cols] = mixed[j * rows : (j + 1) * rows].astype(BF16)


def project(parts, half, o_refs, w_ref, cols):
    z = lax.axis_index("seq")
    total = None
    for j in range(parts):
        start = pl.multiple_of(lax.rem(z + j, parts) * half, LANES)
        term = jnp.dot(o_refs[j][...], w_ref[pl.ds(start, half), cols], preferred_element_type=F32)
        total = term if total is None else total + term
    return total


def send_kernel(parts, half, chunk, first, *refs):
    o_refs = refs[:parts]
    near_ref, far_ref, out_ref = refs[parts:]
    guide = lax.axis_index("guide")
    for value, w_ref in ((1, near_ref), (0, far_ref)):

        @pl.when(guide == value)
        def _():
            for t in range(out_ref.shape[1] // chunk):
                cols = slice(first + t * chunk, first + (t + 1) * chunk)
                out_ref[:, t * chunk : (t + 1) * chunk] = project(parts, half, o_refs, w_ref, cols).astype(BF16)


def keep_kernel(parts, half, chunk, *refs):
    o_refs = refs[:parts]
    near_ref, far_ref, gate_ref, out_ref = refs[parts:]
    guide = lax.axis_index("guide")
    for value, w_ref in ((0, near_ref), (1, far_ref)):

        @pl.when(guide == value)
        def _():
            for t in range(out_ref.shape[1] // chunk):
                cols = slice(t * chunk, (t + 1) * chunk)
                out_ref[:, cols] = gate_ref[:, cols] * project(parts, half, o_refs, w_ref, cols)


def split_dot(head_t, rows):
    dims = (((1,), (1,)), ((), ()))
    high = rows.astype(BF16)
    low = (rows - high.astype(F32)).astype(BF16)
    return lax.dot_general(head_t, high, dims, preferred_element_type=F32) + lax.dot_general(
        head_t, low, dims, preferred_element_type=F32
    )


def early_kernel(
    seq_count, scale_hbm, shift_hbm, head_hbm, owner_ref, steps_ref, out_ref, chosen_ref, weight_ref,
    scale_ref, shift_ref, head_ref, sems,
):
    copies = [
        pltpu.make_async_copy(source, target, sems.at[i])
        for i, (source, target) in enumerate(
            ((scale_hbm, scale_ref), (shift_hbm, shift_ref), (head_hbm, head_ref))
        )
    ]
    for copy in copies:
        copy.start()
    z = lax.axis_index("seq")
    for k in range(seq_count):
        for f in range(seq_count):
            here = jnp.where(owner_ref[0, f] == z ^ k, 1.0, 0.0)
            chosen_ref[k * seq_count + f : k * seq_count + f + 1, :] = jnp.full((1, LANES), here, F32)
    weight_ref[...] = plan_weight(jnp.full((SUBLANES, LANES), steps_ref[0], jnp.int32))
    for copy in copies:
        copy.wait()
    width = scale_ref.shape[1]
    which = lax.broadcasted_iota(jnp.int32, (LANES, width), 0)
    rows = jnp.where(which == 0, 1.0 + scale_ref[...], shift_ref[...])
    high = rows.astype(BF16)
    rest = rows - high.astype(F32)
    mid = rest.astype(BF16)
    low = (rest - mid.astype(F32)).astype(BF16)
    dims = (((1,), (1,)), ((), ()))
    total = None
    for part in (high, mid, low):
        term = lax.dot_general(head_ref[...], part, dims, preferred_element_type=F32)
        total = term if total is None else total + term
    out_ref[...] = total


def head_kernel(first, last, chunk, start, *refs):
    res_ref, hid_ref, got_ref, gate_ref, scale_ref, head_ref = refs[:6]
    if first:
        out_refs = refs[6:]
    else:
        prev_refs, out_refs = refs[6:9], refs[9:]
    channels = head_ref.shape[0]
    rows = hid_ref.shape[0]
    acc_one = jnp.zeros((rows, LANES), F32) if first else prev_refs[1][...]
    acc_two = jnp.zeros((rows, LANES), F32) if first else prev_refs[2][...]
    acc_head = jnp.zeros((channels, rows), F32) if first else prev_refs[0][...]
    for t in range(got_ref.shape[1] // chunk):
        cols = slice(start + t * chunk, start + (t + 1) * chunk)
        arrived = got_ref[:, t * chunk : (t + 1) * chunk].astype(F32)
        hidden = res_ref[:, cols].astype(F32) + hid_ref[:, cols] + gate_ref[:, cols] * arrived
        for s in range(chunk // LANES):
            piece = hidden[:, s * LANES : (s + 1) * LANES]
            acc_one = acc_one + piece
            acc_two = acc_two + piece * piece
        acc_head = acc_head + split_dot(head_ref[:, cols], hidden * (1.0 + scale_ref[:, cols]))
    if last:
        out_ref = out_refs[0]
        out_ref[0:channels, :] = acc_head
        sum_one = jnp.sum(acc_one.T, axis=0, keepdims=True)
        sum_two = jnp.sum(acc_two.T, axis=0, keepdims=True)
        row = lax.broadcasted_iota(jnp.int32, (SUBLANES, rows), 0)
        out_ref[channels : channels + SUBLANES, :] = jnp.where(row == 0, sum_one, sum_two)
    else:
        out_refs[0][...] = acc_head
        out_refs[1][...] = acc_one
        out_refs[2][...] = acc_two


def norm_kernel(width_model, own_ref, got_ref, rows_own_ref, rows_got_ref, keep_ref, send_ref, eps_scr):
    channels = rows_own_ref.shape[0]
    half_channels = channels // 2
    guide = lax.axis_index("guide")
    head = own_ref[0:channels, :] + got_ref[0:channels, :]
    stats = own_ref[channels : channels + SUBLANES, :] + got_ref[channels : channels + SUBLANES, :]
    mean = stats[0:1] / width_model
    var = stats[1:2] / width_model - mean * mean
    inv_std = lax.rsqrt(var + norm_epsilon)
    scaled = rows_own_ref[:, 0:1] + rows_got_ref[:, 0:1]
    shifted = rows_own_ref[:, 1:2] + rows_got_ref[:, 1:2]
    eps_scr[...] = (head - mean * scaled) * inv_std + shifted
    keep_ref[...] = eps_scr[pl.ds(pl.multiple_of(guide * half_channels, SUBLANES), half_channels), :]
    send_ref[...] = eps_scr[pl.ds(pl.multiple_of((1 - guide) * half_channels, SUBLANES), half_channels), :]


def frame_kernel(seq_count, group, chosen_ref, keep_ref, got_ref, *out_refs):
    first = lax.axis_index("guide") == 0
    mine, other = keep_ref[...], got_ref[...]
    fold = LANES // group
    rows = mine.shape[0] // fold
    lane = lax.broadcasted_iota(jnp.int32, (rows, LANES), 1) // group
    for sub, block in enumerate((jnp.where(first, mine, other), jnp.where(first, other, mine))):
        packed = []
        for f in range(seq_count):
            frame = jnp.zeros((rows, LANES), F32)
            for j in range(fold):
                piece = block[j * rows : (j + 1) * rows]
                shift = (j - f) * group % LANES
                frame = jnp.where(lane == j, pltpu.roll(piece, shift, axis=1) if shift else piece, frame)
            packed.append(frame)
        for k in range(seq_count):
            frame = packed[0]
            for f in range(1, seq_count):
                frame = jnp.where(chosen_ref[k * seq_count + f : k * seq_count + f + 1, :] > 0.5, packed[f], frame)
            out_refs[k][sub * rows : (sub + 1) * rows, :] = frame


def final_kernel(seq_count, group, weight_ref, noise_ref, *refs):
    piece_refs, out_ref = refs[:seq_count], refs[seq_count]
    z = lax.axis_index("seq")
    parts = seq_count // 2
    fold = LANES // group
    rows = piece_refs[0].shape[0] // 2
    lane = lax.broadcasted_iota(jnp.int32, (rows, LANES), 1) // group
    for j in range(fold):
        eps_cond = jnp.zeros((rows, LANES), F32)
        eps_free = jnp.zeros((rows, LANES), F32)
        for k in range(seq_count):
            source = z ^ k
            branch, position = source // parts, lax.rem(source, parts)
            for sub in range(2):
                block = parts * sub + position
                shift = lax.rem((block - j) * group + LANES, LANES)
                rolled = pltpu.roll(piece_refs[k][sub * rows : (sub + 1) * rows], shift, axis=1)
                eps_cond = jnp.where((lane == block) & (branch == 0), rolled, eps_cond)
                eps_free = jnp.where((lane == block) & (branch == 1), rolled, eps_free)
        part = slice(j * rows, (j + 1) * rows)
        guided = eps_free + guidance_scale * (eps_cond - eps_free)
        out_ref[part, :] = weight_ref[0:1, :] * (guided - noise_ref[part, :])


def call(kernel, outs, args, specs=None, scratch=(), flops=0, moved=0, grant=16):
    shapes = [jax.ShapeDtypeStruct(s, d) for s, d in outs]
    return pl.pallas_call(
        kernel,
        out_shape=shapes,
        in_specs=specs or [VMEM_SPEC] * len(args),
        out_specs=[VMEM_SPEC] * len(outs),
        scratch_shapes=list(scratch),
        compiler_params=pltpu.CompilerParams(vmem_limit_bytes=grant << 20),
        cost_estimate=pl.CostEstimate(flops=flops, bytes_accessed=moved, transcendentals=0),
    )(*args)


def in_hbm(array):
    return pltpu.with_memory_space_constraint(array, pltpu.HBM)


def fast_plan(
    queries, key_vecs, value_vecs, residual, w_out, attn_gate, norm_shift, norm_scale, w_head, noise,
    timesteps, frame_owner,
):
    seq_count = lax.axis_size("seq")
    parts = seq_count // 2
    rows, width_local = queries.shape[2:]
    half = width_local // parts
    width_shard = residual.shape[3]
    channels = w_head.shape[1]
    group = rows // seq_count
    width_model = float(width_shard * lax.axis_size("shard"))
    both = [(0, 1), (1, 0)]
    axes = ("seq", "guide")

    crossed = [(x * 2 + c, x * 2 + (c + x) % 2) for x in range(2) for c in range(2)]
    straight = [(x * 2 + c, x * 2 + (c + x + 1) % 2) for x in range(2) for c in range(2)]

    def pack(*arrays):
        return call(
            functools.partial(pack_kernel, parts, half, len(arrays)),
            [((len(arrays), rows, half), BF16)] * parts,
            [in_hbm(array[0, 0]) for array in arrays],
            [HBM_SPEC] * len(arrays),
            [pltpu.SemaphoreType.DMA((parts * len(arrays),))],
            moved=4 * len(arrays) * rows * width_local,
        )

    kv_sent = pack(key_vecs, value_vecs)
    there = [
        [
            (z * 2 + c, (parts * c + (z + j) % parts) * 2 + z // parts)
            for z in range(seq_count)
            for c in range(2)
        ]
        for j in range(parts)
    ]
    inside = [[(z, z // parts * parts + (z - j) % parts) for z in range(seq_count)] for j in range(parts)]
    kv_own = [lax.ppermute(kv_sent[j], axes, there[j]) for j in range(parts)]
    q_sent = pack(queries)
    q_own = [lax.ppermute(q_sent[j], axes, there[j]) for j in range(parts)]
    near_w = lax.ppermute(w_out, ("shard", "guide"), crossed)
    far_w = lax.ppermute(w_out, ("shard", "guide"), straight)
    kv_other = [lax.ppermute(block, "guide", both) for block in kv_own]
    res_here = lax.ppermute(residual[0, 0], axes, there[0])

    head_t = w_head.T
    rows_own, chosen, weight = call(
        functools.partial(early_kernel, seq_count),
        [((channels, LANES), F32), ((seq_count * seq_count, LANES), F32), ((SUBLANES, LANES), F32)],
        [in_hbm(norm_scale), in_hbm(norm_shift), in_hbm(head_t), frame_owner, timesteps],
        [HBM_SPEC] * 3 + [SMEM_SPEC] * 2,
        [
            pltpu.VMEM(norm_scale.shape, F32),
            pltpu.VMEM(norm_shift.shape, F32),
            pltpu.VMEM(head_t.shape, BF16),
            pltpu.SemaphoreType.DMA((3,)),
        ],
        moved=4 * width_shard * LANES,
    )
    rows_got = lax.ppermute(rows_own, "shard", both)
    *q_own, rows_own = lax.optimization_barrier((*q_own, rows_own))

    mixed = call(
        functools.partial(attend_kernel, parts),
        [((rows, half), BF16)] * parts,
        q_own + kv_own + kv_other,
        scratch=[
            pltpu.VMEM((half // HEAD_DIM, rows * parts, 2 * parts * rows), F32),
            pltpu.VMEM((half // HEAD_DIM, rows * parts, HEAD_DIM), F32),
        ],
        flops=8 * rows * parts * rows * parts * half,
        moved=2 * rows * half * parts * 6,
    )
    mixed = [mixed[0]] + [lax.ppermute(mixed[j], "seq", inside[j]) for j in range(1, parts)]

    chunk = 128
    pieces = 4
    width_piece = width_shard // pieces
    got = []
    for i in range(pieces):
        partial = call(
            functools.partial(send_kernel, parts, half, chunk, i * width_piece),
            [((rows, width_piece), BF16)],
            mixed + [near_w, far_w],
            flops=2 * rows * width_local * width_piece,
            moved=2 * width_local * width_piece,
        )[0]
        got.append(lax.ppermute(partial, "shard", both))
    hidden = call(
        functools.partial(keep_kernel, parts, half, chunk),
        [((rows, width_shard), F32)],
        mixed + [near_w, far_w, attn_gate],
        flops=2 * rows * width_local * width_shard,
        moved=2 * width_local * width_shard,
    )[0]
    state = []
    for i in range(pieces):
        first, last = i == 0, i == pieces - 1
        state = call(
            functools.partial(head_kernel, first, last, chunk, i * width_piece),
            [((channels + SUBLANES, rows), F32)]
            if last
            else [((channels, rows), F32), ((rows, LANES), F32), ((rows, LANES), F32)],
            [res_here, hidden, got[i], attn_gate, norm_scale, head_t] + list(state),
            flops=4 * rows * channels * width_piece,
            moved=6 * rows * width_piece,
        )
    sums = state[0]
    sums_got = lax.ppermute(sums, "shard", both)
    keep, send = call(
        functools.partial(norm_kernel, width_model),
        [((channels // 2, rows), F32)] * 2,
        [sums, sums_got, rows_own, rows_got],
        scratch=[pltpu.VMEM((channels, rows), F32)],
    )
    eps_got = lax.ppermute(send, "guide", both)
    fold = LANES // group
    frames = call(
        functools.partial(frame_kernel, seq_count, group),
        [((channels // fold, LANES), F32)] * seq_count,
        [chosen, keep, eps_got],
    )
    arrived = [frames[0]] + [
        lax.ppermute(frames[k], "seq", [(z, z ^ k) for z in range(seq_count)])
        for k in range(1, seq_count)
    ]
    out = call(
        functools.partial(final_kernel, seq_count, group),
        [((channels // 2, rows), F32)],
        [weight, noise[0, 0].T] + arrived,
    )[0]
    return out.T[None, None]


def fast_fits(sizes, queries, residual, w_out, w_head):
    seq_count = sizes["seq"]
    step_count, rows, width_local = queries.shape[1:]
    channels = w_head.shape[1]
    if seq_count < 2 or sizes["guide"] != 2 or sizes["shard"] != 2 or seq_count & (seq_count - 1) or step_count != 1 or rows != LANES:
        return False
    if width_local % (seq_count // 2 * HEAD_DIM) or residual.shape[3] % (4 * LANES):
        return False
    if w_out.shape[1] != residual.shape[3] or channels % (2 * SUBLANES):
        return False
    group = rows // seq_count
    if rows % seq_count or LANES % group:
        return False
    fold = LANES // group
    return channels // 2 % (fold * SUBLANES) == 0


def solution(mesh):
    sizes = dict(mesh.shape)

    def on_device(queries, key_vecs, value_vecs, residual, w_out, attn_gate, norm_shift, norm_scale, w_head, *rest):
        fits = fast_fits(sizes, queries, residual, w_out, w_head)
        plan = fast_plan if fits else general_plan
        return plan(queries, key_vecs, value_vecs, residual, w_out, attn_gate, norm_shift, norm_scale, w_head, *rest)

    return jax.shard_map(
        on_device,
        mesh=mesh,
        in_specs=(
            P("guide", "group", "seq", "shard"),
            P("guide", "group", "seq", "shard"),
            P("guide", "group", "seq", "shard"),
            P("guide", "group", "seq", "shard"),
            P("shard", "guide"),
            P("group", "shard"),
            P("group", "shard"),
            P("group", "shard"),
            P("shard", None),
            P("group", "seq", None, "guide"),
            P("group"),
            P("group", None),
        ),
        out_specs=P("group", "seq", None, "guide"),
        check_vma=False,
    )
```

```python
import functools

import jax
import jax.numpy as jnp
from jax import lax
from jax.experimental import pallas as pl
from jax.experimental.pallas import tpu as pltpu
from jax.sharding import PartitionSpec as P


HEAD_DIM = 128
LANES = 128
SUBLANES = 8
beta_low = 0.0001
beta_high = 0.02
guidance_scale = 3.0
norm_epsilon = 1e-06
LOG2E = 1.4426950408889634


F32 = jnp.float32
BF16 = jnp.bfloat16
VMEM_SPEC = pl.BlockSpec(memory_space=pltpu.VMEM)
SMEM_SPEC = pl.BlockSpec(memory_space=pltpu.SMEM)
HBM_SPEC = pl.BlockSpec(memory_space=pltpu.HBM)


def plan_weight(timesteps):
    steps_float = timesteps.astype(jnp.float32)
    exponent = (steps_float + 1.0) * beta_low + (beta_high - beta_low) * steps_float * (
        steps_float + 1.0
    ) / (2.0 * 999.0)
    return 1.0 - jnp.exp(-exponent)


def attend_all(query_split, keys_all, values_all):
    heads_local = query_split.shape[2]
    keys_split = keys_all.reshape(keys_all.shape[0], keys_all.shape[1], heads_local, HEAD_DIM)
    values_split = values_all.reshape(values_all.shape[0], values_all.shape[1], heads_local, HEAD_DIM)
    scores = jnp.einsum(
        "tqhd,tkhd->tqhk", query_split, keys_split, preferred_element_type=F32
    ) * HEAD_DIM ** (-0.5)
    expo = jnp.exp(scores - jnp.max(scores, axis=-1, keepdims=True))
    total = jnp.sum(expo, axis=-1)
    mixed = jnp.einsum("tqhk,tkhd->tqhd", expo.astype(BF16), values_split, preferred_element_type=F32)
    return (mixed / total[..., None]).astype(BF16)


def general_plan(
    queries, key_vecs, value_vecs, residual, w_out, attn_gate, norm_shift, norm_scale, w_head, noise,
    timesteps, frame_owner,
):
    query_local = queries[0]
    step_count, token_count, width_local = query_local.shape
    heads_local = width_local // HEAD_DIM
    attended = attend_all(
        query_local.reshape(step_count, token_count, heads_local, HEAD_DIM),
        lax.all_gather(key_vecs[0], "seq", axis=1, tiled=True),
        lax.all_gather(value_vecs[0], "seq", axis=1, tiled=True),
    )
    row_count = step_count * token_count
    both_rows = jnp.dot(
        lax.all_gather(attended.reshape(row_count, width_local), "guide", axis=0, tiled=True),
        w_out,
        preferred_element_type=F32,
    )
    half_width = w_out.shape[1]
    swapped = lax.all_to_all(
        both_rows.reshape(2, row_count, half_width), "guide", split_axis=0, concat_axis=2, tiled=True
    )
    projected = swapped.reshape(row_count, 2 * half_width)
    attn_out = lax.psum_scatter(projected, "shard", scatter_dimension=1, tiled=True)
    width_shard = attn_out.shape[1]
    width_model = width_shard * lax.axis_size("shard")
    hidden = residual[0].astype(F32) + attn_gate[:, None, :] * attn_out.reshape(
        step_count, token_count, width_shard
    )
    sum_first, sum_second = lax.psum((jnp.sum(hidden, axis=-1), jnp.sum(hidden * hidden, axis=-1)), "shard")
    mean_row = sum_first / width_model
    var_row = sum_second / width_model - mean_row * mean_row
    inv_std = lax.rsqrt(var_row + norm_epsilon)
    modulated = (hidden - mean_row[..., None]) * inv_std[..., None] * (
        1.0 + norm_scale[:, None, :]
    ) + norm_shift[:, None, :]
    partial_head = jnp.einsum(
        "tqd,dc->tqc", modulated, w_head.astype(F32), precision=lax.Precision.HIGHEST
    )
    predicted = lax.psum(partial_head, "shard")
    seq_count = lax.axis_size("seq")
    frame_group = token_count // seq_count
    frames_view = predicted.reshape(step_count, seq_count, frame_group, predicted.shape[-1])
    owner_table = (
        frame_owner[:, :, None] == jnp.arange(seq_count, dtype=jnp.int32)[None, None, :]
    ).astype(F32)
    by_owner = jnp.einsum("tfo,tfgc->togc", owner_table, frames_view, precision=lax.Precision.HIGHEST)
    arrived = lax.all_to_all(
        lax.all_to_all(by_owner[None], "seq", split_axis=2, concat_axis=3, tiled=True),
        "guide",
        split_axis=4,
        concat_axis=0,
        tiled=True,
    )
    guided = arrived[1] + guidance_scale * (arrived[0] - arrived[1])
    return plan_weight(timesteps)[:, None, None, None] * (guided - noise)


def pack_kernel(parts, half, count, *refs):
    source_refs, out_refs, sems = refs[:count], refs[count:-1], refs[-1]
    z = lax.axis_index("seq")
    copies = []
    for j in range(parts):
        cols = pl.ds(pl.multiple_of(lax.rem(z + j, parts) * half, LANES), half)
        for i in range(count):
            copies.append(
                pltpu.make_async_copy(source_refs[i].at[:, cols], out_refs[j].at[i], sems.at[j * count + i])
            )
    for copy in copies:
        copy.start()
    for copy in copies:
        copy.wait()


def split_kernel(source_ref, *refs):
    out_refs, sems = refs[:-1], refs[-1]
    width = out_refs[0].shape[1]
    copies = [
        pltpu.make_async_copy(source_ref.at[:, pl.ds(i * width, width)], out_ref, sems.at[i])
        for i, out_ref in enumerate(out_refs)
    ]
    for copy in copies:
        copy.start()
    for copy in copies:
        copy.wait()


def attend_kernel(parts, *refs):
    q_refs = refs[:parts]
    kv_refs = refs[parts : 3 * parts]
    o_refs = refs[3 * parts : 4 * parts]
    score_scr, total_scr = refs[4 * parts :]
    heads = q_refs[0].shape[2] // HEAD_DIM
    rows = q_refs[0].shape[1]
    for i in range(heads):
        cols = slice(i * HEAD_DIM, (i + 1) * HEAD_DIM)
        q = jnp.concatenate([r[0, :, cols] for r in q_refs], axis=0)
        for b, kv_ref in enumerate(kv_refs):
            scores = lax.dot_general(q, kv_ref[0, :, cols], (((1,), (1,)), ((), ())), preferred_element_type=F32)
            score_scr[i, :, b * rows : (b + 1) * rows] = scores * (HEAD_DIM ** (-0.5) * LOG2E)
    for i in range(heads):
        scores = score_scr[i]
        expo = jnp.exp2(scores - jnp.max(scores, axis=1, keepdims=True))
        score_scr[i] = expo
        total_scr[i] = jnp.broadcast_to(jnp.sum(expo, axis=1, keepdims=True), total_scr.shape[1:])
    for i in range(heads):
        cols = slice(i * HEAD_DIM, (i + 1) * HEAD_DIM)
        values = jnp.concatenate([r[1, :, cols] for r in kv_refs], axis=0)
        mixed = jnp.dot(score_scr[i].astype(BF16), values, preferred_element_type=F32) / total_scr[i]
        for j in range(parts):
            o_refs[j][:, cols] = mixed[j * rows : (j + 1) * rows].astype(BF16)


def project(parts, half, o_refs, w_ref, cols):
    z = lax.axis_index("seq")
    total = None
    for j in range(parts):
        start = pl.multiple_of(lax.rem(z + j, parts) * half, LANES)
        term = jnp.dot(o_refs[j][...], w_ref[pl.ds(start, half), cols], preferred_element_type=F32)
        total = term if total is None else total + term
    return total


def send_kernel(parts, half, chunk, first, *refs):
    o_refs = refs[:parts]
    near_ref, far_ref, out_ref = refs[parts:]
    guide = lax.axis_index("guide")
    for value, w_ref in ((1, near_ref), (0, far_ref)):

        @pl.when(guide == value)
        def _():
            for t in range(out_ref.shape[1] // chunk):
                cols = slice(first + t * chunk, first + (t + 1) * chunk)
                out_ref[:, t * chunk : (t + 1) * chunk] = project(parts, half, o_refs, w_ref, cols).astype(BF16)


def keep_kernel(parts, half, chunk, *refs):
    o_refs = refs[:parts]
    near_ref, far_ref, gate_ref, out_ref = refs[parts:]
    guide = lax.axis_index("guide")
    for value, w_ref in ((0, near_ref), (1, far_ref)):

        @pl.when(guide == value)
        def _():
            for t in range(out_ref.shape[1] // chunk):
                cols = slice(t * chunk, (t + 1) * chunk)
                out_ref[:, cols] = gate_ref[:, cols] * project(parts, half, o_refs, w_ref, cols)


def split_dot(head_t, rows):
    dims = (((1,), (1,)), ((), ()))
    high = rows.astype(BF16)
    low = (rows - high.astype(F32)).astype(BF16)
    return lax.dot_general(head_t, high, dims, preferred_element_type=F32) + lax.dot_general(
        head_t, low, dims, preferred_element_type=F32
    )


def early_kernel(
    seq_count, scale_hbm, shift_hbm, head_hbm, owner_ref, steps_ref, out_ref, chosen_ref, weight_ref,
    scale_ref, shift_ref, head_ref, sems,
):
    copies = [
        pltpu.make_async_copy(source, target, sems.at[i])
        for i, (source, target) in enumerate(
            ((scale_hbm, scale_ref), (shift_hbm, shift_ref), (head_hbm, head_ref))
        )
    ]
    for copy in copies:
        copy.start()
    z = lax.axis_index("seq")
    for k in range(seq_count):
        for f in range(seq_count):
            here = jnp.where(owner_ref[0, f] == z ^ k, 1.0, 0.0)
            chosen_ref[k * seq_count + f : k * seq_count + f + 1, :] = jnp.full((1, LANES), here, F32)
    weight_ref[...] = plan_weight(jnp.full((SUBLANES, LANES), steps_ref[0], jnp.int32))
    for copy in copies:
        copy.wait()
    width = scale_ref.shape[1]
    which = lax.broadcasted_iota(jnp.int32, (LANES, width), 0)
    rows = jnp.where(which == 0, 1.0 + scale_ref[...], shift_ref[...])
    high = rows.astype(BF16)
    rest = rows - high.astype(F32)
    mid = rest.astype(BF16)
    low = (rest - mid.astype(F32)).astype(BF16)
    dims = (((1,), (1,)), ((), ()))
    total = None
    for part in (high, mid, low):
        term = lax.dot_general(head_ref[...], part, dims, preferred_element_type=F32)
        total = term if total is None else total + term
    out_ref[...] = total


def head_kernel(first, last, chunk, start, *refs):
    res_ref, hid_ref, got_ref, gate_ref, scale_ref, head_ref = refs[:6]
    if first:
        out_refs = refs[6:]
    else:
        prev_refs, out_refs = refs[6:9], refs[9:]
    channels = head_ref.shape[0]
    rows = hid_ref.shape[0]
    acc_one = jnp.zeros((rows, LANES), F32) if first else prev_refs[1][...]
    acc_two = jnp.zeros((rows, LANES), F32) if first else prev_refs[2][...]
    acc_head = jnp.zeros((channels, rows), F32) if first else prev_refs[0][...]
    for t in range(got_ref.shape[1] // chunk):
        cols = slice(start + t * chunk, start + (t + 1) * chunk)
        arrived = got_ref[:, t * chunk : (t + 1) * chunk].astype(F32)
        here = slice(cols.start % res_ref.shape[1], cols.start % res_ref.shape[1] + chunk)
        hidden = res_ref[:, here].astype(F32) + hid_ref[:, cols] + gate_ref[:, cols] * arrived
        for s in range(chunk // LANES):
            piece = hidden[:, s * LANES : (s + 1) * LANES]
            acc_one = acc_one + piece
            acc_two = acc_two + piece * piece
        acc_head = acc_head + split_dot(head_ref[:, cols], hidden * (1.0 + scale_ref[:, cols]))
    if last:
        out_ref = out_refs[0]
        out_ref[0:channels, :] = acc_head
        sum_one = jnp.sum(acc_one.T, axis=0, keepdims=True)
        sum_two = jnp.sum(acc_two.T, axis=0, keepdims=True)
        row = lax.broadcasted_iota(jnp.int32, (SUBLANES, rows), 0)
        out_ref[channels : channels + SUBLANES, :] = jnp.where(row == 0, sum_one, sum_two)
    else:
        out_refs[0][...] = acc_head
        out_refs[1][...] = acc_one
        out_refs[2][...] = acc_two


def norm_kernel(width_model, own_ref, got_ref, rows_own_ref, rows_got_ref, keep_ref, send_ref, eps_scr):
    channels = rows_own_ref.shape[0]
    half_channels = channels // 2
    guide = lax.axis_index("guide")
    head = own_ref[0:channels, :] + got_ref[0:channels, :]
    stats = own_ref[channels : channels + SUBLANES, :] + got_ref[channels : channels + SUBLANES, :]
    mean = stats[0:1] / width_model
    var = stats[1:2] / width_model - mean * mean
    inv_std = lax.rsqrt(var + norm_epsilon)
    scaled = rows_own_ref[:, 0:1] + rows_got_ref[:, 0:1]
    shifted = rows_own_ref[:, 1:2] + rows_got_ref[:, 1:2]
    eps_scr[...] = (head - mean * scaled) * inv_std + shifted
    keep_ref[...] = eps_scr[pl.ds(pl.multiple_of(guide * half_channels, SUBLANES), half_channels), :]
    send_ref[...] = eps_scr[pl.ds(pl.multiple_of((1 - guide) * half_channels, SUBLANES), half_channels), :]


def frame_kernel(seq_count, group, chosen_ref, keep_ref, got_ref, *out_refs):
    first = lax.axis_index("guide") == 0
    mine, other = keep_ref[...], got_ref[...]
    fold = LANES // group
    rows = mine.shape[0] // fold
    lane = lax.broadcasted_iota(jnp.int32, (rows, LANES), 1) // group
    for sub, block in enumerate((jnp.where(first, mine, other), jnp.where(first, other, mine))):
        packed = []
        for f in range(seq_count):
            frame = jnp.zeros((rows, LANES), F32)
            for j in range(fold):
                piece = block[j * rows : (j + 1) * rows]
                shift = (j - f) * group % LANES
                frame = jnp.where(lane == j, pltpu.roll(piece, shift, axis=1) if shift else piece, frame)
            packed.append(frame)
        for k in range(seq_count):
            frame = packed[0]
            for f in range(1, seq_count):
                frame = jnp.where(chosen_ref[k * seq_count + f : k * seq_count + f + 1, :] > 0.5, packed[f], frame)
            out_refs[k][sub * rows : (sub + 1) * rows, :] = frame


def final_kernel(seq_count, group, weight_ref, noise_ref, *refs):
    piece_refs, out_ref = refs[:seq_count], refs[seq_count]
    z = lax.axis_index("seq")
    parts = seq_count // 2
    fold = LANES // group
    rows = piece_refs[0].shape[0] // 2
    lane = lax.broadcasted_iota(jnp.int32, (rows, LANES), 1) // group
    for j in range(fold):
        eps_cond = jnp.zeros((rows, LANES), F32)
        eps_free = jnp.zeros((rows, LANES), F32)
        for k in range(seq_count):
            source = z ^ k
            branch, position = source // parts, lax.rem(source, parts)
            for sub in range(2):
                block = parts * sub + position
                shift = lax.rem((block - j) * group + LANES, LANES)
                rolled = pltpu.roll(piece_refs[k][sub * rows : (sub + 1) * rows], shift, axis=1)
                eps_cond = jnp.where((lane == block) & (branch == 0), rolled, eps_cond)
                eps_free = jnp.where((lane == block) & (branch == 1), rolled, eps_free)
        part = slice(j * rows, (j + 1) * rows)
        guided = eps_free + guidance_scale * (eps_cond - eps_free)
        out_ref[part, :] = weight_ref[0:1, :] * (guided - noise_ref[part, :])


def call(kernel, outs, args, specs=None, scratch=(), flops=0, moved=0, grant=16):
    shapes = [jax.ShapeDtypeStruct(s, d) for s, d in outs]
    return pl.pallas_call(
        kernel,
        out_shape=shapes,
        in_specs=specs or [VMEM_SPEC] * len(args),
        out_specs=[VMEM_SPEC] * len(outs),
        scratch_shapes=list(scratch),
        compiler_params=pltpu.CompilerParams(vmem_limit_bytes=grant << 20),
        cost_estimate=pl.CostEstimate(flops=flops, bytes_accessed=moved, transcendentals=0),
    )(*args)


def in_hbm(array):
    return pltpu.with_memory_space_constraint(array, pltpu.HBM)


def fast_plan(
    queries, key_vecs, value_vecs, residual, w_out, attn_gate, norm_shift, norm_scale, w_head, noise,
    timesteps, frame_owner,
):
    seq_count = lax.axis_size("seq")
    parts = seq_count // 2
    rows, width_local = queries.shape[2:]
    half = width_local // parts
    width_shard = residual.shape[3]
    channels = w_head.shape[1]
    group = rows // seq_count
    width_model = float(width_shard * lax.axis_size("shard"))
    both = [(0, 1), (1, 0)]
    axes = ("seq", "guide")

    crossed = [(x * 2 + c, x * 2 + (c + x) % 2) for x in range(2) for c in range(2)]
    straight = [(x * 2 + c, x * 2 + (c + x + 1) % 2) for x in range(2) for c in range(2)]

    def pack(*arrays):
        return call(
            functools.partial(pack_kernel, parts, half, len(arrays)),
            [((len(arrays), rows, half), BF16)] * parts,
            [in_hbm(array[0, 0]) for array in arrays],
            [HBM_SPEC] * len(arrays),
            [pltpu.SemaphoreType.DMA((parts * len(arrays),))],
            moved=4 * len(arrays) * rows * width_local,
        )

    kv_sent = pack(key_vecs, value_vecs)
    there = [
        [
            (z * 2 + c, (parts * c + (z + j) % parts) * 2 + z // parts)
            for z in range(seq_count)
            for c in range(2)
        ]
        for j in range(parts)
    ]
    inside = [[(z, z // parts * parts + (z - j) % parts) for z in range(seq_count)] for j in range(parts)]
    kv_own = [lax.ppermute(kv_sent[j], axes, there[j]) for j in range(parts)]
    q_sent = pack(queries)
    q_own = [lax.ppermute(q_sent[j], axes, there[j]) for j in range(parts)]
    near_w = lax.ppermute(w_out, ("shard", "guide"), crossed)
    far_w = lax.ppermute(w_out, ("shard", "guide"), straight)
    kv_other = [lax.ppermute(block, "guide", both) for block in kv_own]
    res_sent = call(
        split_kernel,
        [((rows, width_shard // 2), BF16)] * 2,
        [in_hbm(residual[0, 0])],
        [HBM_SPEC],
        [pltpu.SemaphoreType.DMA((2,))],
        moved=4 * rows * width_shard,
    )
    res_here = [lax.ppermute(block, axes, there[0]) for block in res_sent]

    head_t = w_head.T
    rows_own, chosen, weight = call(
        functools.partial(early_kernel, seq_count),
        [((channels, LANES), F32), ((seq_count * seq_count, LANES), F32), ((SUBLANES, LANES), F32)],
        [in_hbm(norm_scale), in_hbm(norm_shift), in_hbm(head_t), frame_owner, timesteps],
        [HBM_SPEC] * 3 + [SMEM_SPEC] * 2,
        [
            pltpu.VMEM(norm_scale.shape, F32),
            pltpu.VMEM(norm_shift.shape, F32),
            pltpu.VMEM(head_t.shape, BF16),
            pltpu.SemaphoreType.DMA((3,)),
        ],
        moved=4 * width_shard * LANES,
    )
    rows_got = lax.ppermute(rows_own, "shard", both)
    *q_own, rows_own = lax.optimization_barrier((*q_own, rows_own))

    mixed = call(
        functools.partial(attend_kernel, parts),
        [((rows, half), BF16)] * parts,
        q_own + kv_own + kv_other,
        scratch=[
            pltpu.VMEM((half // HEAD_DIM, rows * parts, 2 * parts * rows), F32),
            pltpu.VMEM((half // HEAD_DIM, rows * parts, HEAD_DIM), F32),
        ],
        flops=8 * rows * parts * rows * parts * half,
        moved=2 * rows * half * parts * 6,
    )
    mixed = [mixed[0]] + [lax.ppermute(mixed[j], "seq", inside[j]) for j in range(1, parts)]

    chunk = 128
    quarter = width_shard // 4
    pieces = [(0, 2 * quarter), (2 * quarter, quarter), (3 * quarter, quarter)]
    got = []
    for start, width in pieces:
        partial = call(
            functools.partial(send_kernel, parts, half, chunk, start),
            [((rows, width), BF16)],
            mixed + [near_w, far_w],
            flops=2 * rows * width_local * width,
            moved=2 * width_local * width,
        )[0]
        got.append(lax.ppermute(partial, "shard", both))
    hidden = call(
        functools.partial(keep_kernel, parts, half, chunk),
        [((rows, width_shard), F32)],
        mixed + [near_w, far_w, attn_gate],
        flops=2 * rows * width_local * width_shard,
        moved=2 * width_local * width_shard,
    )[0]
    state = []
    for i, (start, width) in enumerate(pieces):
        first, last = i == 0, i == len(pieces) - 1
        state = call(
            functools.partial(head_kernel, first, last, chunk, start),
            [((channels + SUBLANES, rows), F32)]
            if last
            else [((channels, rows), F32), ((rows, LANES), F32), ((rows, LANES), F32)],
            [res_here[0 if first else 1], hidden, got[i], attn_gate, norm_scale, head_t] + list(state),
            flops=4 * rows * channels * width,
            moved=6 * rows * width,
        )
    sums = state[0]
    sums_got = lax.ppermute(sums, "shard", both)
    keep, send = call(
        functools.partial(norm_kernel, width_model),
        [((channels // 2, rows), F32)] * 2,
        [sums, sums_got, rows_own, rows_got],
        scratch=[pltpu.VMEM((channels, rows), F32)],
    )
    eps_got = lax.ppermute(send, "guide", both)
    fold = LANES // group
    frames = call(
        functools.partial(frame_kernel, seq_count, group),
        [((channels // fold, LANES), F32)] * seq_count,
        [chosen, keep, eps_got],
    )
    arrived = [frames[0]] + [
        lax.ppermute(frames[k], "seq", [(z, z ^ k) for z in range(seq_count)])
        for k in range(1, seq_count)
    ]
    out = call(
        functools.partial(final_kernel, seq_count, group),
        [((channels // 2, rows), F32)],
        [weight, noise[0, 0].T] + arrived,
    )[0]
    return out.T[None, None]


def fast_fits(sizes, queries, residual, w_out, w_head):
    seq_count = sizes["seq"]
    step_count, rows, width_local = queries.shape[1:]
    channels = w_head.shape[1]
    if seq_count < 2 or sizes["guide"] != 2 or sizes["shard"] != 2 or seq_count & (seq_count - 1) or step_count != 1 or rows != LANES:
        return False
    if width_local % (seq_count // 2 * HEAD_DIM) or residual.shape[3] % (4 * LANES):
        return False
    if w_out.shape[1] != residual.shape[3] or channels % (2 * SUBLANES):
        return False
    group = rows // seq_count
    if rows % seq_count or LANES % group:
        return False
    fold = LANES // group
    return channels // 2 % (fold * SUBLANES) == 0


def solution(mesh):
    sizes = dict(mesh.shape)

    def on_device(queries, key_vecs, value_vecs, residual, w_out, attn_gate, norm_shift, norm_scale, w_head, *rest):
        fits = fast_fits(sizes, queries, residual, w_out, w_head)
        plan = fast_plan if fits else general_plan
        return plan(queries, key_vecs, value_vecs, residual, w_out, attn_gate, norm_shift, norm_scale, w_head, *rest)

    return jax.shard_map(
        on_device,
        mesh=mesh,
        in_specs=(
            P("guide", "group", "seq", "shard"),
            P("guide", "group", "seq", "shard"),
            P("guide", "group", "seq", "shard"),
            P("guide", "group", "seq", "shard"),
            P("shard", "guide"),
            P("group", "shard"),
            P("group", "shard"),
            P("group", "shard"),
            P("shard", None),
            P("group", "seq", None, "guide"),
            P("group"),
            P("group", None),
        ),
        out_specs=P("group", "seq", None, "guide"),
        check_vma=False,
    )
```

```python
import functools

import jax
import jax.numpy as jnp
from jax import lax
from jax.experimental import pallas as pl
from jax.experimental.pallas import tpu as pltpu
from jax.sharding import PartitionSpec as P


HEAD_DIM = 128
LANES = 128
SUBLANES = 8
beta_low = 0.0001
beta_high = 0.02
guidance_scale = 3.0
norm_epsilon = 1e-06
LOG2E = 1.4426950408889634


F32 = jnp.float32
BF16 = jnp.bfloat16
VMEM_SPEC = pl.BlockSpec(memory_space=pltpu.VMEM)
SMEM_SPEC = pl.BlockSpec(memory_space=pltpu.SMEM)
HBM_SPEC = pl.BlockSpec(memory_space=pltpu.HBM)


def plan_weight(timesteps):
    steps_float = timesteps.astype(jnp.float32)
    exponent = (steps_float + 1.0) * beta_low + (beta_high - beta_low) * steps_float * (
        steps_float + 1.0
    ) / (2.0 * 999.0)
    return 1.0 - jnp.exp(-exponent)


def attend_all(query_split, keys_all, values_all):
    heads_local = query_split.shape[2]
    keys_split = keys_all.reshape(keys_all.shape[0], keys_all.shape[1], heads_local, HEAD_DIM)
    values_split = values_all.reshape(values_all.shape[0], values_all.shape[1], heads_local, HEAD_DIM)
    scores = jnp.einsum(
        "tqhd,tkhd->tqhk", query_split, keys_split, preferred_element_type=F32
    ) * HEAD_DIM ** (-0.5)
    expo = jnp.exp(scores - jnp.max(scores, axis=-1, keepdims=True))
    total = jnp.sum(expo, axis=-1)
    mixed = jnp.einsum("tqhk,tkhd->tqhd", expo.astype(BF16), values_split, preferred_element_type=F32)
    return (mixed / total[..., None]).astype(BF16)


def general_plan(
    queries, key_vecs, value_vecs, residual, w_out, attn_gate, norm_shift, norm_scale, w_head, noise,
    timesteps, frame_owner,
):
    query_local = queries[0]
    step_count, token_count, width_local = query_local.shape
    heads_local = width_local // HEAD_DIM
    attended = attend_all(
        query_local.reshape(step_count, token_count, heads_local, HEAD_DIM),
        lax.all_gather(key_vecs[0], "seq", axis=1, tiled=True),
        lax.all_gather(value_vecs[0], "seq", axis=1, tiled=True),
    )
    row_count = step_count * token_count
    both_rows = jnp.dot(
        lax.all_gather(attended.reshape(row_count, width_local), "guide", axis=0, tiled=True),
        w_out,
        preferred_element_type=F32,
    )
    half_width = w_out.shape[1]
    swapped = lax.all_to_all(
        both_rows.reshape(2, row_count, half_width), "guide", split_axis=0, concat_axis=2, tiled=True
    )
    projected = swapped.reshape(row_count, 2 * half_width)
    attn_out = lax.psum_scatter(projected, "shard", scatter_dimension=1, tiled=True)
    width_shard = attn_out.shape[1]
    width_model = width_shard * lax.axis_size("shard")
    hidden = residual[0].astype(F32) + attn_gate[:, None, :] * attn_out.reshape(
        step_count, token_count, width_shard
    )
    sum_first, sum_second = lax.psum((jnp.sum(hidden, axis=-1), jnp.sum(hidden * hidden, axis=-1)), "shard")
    mean_row = sum_first / width_model
    var_row = sum_second / width_model - mean_row * mean_row
    inv_std = lax.rsqrt(var_row + norm_epsilon)
    modulated = (hidden - mean_row[..., None]) * inv_std[..., None] * (
        1.0 + norm_scale[:, None, :]
    ) + norm_shift[:, None, :]
    partial_head = jnp.einsum(
        "tqd,dc->tqc", modulated, w_head.astype(F32), precision=lax.Precision.HIGHEST
    )
    predicted = lax.psum(partial_head, "shard")
    seq_count = lax.axis_size("seq")
    frame_group = token_count // seq_count
    frames_view = predicted.reshape(step_count, seq_count, frame_group, predicted.shape[-1])
    owner_table = (
        frame_owner[:, :, None] == jnp.arange(seq_count, dtype=jnp.int32)[None, None, :]
    ).astype(F32)
    by_owner = jnp.einsum("tfo,tfgc->togc", owner_table, frames_view, precision=lax.Precision.HIGHEST)
    arrived = lax.all_to_all(
        lax.all_to_all(by_owner[None], "seq", split_axis=2, concat_axis=3, tiled=True),
        "guide",
        split_axis=4,
        concat_axis=0,
        tiled=True,
    )
    guided = arrived[1] + guidance_scale * (arrived[0] - arrived[1])
    return plan_weight(timesteps)[:, None, None, None] * (guided - noise)


def pack_kernel(parts, half, count, *refs):
    source_refs, out_refs, sems = refs[:count], refs[count:-1], refs[-1]
    z = lax.axis_index("seq")
    copies = []
    for j in range(parts):
        cols = pl.ds(pl.multiple_of(lax.rem(z + j, parts) * half, LANES), half)
        for i in range(count):
            copies.append(
                pltpu.make_async_copy(source_refs[i].at[:, cols], out_refs[j].at[i], sems.at[j * count + i])
            )
    for copy in copies:
        copy.start()
    for copy in copies:
        copy.wait()


def split_kernel(source_ref, *refs):
    out_refs, sems = refs[:-1], refs[-1]
    width = out_refs[0].shape[1]
    copies = [
        pltpu.make_async_copy(source_ref.at[:, pl.ds(i * width, width)], out_ref, sems.at[i])
        for i, out_ref in enumerate(out_refs)
    ]
    for copy in copies:
        copy.start()
    for copy in copies:
        copy.wait()


def attend_kernel(parts, *refs):
    q_refs = refs[:parts]
    kv_refs = refs[parts : 3 * parts]
    o_refs = refs[3 * parts : 4 * parts]
    score_scr, total_scr = refs[4 * parts :]
    heads = q_refs[0].shape[2] // HEAD_DIM
    rows = q_refs[0].shape[1]
    for i in range(heads):
        cols = slice(i * HEAD_DIM, (i + 1) * HEAD_DIM)
        q = jnp.concatenate([r[0, :, cols] for r in q_refs], axis=0)
        for b, kv_ref in enumerate(kv_refs):
            scores = lax.dot_general(q, kv_ref[0, :, cols], (((1,), (1,)), ((), ())), preferred_element_type=F32)
            score_scr[i, :, b * rows : (b + 1) * rows] = scores * (HEAD_DIM ** (-0.5) * LOG2E)
    for i in range(heads):
        scores = score_scr[i]
        expo = jnp.exp2(scores - jnp.max(scores, axis=1, keepdims=True))
        score_scr[i] = expo
        total_scr[i] = jnp.broadcast_to(jnp.sum(expo, axis=1, keepdims=True), total_scr.shape[1:])
    for i in range(heads):
        cols = slice(i * HEAD_DIM, (i + 1) * HEAD_DIM)
        values = jnp.concatenate([r[1, :, cols] for r in kv_refs], axis=0)
        mixed = jnp.dot(score_scr[i].astype(BF16), values, preferred_element_type=F32) / total_scr[i]
        for j in range(parts):
            o_refs[j][:, cols] = mixed[j * rows : (j + 1) * rows].astype(BF16)


def project(parts, half, o_refs, w_ref, cols):
    z = lax.axis_index("seq")
    total = None
    for j in range(parts):
        start = pl.multiple_of(lax.rem(z + j, parts) * half, LANES)
        term = jnp.dot(o_refs[j][...], w_ref[pl.ds(start, half), cols], preferred_element_type=F32)
        total = term if total is None else total + term
    return total


def send_kernel(parts, half, chunk, first, *refs):
    o_refs = refs[:parts]
    near_ref, far_ref, out_ref = refs[parts:]
    guide = lax.axis_index("guide")
    for value, w_ref in ((1, near_ref), (0, far_ref)):

        @pl.when(guide == value)
        def _():
            for t in range(out_ref.shape[1] // chunk):
                cols = slice(first + t * chunk, first + (t + 1) * chunk)
                out_ref[:, t * chunk : (t + 1) * chunk] = project(parts, half, o_refs, w_ref, cols).astype(BF16)


def keep_kernel(parts, half, chunk, *refs):
    o_refs = refs[:parts]
    near_ref, far_ref, gate_ref, out_ref = refs[parts:]
    guide = lax.axis_index("guide")
    for value, w_ref in ((0, near_ref), (1, far_ref)):

        @pl.when(guide == value)
        def _():
            for t in range(out_ref.shape[1] // chunk):
                cols = slice(t * chunk, (t + 1) * chunk)
                out_ref[:, cols] = gate_ref[:, cols] * project(parts, half, o_refs, w_ref, cols)


def split_dot(head_t, rows):
    dims = (((1,), (1,)), ((), ()))
    high = rows.astype(BF16)
    low = (rows - high.astype(F32)).astype(BF16)
    return lax.dot_general(head_t, high, dims, preferred_element_type=F32) + lax.dot_general(
        head_t, low, dims, preferred_element_type=F32
    )


def early_kernel(
    seq_count, scale_hbm, shift_hbm, head_hbm, owner_ref, steps_ref, out_ref, chosen_ref, weight_ref,
    scale_ref, shift_ref, head_ref, sems,
):
    copies = [
        pltpu.make_async_copy(source, target, sems.at[i])
        for i, (source, target) in enumerate(
            ((scale_hbm, scale_ref), (shift_hbm, shift_ref), (head_hbm, head_ref))
        )
    ]
    for copy in copies:
        copy.start()
    z = lax.axis_index("seq")
    for k in range(seq_count):
        for f in range(seq_count):
            here = jnp.where(owner_ref[0, f] == z ^ k, 1.0, 0.0)
            chosen_ref[k * seq_count + f : k * seq_count + f + 1, :] = jnp.full((1, LANES), here, F32)
    weight_ref[...] = plan_weight(jnp.full((SUBLANES, LANES), steps_ref[0], jnp.int32))
    for copy in copies:
        copy.wait()
    width = scale_ref.shape[1]
    which = lax.broadcasted_iota(jnp.int32, (LANES, width), 0)
    rows = jnp.where(which == 0, 1.0 + scale_ref[...], shift_ref[...])
    high = rows.astype(BF16)
    rest = rows - high.astype(F32)
    mid = rest.astype(BF16)
    low = (rest - mid.astype(F32)).astype(BF16)
    dims = (((1,), (1,)), ((), ()))
    total = None
    for part in (high, mid, low):
        term = lax.dot_general(head_ref[...], part, dims, preferred_element_type=F32)
        total = term if total is None else total + term
    out_ref[...] = total


def head_kernel(first, last, chunk, start, *refs):
    res_ref, hid_ref, got_ref, gate_ref, scale_ref, head_ref = refs[:6]
    if first:
        out_refs = refs[6:]
    else:
        prev_refs, out_refs = refs[6:9], refs[9:]
    channels = head_ref.shape[0]
    rows = hid_ref.shape[0]
    acc_one = jnp.zeros((rows, LANES), F32) if first else prev_refs[1][...]
    acc_two = jnp.zeros((rows, LANES), F32) if first else prev_refs[2][...]
    acc_head = jnp.zeros((channels, rows), F32) if first else prev_refs[0][...]
    for t in range(got_ref.shape[1] // chunk):
        cols = slice(start + t * chunk, start + (t + 1) * chunk)
        arrived = got_ref[:, t * chunk : (t + 1) * chunk].astype(F32)
        here = slice(cols.start % res_ref.shape[1], cols.start % res_ref.shape[1] + chunk)
        hidden = res_ref[:, here].astype(F32) + hid_ref[:, cols] + gate_ref[:, cols] * arrived
        for s in range(chunk // LANES):
            piece = hidden[:, s * LANES : (s + 1) * LANES]
            acc_one = acc_one + piece
            acc_two = acc_two + piece * piece
        acc_head = acc_head + split_dot(head_ref[:, cols], hidden * (1.0 + scale_ref[:, cols]))
    if last:
        out_ref = out_refs[0]
        out_ref[0:channels, :] = acc_head
        sum_one = jnp.sum(acc_one.T, axis=0, keepdims=True)
        sum_two = jnp.sum(acc_two.T, axis=0, keepdims=True)
        row = lax.broadcasted_iota(jnp.int32, (SUBLANES, rows), 0)
        out_ref[channels : channels + SUBLANES, :] = jnp.where(row == 0, sum_one, sum_two)
    else:
        out_refs[0][...] = acc_head
        out_refs[1][...] = acc_one
        out_refs[2][...] = acc_two


def norm_kernel(width_model, own_ref, got_ref, rows_own_ref, rows_got_ref, keep_ref, send_ref, eps_scr):
    channels = rows_own_ref.shape[0]
    half_channels = channels // 2
    guide = lax.axis_index("guide")
    head = own_ref[0:channels, :] + got_ref[0:channels, :]
    stats = own_ref[channels : channels + SUBLANES, :] + got_ref[channels : channels + SUBLANES, :]
    mean = stats[0:1] / width_model
    var = stats[1:2] / width_model - mean * mean
    inv_std = lax.rsqrt(var + norm_epsilon)
    scaled = rows_own_ref[:, 0:1] + rows_got_ref[:, 0:1]
    shifted = rows_own_ref[:, 1:2] + rows_got_ref[:, 1:2]
    eps_scr[...] = (head - mean * scaled) * inv_std + shifted
    keep_ref[...] = eps_scr[pl.ds(pl.multiple_of(guide * half_channels, SUBLANES), half_channels), :]
    send_ref[...] = eps_scr[pl.ds(pl.multiple_of((1 - guide) * half_channels, SUBLANES), half_channels), :]


def frame_kernel(seq_count, group, chosen_ref, keep_ref, got_ref, *out_refs):
    first = lax.axis_index("guide") == 0
    mine, other = keep_ref[...], got_ref[...]
    fold = LANES // group
    rows = mine.shape[0] // fold
    lane = lax.broadcasted_iota(jnp.int32, (rows, LANES), 1) // group
    for sub, block in enumerate((jnp.where(first, mine, other), jnp.where(first, other, mine))):
        packed = []
        for f in range(seq_count):
            frame = jnp.zeros((rows, LANES), F32)
            for j in range(fold):
                piece = block[j * rows : (j + 1) * rows]
                shift = (j - f) * group % LANES
                frame = jnp.where(lane == j, pltpu.roll(piece, shift, axis=1) if shift else piece, frame)
            packed.append(frame)
        for k in range(seq_count):
            frame = packed[0]
            for f in range(1, seq_count):
                frame = jnp.where(chosen_ref[k * seq_count + f : k * seq_count + f + 1, :] > 0.5, packed[f], frame)
            out_refs[k][sub * rows : (sub + 1) * rows, :] = frame


def final_kernel(seq_count, group, weight_ref, noise_ref, *refs):
    piece_refs, out_ref = refs[:seq_count], refs[seq_count]
    z = lax.axis_index("seq")
    parts = seq_count // 2
    fold = LANES // group
    rows = piece_refs[0].shape[0] // 2
    lane = lax.broadcasted_iota(jnp.int32, (rows, LANES), 1) // group
    for j in range(fold):
        eps_cond = jnp.zeros((rows, LANES), F32)
        eps_free = jnp.zeros((rows, LANES), F32)
        for k in range(seq_count):
            source = z ^ k
            branch, position = source // parts, lax.rem(source, parts)
            for sub in range(2):
                block = parts * sub + position
                shift = lax.rem((block - j) * group + LANES, LANES)
                rolled = pltpu.roll(piece_refs[k][sub * rows : (sub + 1) * rows], shift, axis=1)
                eps_cond = jnp.where((lane == block) & (branch == 0), rolled, eps_cond)
                eps_free = jnp.where((lane == block) & (branch == 1), rolled, eps_free)
        part = slice(j * rows, (j + 1) * rows)
        guided = eps_free + guidance_scale * (eps_cond - eps_free)
        out_ref[part, :] = weight_ref[0:1, :] * (guided - noise_ref[part, :])


def call(kernel, outs, args, specs=None, scratch=(), flops=0, moved=0, grant=16):
    shapes = [jax.ShapeDtypeStruct(s, d) for s, d in outs]
    return pl.pallas_call(
        kernel,
        out_shape=shapes,
        in_specs=specs or [VMEM_SPEC] * len(args),
        out_specs=[VMEM_SPEC] * len(outs),
        scratch_shapes=list(scratch),
        compiler_params=pltpu.CompilerParams(vmem_limit_bytes=grant << 20),
        cost_estimate=pl.CostEstimate(flops=flops, bytes_accessed=moved, transcendentals=0),
    )(*args)


def in_hbm(array):
    return pltpu.with_memory_space_constraint(array, pltpu.HBM)


def fast_plan(
    queries, key_vecs, value_vecs, residual, w_out, attn_gate, norm_shift, norm_scale, w_head, noise,
    timesteps, frame_owner,
):
    seq_count = lax.axis_size("seq")
    parts = seq_count // 2
    rows, width_local = queries.shape[2:]
    half = width_local // parts
    width_shard = residual.shape[3]
    channels = w_head.shape[1]
    group = rows // seq_count
    width_model = float(width_shard * lax.axis_size("shard"))
    both = [(0, 1), (1, 0)]
    axes = ("seq", "guide")

    crossed = [(x * 2 + c, x * 2 + (c + x) % 2) for x in range(2) for c in range(2)]
    straight = [(x * 2 + c, x * 2 + (c + x + 1) % 2) for x in range(2) for c in range(2)]

    def pack(*arrays):
        return call(
            functools.partial(pack_kernel, parts, half, len(arrays)),
            [((len(arrays), rows, half), BF16)] * parts,
            [in_hbm(array[0, 0]) for array in arrays],
            [HBM_SPEC] * len(arrays),
            [pltpu.SemaphoreType.DMA((parts * len(arrays),))],
            moved=4 * len(arrays) * rows * width_local,
        )

    kv_sent = pack(key_vecs, value_vecs)
    there = [
        [
            (z * 2 + c, (parts * c + (z + j) % parts) * 2 + z // parts)
            for z in range(seq_count)
            for c in range(2)
        ]
        for j in range(parts)
    ]
    inside = [[(z, z // parts * parts + (z - j) % parts) for z in range(seq_count)] for j in range(parts)]
    kv_own = [lax.ppermute(kv_sent[j], axes, there[j]) for j in range(parts)]
    q_sent = pack(queries)
    q_own = [lax.ppermute(q_sent[j], axes, there[j]) for j in range(parts)]
    near_w = lax.ppermute(w_out, ("shard", "guide"), crossed)
    far_w = lax.ppermute(w_out, ("shard", "guide"), straight)
    kv_other = [lax.ppermute(block, "guide", both) for block in kv_own]
    res_sent = call(
        split_kernel,
        [((rows, width_shard // 2), BF16)] * 2,
        [in_hbm(residual[0, 0])],
        [HBM_SPEC],
        [pltpu.SemaphoreType.DMA((2,))],
        moved=4 * rows * width_shard,
    )
    res_here = [lax.ppermute(block, axes, there[0]) for block in res_sent]

    head_t = w_head.T
    rows_own, chosen, weight = call(
        functools.partial(early_kernel, seq_count),
        [((channels, LANES), F32), ((seq_count * seq_count, LANES), F32), ((SUBLANES, LANES), F32)],
        [in_hbm(norm_scale), in_hbm(norm_shift), in_hbm(head_t), frame_owner, timesteps],
        [HBM_SPEC] * 3 + [SMEM_SPEC] * 2,
        [
            pltpu.VMEM(norm_scale.shape, F32),
            pltpu.VMEM(norm_shift.shape, F32),
            pltpu.VMEM(head_t.shape, BF16),
            pltpu.SemaphoreType.DMA((3,)),
        ],
        moved=4 * width_shard * LANES,
    )
    rows_got = lax.ppermute(rows_own, "shard", both)
    *q_own, rows_own = lax.optimization_barrier((*q_own, rows_own))

    mixed = call(
        functools.partial(attend_kernel, parts),
        [((rows, half), BF16)] * parts,
        q_own + kv_own + kv_other,
        scratch=[
            pltpu.VMEM((half // HEAD_DIM, rows * parts, 2 * parts * rows), F32),
            pltpu.VMEM((half // HEAD_DIM, rows * parts, HEAD_DIM), F32),
        ],
        flops=8 * rows * parts * rows * parts * half,
        moved=2 * rows * half * parts * 6,
    )
    mixed = [mixed[0]] + [lax.ppermute(mixed[j], "seq", inside[j]) for j in range(1, parts)]

    chunk = 128
    pieces = 4
    width_piece = width_shard // pieces
    got = []
    for i in range(pieces):
        partial = call(
            functools.partial(send_kernel, parts, half, chunk, i * width_piece),
            [((rows, width_piece), BF16)],
            mixed + [near_w, far_w],
            flops=2 * rows * width_local * width_piece,
            moved=2 * width_local * width_piece,
        )[0]
        got.append(lax.ppermute(partial, "shard", both))
    hidden = call(
        functools.partial(keep_kernel, parts, half, chunk),
        [((rows, width_shard), F32)],
        mixed + [near_w, far_w, attn_gate],
        flops=2 * rows * width_local * width_shard,
        moved=2 * width_local * width_shard,
    )[0]
    state = []
    for i in range(pieces):
        first, last = i == 0, i == pieces - 1
        state = call(
            functools.partial(head_kernel, first, last, chunk, i * width_piece),
            [((channels + SUBLANES, rows), F32)]
            if last
            else [((channels, rows), F32), ((rows, LANES), F32), ((rows, LANES), F32)],
            [res_here[i * 2 // pieces], hidden, got[i], attn_gate, norm_scale, head_t] + list(state),
            flops=4 * rows * channels * width_piece,
            moved=6 * rows * width_piece,
        )
    sums = state[0]
    sums_got = lax.ppermute(sums, "shard", both)
    keep, send = call(
        functools.partial(norm_kernel, width_model),
        [((channels // 2, rows), F32)] * 2,
        [sums, sums_got, rows_own, rows_got],
        scratch=[pltpu.VMEM((channels, rows), F32)],
    )
    eps_got = lax.ppermute(send, "guide", both)
    fold = LANES // group
    frames = call(
        functools.partial(frame_kernel, seq_count, group),
        [((channels // fold, LANES), F32)] * seq_count,
        [chosen, keep, eps_got],
    )
    arrived = [frames[0]] + [
        lax.ppermute(frames[k], "seq", [(z, z ^ k) for z in range(seq_count)])
        for k in range(1, seq_count)
    ]
    out = call(
        functools.partial(final_kernel, seq_count, group),
        [((channels // 2, rows), F32)],
        [weight, noise[0, 0].T] + arrived,
    )[0]
    return out.T[None, None]


def fast_fits(sizes, queries, residual, w_out, w_head):
    seq_count = sizes["seq"]
    step_count, rows, width_local = queries.shape[1:]
    channels = w_head.shape[1]
    if seq_count < 2 or sizes["guide"] != 2 or sizes["shard"] != 2 or seq_count & (seq_count - 1) or step_count != 1 or rows != LANES:
        return False
    if width_local % (seq_count // 2 * HEAD_DIM) or residual.shape[3] % (4 * LANES):
        return False
    if w_out.shape[1] != residual.shape[3] or channels % (2 * SUBLANES):
        return False
    group = rows // seq_count
    if rows % seq_count or LANES % group:
        return False
    fold = LANES // group
    return channels // 2 % (fold * SUBLANES) == 0


def solution(mesh):
    sizes = dict(mesh.shape)

    def on_device(queries, key_vecs, value_vecs, residual, w_out, attn_gate, norm_shift, norm_scale, w_head, *rest):
        fits = fast_fits(sizes, queries, residual, w_out, w_head)
        plan = fast_plan if fits else general_plan
        return plan(queries, key_vecs, value_vecs, residual, w_out, attn_gate, norm_shift, norm_scale, w_head, *rest)

    return jax.shard_map(
        on_device,
        mesh=mesh,
        in_specs=(
            P("guide", "group", "seq", "shard"),
            P("guide", "group", "seq", "shard"),
            P("guide", "group", "seq", "shard"),
            P("guide", "group", "seq", "shard"),
            P("shard", "guide"),
            P("group", "shard"),
            P("group", "shard"),
            P("group", "shard"),
            P("shard", None),
            P("group", "seq", None, "guide"),
            P("group"),
            P("group", None),
        ),
        out_specs=P("group", "seq", None, "guide"),
        check_vma=False,
    )
```

```python
import functools

import jax
import jax.numpy as jnp
from jax import lax
from jax.experimental import pallas as pl
from jax.experimental.pallas import tpu as pltpu
from jax.sharding import PartitionSpec as P


HEAD_DIM = 128
LANES = 128
SUBLANES = 8
beta_low = 0.0001
beta_high = 0.02
guidance_scale = 3.0
norm_epsilon = 1e-06
LOG2E = 1.4426950408889634


F32 = jnp.float32
BF16 = jnp.bfloat16
VMEM_SPEC = pl.BlockSpec(memory_space=pltpu.VMEM)
SMEM_SPEC = pl.BlockSpec(memory_space=pltpu.SMEM)
HBM_SPEC = pl.BlockSpec(memory_space=pltpu.HBM)


def plan_weight(timesteps):
    steps_float = timesteps.astype(jnp.float32)
    exponent = (steps_float + 1.0) * beta_low + (beta_high - beta_low) * steps_float * (
        steps_float + 1.0
    ) / (2.0 * 999.0)
    return 1.0 - jnp.exp(-exponent)


def attend_all(query_split, keys_all, values_all):
    heads_local = query_split.shape[2]
    keys_split = keys_all.reshape(keys_all.shape[0], keys_all.shape[1], heads_local, HEAD_DIM)
    values_split = values_all.reshape(values_all.shape[0], values_all.shape[1], heads_local, HEAD_DIM)
    scores = jnp.einsum(
        "tqhd,tkhd->tqhk", query_split, keys_split, preferred_element_type=F32
    ) * HEAD_DIM ** (-0.5)
    expo = jnp.exp(scores - jnp.max(scores, axis=-1, keepdims=True))
    total = jnp.sum(expo, axis=-1)
    mixed = jnp.einsum("tqhk,tkhd->tqhd", expo.astype(BF16), values_split, preferred_element_type=F32)
    return (mixed / total[..., None]).astype(BF16)


def general_plan(
    queries, key_vecs, value_vecs, residual, w_out, attn_gate, norm_shift, norm_scale, w_head, noise,
    timesteps, frame_owner,
):
    query_local = queries[0]
    step_count, token_count, width_local = query_local.shape
    heads_local = width_local // HEAD_DIM
    attended = attend_all(
        query_local.reshape(step_count, token_count, heads_local, HEAD_DIM),
        lax.all_gather(key_vecs[0], "seq", axis=1, tiled=True),
        lax.all_gather(value_vecs[0], "seq", axis=1, tiled=True),
    )
    row_count = step_count * token_count
    both_rows = jnp.dot(
        lax.all_gather(attended.reshape(row_count, width_local), "guide", axis=0, tiled=True),
        w_out,
        preferred_element_type=F32,
    )
    half_width = w_out.shape[1]
    swapped = lax.all_to_all(
        both_rows.reshape(2, row_count, half_width), "guide", split_axis=0, concat_axis=2, tiled=True
    )
    projected = swapped.reshape(row_count, 2 * half_width)
    attn_out = lax.psum_scatter(projected, "shard", scatter_dimension=1, tiled=True)
    width_shard = attn_out.shape[1]
    width_model = width_shard * lax.axis_size("shard")
    hidden = residual[0].astype(F32) + attn_gate[:, None, :] * attn_out.reshape(
        step_count, token_count, width_shard
    )
    sum_first, sum_second = lax.psum((jnp.sum(hidden, axis=-1), jnp.sum(hidden * hidden, axis=-1)), "shard")
    mean_row = sum_first / width_model
    var_row = sum_second / width_model - mean_row * mean_row
    inv_std = lax.rsqrt(var_row + norm_epsilon)
    modulated = (hidden - mean_row[..., None]) * inv_std[..., None] * (
        1.0 + norm_scale[:, None, :]
    ) + norm_shift[:, None, :]
    partial_head = jnp.einsum(
        "tqd,dc->tqc", modulated, w_head.astype(F32), precision=lax.Precision.HIGHEST
    )
    predicted = lax.psum(partial_head, "shard")
    seq_count = lax.axis_size("seq")
    frame_group = token_count // seq_count
    frames_view = predicted.reshape(step_count, seq_count, frame_group, predicted.shape[-1])
    owner_table = (
        frame_owner[:, :, None] == jnp.arange(seq_count, dtype=jnp.int32)[None, None, :]
    ).astype(F32)
    by_owner = jnp.einsum("tfo,tfgc->togc", owner_table, frames_view, precision=lax.Precision.HIGHEST)
    arrived = lax.all_to_all(
        lax.all_to_all(by_owner[None], "seq", split_axis=2, concat_axis=3, tiled=True),
        "guide",
        split_axis=4,
        concat_axis=0,
        tiled=True,
    )
    guided = arrived[1] + guidance_scale * (arrived[0] - arrived[1])
    return plan_weight(timesteps)[:, None, None, None] * (guided - noise)


def pack_kernel(parts, half, count, *refs):
    source_refs, out_refs, sems = refs[:count], refs[count:-1], refs[-1]
    z = lax.axis_index("seq")
    copies = []
    for j in range(parts):
        cols = pl.ds(pl.multiple_of(lax.rem(z + j, parts) * half, LANES), half)
        for i in range(count):
            copies.append(
                pltpu.make_async_copy(source_refs[i].at[:, cols], out_refs[j].at[i], sems.at[j * count + i])
            )
    for copy in copies:
        copy.start()
    for copy in copies:
        copy.wait()


def split_kernel(source_ref, *refs):
    out_refs, sems = refs[:-1], refs[-1]
    width = out_refs[0].shape[1]
    copies = [
        pltpu.make_async_copy(source_ref.at[:, pl.ds(i * width, width)], out_ref, sems.at[i])
        for i, out_ref in enumerate(out_refs)
    ]
    for copy in copies:
        copy.start()
    for copy in copies:
        copy.wait()


def attend_kernel(parts, *refs):
    q_refs = refs[:parts]
    kv_refs = refs[parts : 3 * parts]
    o_refs = refs[3 * parts : 4 * parts]
    score_scr, total_scr = refs[4 * parts :]
    heads = q_refs[0].shape[2] // HEAD_DIM
    rows = q_refs[0].shape[1]
    for i in range(heads):
        cols = slice(i * HEAD_DIM, (i + 1) * HEAD_DIM)
        q = jnp.concatenate([r[0, :, cols] for r in q_refs], axis=0)
        for b, kv_ref in enumerate(kv_refs):
            scores = lax.dot_general(q, kv_ref[0, :, cols], (((1,), (1,)), ((), ())), preferred_element_type=F32)
            score_scr[i, :, b * rows : (b + 1) * rows] = scores * (HEAD_DIM ** (-0.5) * LOG2E)
    for i in range(heads):
        scores = score_scr[i]
        expo = jnp.exp2(scores - jnp.max(scores, axis=1, keepdims=True))
        score_scr[i] = expo
        total_scr[i] = jnp.broadcast_to(jnp.sum(expo, axis=1, keepdims=True), total_scr.shape[1:])
    for i in range(heads):
        cols = slice(i * HEAD_DIM, (i + 1) * HEAD_DIM)
        values = jnp.concatenate([r[1, :, cols] for r in kv_refs], axis=0)
        mixed = jnp.dot(score_scr[i].astype(BF16), values, preferred_element_type=F32) / total_scr[i]
        for j in range(parts):
            o_refs[j][:, cols] = mixed[j * rows : (j + 1) * rows].astype(BF16)


def project(parts, half, o_refs, w_ref, cols):
    z = lax.axis_index("seq")
    total = None
    for j in range(parts):
        start = pl.multiple_of(lax.rem(z + j, parts) * half, LANES)
        term = jnp.dot(o_refs[j][...], w_ref[pl.ds(start, half), cols], preferred_element_type=F32)
        total = term if total is None else total + term
    return total


def send_kernel(parts, half, chunk, first, *refs):
    o_refs = refs[:parts]
    near_ref, far_ref, out_ref = refs[parts:]
    guide = lax.axis_index("guide")
    for value, w_ref in ((1, near_ref), (0, far_ref)):

        @pl.when(guide == value)
        def _():
            for t in range(out_ref.shape[1] // chunk):
                cols = slice(first + t * chunk, first + (t + 1) * chunk)
                out_ref[:, t * chunk : (t + 1) * chunk] = project(parts, half, o_refs, w_ref, cols).astype(BF16)


def keep_kernel(parts, half, chunk, *refs):
    o_refs = refs[:parts]
    near_ref, far_ref, gate_ref, out_ref = refs[parts:]
    guide = lax.axis_index("guide")
    for value, w_ref in ((0, near_ref), (1, far_ref)):

        @pl.when(guide == value)
        def _():
            for t in range(out_ref.shape[1] // chunk):
                cols = slice(t * chunk, (t + 1) * chunk)
                out_ref[:, cols] = gate_ref[:, cols] * project(parts, half, o_refs, w_ref, cols)


def split_dot(head_t, rows):
    dims = (((1,), (1,)), ((), ()))
    high = rows.astype(BF16)
    low = (rows - high.astype(F32)).astype(BF16)
    return lax.dot_general(head_t, high, dims, preferred_element_type=F32) + lax.dot_general(
        head_t, low, dims, preferred_element_type=F32
    )


def early_kernel(
    seq_count, scale_hbm, shift_hbm, head_hbm, owner_ref, steps_ref, out_ref, chosen_ref, weight_ref,
    scale_ref, shift_ref, head_ref, sems,
):
    copies = [
        pltpu.make_async_copy(source, target, sems.at[i])
        for i, (source, target) in enumerate(
            ((scale_hbm, scale_ref), (shift_hbm, shift_ref), (head_hbm, head_ref))
        )
    ]
    for copy in copies:
        copy.start()
    z = lax.axis_index("seq")
    for k in range(seq_count):
        for f in range(seq_count):
            here = jnp.where(owner_ref[0, f] == lax.rem(z + k, seq_count), 1.0, 0.0)
            chosen_ref[k * seq_count + f : k * seq_count + f + 1, :] = jnp.full((1, LANES), here, F32)
    weight_ref[...] = plan_weight(jnp.full((SUBLANES, LANES), steps_ref[0], jnp.int32))
    for copy in copies:
        copy.wait()
    width = scale_ref.shape[1]
    which = lax.broadcasted_iota(jnp.int32, (LANES, width), 0)
    rows = jnp.where(which == 0, 1.0 + scale_ref[...], shift_ref[...])
    high = rows.astype(BF16)
    rest = rows - high.astype(F32)
    mid = rest.astype(BF16)
    low = (rest - mid.astype(F32)).astype(BF16)
    dims = (((1,), (1,)), ((), ()))
    total = None
    for part in (high, mid, low):
        term = lax.dot_general(head_ref[...], part, dims, preferred_element_type=F32)
        total = term if total is None else total + term
    out_ref[...] = total


def head_kernel(first, last, chunk, start, *refs):
    res_ref, hid_ref, got_ref, gate_ref, scale_ref, head_ref = refs[:6]
    if first:
        out_refs = refs[6:]
    else:
        prev_refs, out_refs = refs[6:9], refs[9:]
    channels = head_ref.shape[0]
    rows = hid_ref.shape[0]
    acc_one = jnp.zeros((rows, LANES), F32) if first else prev_refs[1][...]
    acc_two = jnp.zeros((rows, LANES), F32) if first else prev_refs[2][...]
    acc_head = jnp.zeros((channels, rows), F32) if first else prev_refs[0][...]
    for t in range(got_ref.shape[1] // chunk):
        cols = slice(start + t * chunk, start + (t + 1) * chunk)
        arrived = got_ref[:, t * chunk : (t + 1) * chunk].astype(F32)
        here = slice(cols.start % res_ref.shape[1], cols.start % res_ref.shape[1] + chunk)
        hidden = res_ref[:, here].astype(F32) + hid_ref[:, cols] + gate_ref[:, cols] * arrived
        for s in range(chunk // LANES):
            piece = hidden[:, s * LANES : (s + 1) * LANES]
            acc_one = acc_one + piece
            acc_two = acc_two + piece * piece
        acc_head = acc_head + split_dot(head_ref[:, cols], hidden * (1.0 + scale_ref[:, cols]))
    if last:
        out_ref = out_refs[0]
        out_ref[0:channels, :] = acc_head
        sum_one = jnp.sum(acc_one.T, axis=0, keepdims=True)
        sum_two = jnp.sum(acc_two.T, axis=0, keepdims=True)
        row = lax.broadcasted_iota(jnp.int32, (SUBLANES, rows), 0)
        out_ref[channels : channels + SUBLANES, :] = jnp.where(row == 0, sum_one, sum_two)
    else:
        out_refs[0][...] = acc_head
        out_refs[1][...] = acc_one
        out_refs[2][...] = acc_two


def norm_kernel(width_model, own_ref, got_ref, rows_own_ref, rows_got_ref, keep_ref, send_ref, eps_scr):
    channels = rows_own_ref.shape[0]
    half_channels = channels // 2
    guide = lax.axis_index("guide")
    head = own_ref[0:channels, :] + got_ref[0:channels, :]
    stats = own_ref[channels : channels + SUBLANES, :] + got_ref[channels : channels + SUBLANES, :]
    mean = stats[0:1] / width_model
    var = stats[1:2] / width_model - mean * mean
    inv_std = lax.rsqrt(var + norm_epsilon)
    scaled = rows_own_ref[:, 0:1] + rows_got_ref[:, 0:1]
    shifted = rows_own_ref[:, 1:2] + rows_got_ref[:, 1:2]
    eps_scr[...] = (head - mean * scaled) * inv_std + shifted
    keep_ref[...] = eps_scr[pl.ds(pl.multiple_of(guide * half_channels, SUBLANES), half_channels), :]
    send_ref[...] = eps_scr[pl.ds(pl.multiple_of((1 - guide) * half_channels, SUBLANES), half_channels), :]


def frame_kernel(seq_count, group, chosen_ref, keep_ref, got_ref, *out_refs):
    first = lax.axis_index("guide") == 0
    mine, other = keep_ref[...], got_ref[...]
    fold = LANES // group
    rows = mine.shape[0] // fold
    lane = lax.broadcasted_iota(jnp.int32, (rows, LANES), 1) // group
    for sub, block in enumerate((jnp.where(first, mine, other), jnp.where(first, other, mine))):
        packed = []
        for f in range(seq_count):
            frame = jnp.zeros((rows, LANES), F32)
            for j in range(fold):
                piece = block[j * rows : (j + 1) * rows]
                shift = (j - f) * group % LANES
                frame = jnp.where(lane == j, pltpu.roll(piece, shift, axis=1) if shift else piece, frame)
            packed.append(frame)
        for k in range(seq_count):
            frame = packed[0]
            for f in range(1, seq_count):
                frame = jnp.where(chosen_ref[k * seq_count + f : k * seq_count + f + 1, :] > 0.5, packed[f], frame)
            out_refs[k][sub * rows : (sub + 1) * rows, :] = frame


def final_kernel(seq_count, group, weight_ref, noise_ref, *refs):
    piece_refs, out_ref = refs[:seq_count], refs[seq_count]
    z = lax.axis_index("seq")
    parts = seq_count // 2
    fold = LANES // group
    rows = piece_refs[0].shape[0] // 2
    lane = lax.broadcasted_iota(jnp.int32, (rows, LANES), 1) // group
    for j in range(fold):
        eps_cond = jnp.zeros((rows, LANES), F32)
        eps_free = jnp.zeros((rows, LANES), F32)
        for k in range(seq_count):
            source = lax.rem(z - k + seq_count, seq_count)
            branch, position = source // parts, lax.rem(source, parts)
            for sub in range(2):
                block = parts * sub + position
                shift = lax.rem((block - j) * group + LANES, LANES)
                rolled = pltpu.roll(piece_refs[k][sub * rows : (sub + 1) * rows], shift, axis=1)
                eps_cond = jnp.where((lane == block) & (branch == 0), rolled, eps_cond)
                eps_free = jnp.where((lane == block) & (branch == 1), rolled, eps_free)
        part = slice(j * rows, (j + 1) * rows)
        guided = eps_free + guidance_scale * (eps_cond - eps_free)
        out_ref[part, :] = weight_ref[0:1, :] * (guided - noise_ref[part, :])


def call(kernel, outs, args, specs=None, scratch=(), flops=0, moved=0, grant=16):
    shapes = [jax.ShapeDtypeStruct(s, d) for s, d in outs]
    return pl.pallas_call(
        kernel,
        out_shape=shapes,
        in_specs=specs or [VMEM_SPEC] * len(args),
        out_specs=[VMEM_SPEC] * len(outs),
        scratch_shapes=list(scratch),
        compiler_params=pltpu.CompilerParams(vmem_limit_bytes=grant << 20),
        cost_estimate=pl.CostEstimate(flops=flops, bytes_accessed=moved, transcendentals=0),
    )(*args)


def in_hbm(array):
    return pltpu.with_memory_space_constraint(array, pltpu.HBM)


def fast_plan(
    queries, key_vecs, value_vecs, residual, w_out, attn_gate, norm_shift, norm_scale, w_head, noise,
    timesteps, frame_owner,
):
    seq_count = lax.axis_size("seq")
    parts = seq_count // 2
    rows, width_local = queries.shape[2:]
    half = width_local // parts
    width_shard = residual.shape[3]
    channels = w_head.shape[1]
    group = rows // seq_count
    width_model = float(width_shard * lax.axis_size("shard"))
    both = [(0, 1), (1, 0)]
    axes = ("seq", "guide")

    crossed = [(x * 2 + c, x * 2 + (c + x) % 2) for x in range(2) for c in range(2)]
    straight = [(x * 2 + c, x * 2 + (c + x + 1) % 2) for x in range(2) for c in range(2)]

    def pack(*arrays):
        return call(
            functools.partial(pack_kernel, parts, half, len(arrays)),
            [((len(arrays), rows, half), BF16)] * parts,
            [in_hbm(array[0, 0]) for array in arrays],
            [HBM_SPEC] * len(arrays),
            [pltpu.SemaphoreType.DMA((parts * len(arrays),))],
            moved=4 * len(arrays) * rows * width_local,
        )

    kv_sent = pack(key_vecs, value_vecs)
    there = [
        [
            (z * 2 + c, (parts * c + (z + j) % parts) * 2 + z // parts)
            for z in range(seq_count)
            for c in range(2)
        ]
        for j in range(parts)
    ]
    inside = [[(z, z // parts * parts + (z - j) % parts) for z in range(seq_count)] for j in range(parts)]
    kv_own = [lax.ppermute(kv_sent[j], axes, there[j]) for j in range(parts)]
    q_sent = pack(queries)
    q_own = [lax.ppermute(q_sent[j], axes, there[j]) for j in range(parts)]
    near_w = lax.ppermute(w_out, ("shard", "guide"), crossed)
    far_w = lax.ppermute(w_out, ("shard", "guide"), straight)
    kv_other = [lax.ppermute(block, "guide", both) for block in kv_own]
    res_sent = call(
        split_kernel,
        [((rows, width_shard // 2), BF16)] * 2,
        [in_hbm(residual[0, 0])],
        [HBM_SPEC],
        [pltpu.SemaphoreType.DMA((2,))],
        moved=4 * rows * width_shard,
    )
    res_here = [lax.ppermute(block, axes, there[0]) for block in res_sent]

    head_t = w_head.T
    rows_own, chosen, weight = call(
        functools.partial(early_kernel, seq_count),
        [((channels, LANES), F32), ((seq_count * seq_count, LANES), F32), ((SUBLANES, LANES), F32)],
        [in_hbm(norm_scale), in_hbm(norm_shift), in_hbm(head_t), frame_owner, timesteps],
        [HBM_SPEC] * 3 + [SMEM_SPEC] * 2,
        [
            pltpu.VMEM(norm_scale.shape, F32),
            pltpu.VMEM(norm_shift.shape, F32),
            pltpu.VMEM(head_t.shape, BF16),
            pltpu.SemaphoreType.DMA((3,)),
        ],
        moved=4 * width_shard * LANES,
    )
    rows_got = lax.ppermute(rows_own, "shard", both)
    *q_own, rows_own = lax.optimization_barrier((*q_own, rows_own))

    mixed = call(
        functools.partial(attend_kernel, parts),
        [((rows, half), BF16)] * parts,
        q_own + kv_own + kv_other,
        scratch=[
            pltpu.VMEM((half // HEAD_DIM, rows * parts, 2 * parts * rows), F32),
            pltpu.VMEM((half // HEAD_DIM, rows * parts, HEAD_DIM), F32),
        ],
        flops=8 * rows * parts * rows * parts * half,
        moved=2 * rows * half * parts * 6,
    )
    mixed = [mixed[0]] + [lax.ppermute(mixed[j], "seq", inside[j]) for j in range(1, parts)]

    chunk = 128
    pieces = 4
    width_piece = width_shard // pieces
    got = []
    for i in range(pieces):
        partial = call(
            functools.partial(send_kernel, parts, half, chunk, i * width_piece),
            [((rows, width_piece), BF16)],
            mixed + [near_w, far_w],
            flops=2 * rows * width_local * width_piece,
            moved=2 * width_local * width_piece,
        )[0]
        got.append(lax.ppermute(partial, "shard", both))
    hidden = call(
        functools.partial(keep_kernel, parts, half, chunk),
        [((rows, width_shard), F32)],
        mixed + [near_w, far_w, attn_gate],
        flops=2 * rows * width_local * width_shard,
        moved=2 * width_local * width_shard,
    )[0]
    state = []
    for i in range(pieces):
        first, last = i == 0, i == pieces - 1
        state = call(
            functools.partial(head_kernel, first, last, chunk, i * width_piece),
            [((channels + SUBLANES, rows), F32)]
            if last
            else [((channels, rows), F32), ((rows, LANES), F32), ((rows, LANES), F32)],
            [res_here[i * 2 // pieces], hidden, got[i], attn_gate, norm_scale, head_t] + list(state),
            flops=4 * rows * channels * width_piece,
            moved=6 * rows * width_piece,
        )
    sums = state[0]
    sums_got = lax.ppermute(sums, "shard", both)
    keep, send = call(
        functools.partial(norm_kernel, width_model),
        [((channels // 2, rows), F32)] * 2,
        [sums, sums_got, rows_own, rows_got],
        scratch=[pltpu.VMEM((channels, rows), F32)],
    )
    eps_got = lax.ppermute(send, "guide", both)
    fold = LANES // group
    frames = call(
        functools.partial(frame_kernel, seq_count, group),
        [((channels // fold, LANES), F32)] * seq_count,
        [chosen, keep, eps_got],
    )
    arrived = [frames[0]] + [
        lax.ppermute(frames[k], "seq", [(z, (z + k) % seq_count) for z in range(seq_count)])
        for k in range(1, seq_count)
    ]
    out = call(
        functools.partial(final_kernel, seq_count, group),
        [((channels // 2, rows), F32)],
        [weight, noise[0, 0].T] + arrived,
    )[0]
    return out.T[None, None]


def fast_fits(sizes, queries, residual, w_out, w_head):
    seq_count = sizes["seq"]
    step_count, rows, width_local = queries.shape[1:]
    channels = w_head.shape[1]
    if seq_count < 2 or sizes["guide"] != 2 or sizes["shard"] != 2 or seq_count & (seq_count - 1) or step_count != 1 or rows != LANES:
        return False
    if width_local % (seq_count // 2 * HEAD_DIM) or residual.shape[3] % (4 * LANES):
        return False
    if w_out.shape[1] != residual.shape[3] or channels % (2 * SUBLANES):
        return False
    group = rows // seq_count
    if rows % seq_count or LANES % group:
        return False
    fold = LANES // group
    return channels // 2 % (fold * SUBLANES) == 0


def solution(mesh):
    sizes = dict(mesh.shape)

    def on_device(queries, key_vecs, value_vecs, residual, w_out, attn_gate, norm_shift, norm_scale, w_head, *rest):
        fits = fast_fits(sizes, queries, residual, w_out, w_head)
        plan = fast_plan if fits else general_plan
        return plan(queries, key_vecs, value_vecs, residual, w_out, attn_gate, norm_shift, norm_scale, w_head, *rest)

    return jax.shard_map(
        on_device,
        mesh=mesh,
        in_specs=(
            P("guide", "group", "seq", "shard"),
            P("guide", "group", "seq", "shard"),
            P("guide", "group", "seq", "shard"),
            P("guide", "group", "seq", "shard"),
            P("shard", "guide"),
            P("group", "shard"),
            P("group", "shard"),
            P("group", "shard"),
            P("shard", None),
            P("group", "seq", None, "guide"),
            P("group"),
            P("group", None),
        ),
        out_specs=P("group", "seq", None, "guide"),
        check_vma=False,
    )
```

```python
import functools

import jax
import jax.numpy as jnp
from jax import lax
from jax.experimental import pallas as pl
from jax.experimental.pallas import tpu as pltpu
from jax.sharding import PartitionSpec as P


HEAD_DIM = 128
LANES = 128
SUBLANES = 8
beta_low = 0.0001
beta_high = 0.02
guidance_scale = 3.0
norm_epsilon = 1e-06
LOG2E = 1.4426950408889634


F32 = jnp.float32
BF16 = jnp.bfloat16
VMEM_SPEC = pl.BlockSpec(memory_space=pltpu.VMEM)
SMEM_SPEC = pl.BlockSpec(memory_space=pltpu.SMEM)
HBM_SPEC = pl.BlockSpec(memory_space=pltpu.HBM)


def plan_weight(timesteps):
    steps_float = timesteps.astype(jnp.float32)
    exponent = (steps_float + 1.0) * beta_low + (beta_high - beta_low) * steps_float * (
        steps_float + 1.0
    ) / (2.0 * 999.0)
    return 1.0 - jnp.exp(-exponent)


def attend_all(query_split, keys_all, values_all):
    heads_local = query_split.shape[2]
    keys_split = keys_all.reshape(keys_all.shape[0], keys_all.shape[1], heads_local, HEAD_DIM)
    values_split = values_all.reshape(values_all.shape[0], values_all.shape[1], heads_local, HEAD_DIM)
    scores = jnp.einsum(
        "tqhd,tkhd->tqhk", query_split, keys_split, preferred_element_type=F32
    ) * HEAD_DIM ** (-0.5)
    expo = jnp.exp(scores - jnp.max(scores, axis=-1, keepdims=True))
    total = jnp.sum(expo, axis=-1)
    mixed = jnp.einsum("tqhk,tkhd->tqhd", expo.astype(BF16), values_split, preferred_element_type=F32)
    return (mixed / total[..., None]).astype(BF16)


def general_plan(
    queries, key_vecs, value_vecs, residual, w_out, attn_gate, norm_shift, norm_scale, w_head, noise,
    timesteps, frame_owner,
):
    query_local = queries[0]
    step_count, token_count, width_local = query_local.shape
    heads_local = width_local // HEAD_DIM
    attended = attend_all(
        query_local.reshape(step_count, token_count, heads_local, HEAD_DIM),
        lax.all_gather(key_vecs[0], "seq", axis=1, tiled=True),
        lax.all_gather(value_vecs[0], "seq", axis=1, tiled=True),
    )
    row_count = step_count * token_count
    both_rows = jnp.dot(
        lax.all_gather(attended.reshape(row_count, width_local), "guide", axis=0, tiled=True),
        w_out,
        preferred_element_type=F32,
    )
    half_width = w_out.shape[1]
    swapped = lax.all_to_all(
        both_rows.reshape(2, row_count, half_width), "guide", split_axis=0, concat_axis=2, tiled=True
    )
    projected = swapped.reshape(row_count, 2 * half_width)
    attn_out = lax.psum_scatter(projected, "shard", scatter_dimension=1, tiled=True)
    width_shard = attn_out.shape[1]
    width_model = width_shard * lax.axis_size("shard")
    hidden = residual[0].astype(F32) + attn_gate[:, None, :] * attn_out.reshape(
        step_count, token_count, width_shard
    )
    sum_first, sum_second = lax.psum((jnp.sum(hidden, axis=-1), jnp.sum(hidden * hidden, axis=-1)), "shard")
    mean_row = sum_first / width_model
    var_row = sum_second / width_model - mean_row * mean_row
    inv_std = lax.rsqrt(var_row + norm_epsilon)
    modulated = (hidden - mean_row[..., None]) * inv_std[..., None] * (
        1.0 + norm_scale[:, None, :]
    ) + norm_shift[:, None, :]
    partial_head = jnp.einsum(
        "tqd,dc->tqc", modulated, w_head.astype(F32), precision=lax.Precision.HIGHEST
    )
    predicted = lax.psum(partial_head, "shard")
    seq_count = lax.axis_size("seq")
    frame_group = token_count // seq_count
    frames_view = predicted.reshape(step_count, seq_count, frame_group, predicted.shape[-1])
    owner_table = (
        frame_owner[:, :, None] == jnp.arange(seq_count, dtype=jnp.int32)[None, None, :]
    ).astype(F32)
    by_owner = jnp.einsum("tfo,tfgc->togc", owner_table, frames_view, precision=lax.Precision.HIGHEST)
    arrived = lax.all_to_all(
        lax.all_to_all(by_owner[None], "seq", split_axis=2, concat_axis=3, tiled=True),
        "guide",
        split_axis=4,
        concat_axis=0,
        tiled=True,
    )
    guided = arrived[1] + guidance_scale * (arrived[0] - arrived[1])
    return plan_weight(timesteps)[:, None, None, None] * (guided - noise)


def pack_kernel(parts, half, count, *refs):
    source_refs, out_refs, sems = refs[:count], refs[count:-1], refs[-1]
    z = lax.axis_index("seq")
    copies = []
    for j in range(parts):
        cols = pl.ds(pl.multiple_of(lax.rem(z + j, parts) * half, LANES), half)
        for i in range(count):
            copies.append(
                pltpu.make_async_copy(source_refs[i].at[:, cols], out_refs[j].at[i], sems.at[j * count + i])
            )
    for copy in copies:
        copy.start()
    for copy in copies:
        copy.wait()


def split_kernel(source_ref, *refs):
    out_refs, sems = refs[:-1], refs[-1]
    copies, start = [], 0
    for i, out_ref in enumerate(out_refs):
        width = out_ref.shape[1]
        copies.append(pltpu.make_async_copy(source_ref.at[:, pl.ds(start, width)], out_ref, sems.at[i]))
        copies[-1].start()
        start += width
    for copy in copies:
        copy.wait()


def attend_kernel(parts, *refs):
    q_refs = refs[:parts]
    kv_refs = refs[parts : 3 * parts]
    o_refs = refs[3 * parts : 4 * parts]
    score_scr, total_scr = refs[4 * parts :]
    heads = q_refs[0].shape[2] // HEAD_DIM
    rows = q_refs[0].shape[1]
    for i in range(heads):
        cols = slice(i * HEAD_DIM, (i + 1) * HEAD_DIM)
        q = jnp.concatenate([r[0, :, cols] for r in q_refs], axis=0)
        for b, kv_ref in enumerate(kv_refs):
            scores = lax.dot_general(q, kv_ref[0, :, cols], (((1,), (1,)), ((), ())), preferred_element_type=F32)
            score_scr[i, :, b * rows : (b + 1) * rows] = scores * (HEAD_DIM ** (-0.5) * LOG2E)
    for i in range(heads):
        scores = score_scr[i]
        expo = jnp.exp2(scores - jnp.max(scores, axis=1, keepdims=True))
        score_scr[i] = expo
        total_scr[i] = jnp.broadcast_to(jnp.sum(expo, axis=1, keepdims=True), total_scr.shape[1:])
    for i in range(heads):
        cols = slice(i * HEAD_DIM, (i + 1) * HEAD_DIM)
        values = jnp.concatenate([r[1, :, cols] for r in kv_refs], axis=0)
        mixed = jnp.dot(score_scr[i].astype(BF16), values, preferred_element_type=F32) / total_scr[i]
        for j in range(parts):
            o_refs[j][:, cols] = mixed[j * rows : (j + 1) * rows].astype(BF16)


def project(parts, half, o_refs, w_ref, cols):
    z = lax.axis_index("seq")
    total = None
    for j in range(parts):
        start = pl.multiple_of(lax.rem(z + j, parts) * half, LANES)
        term = jnp.dot(o_refs[j][...], w_ref[pl.ds(start, half), cols], preferred_element_type=F32)
        total = term if total is None else total + term
    return total


def send_kernel(parts, half, chunk, first, *refs):
    o_refs = refs[:parts]
    near_ref, far_ref, out_ref = refs[parts:]
    guide = lax.axis_index("guide")
    for value, w_ref in ((1, near_ref), (0, far_ref)):

        @pl.when(guide == value)
        def _():
            for t in range(out_ref.shape[1] // chunk):
                cols = slice(first + t * chunk, first + (t + 1) * chunk)
                out_ref[:, t * chunk : (t + 1) * chunk] = project(parts, half, o_refs, w_ref, cols).astype(BF16)


def keep_kernel(parts, half, chunk, *refs):
    o_refs = refs[:parts]
    near_ref, far_ref, gate_ref, out_ref = refs[parts:]
    guide = lax.axis_index("guide")
    for value, w_ref in ((0, near_ref), (1, far_ref)):

        @pl.when(guide == value)
        def _():
            for t in range(out_ref.shape[1] // chunk):
                cols = slice(t * chunk, (t + 1) * chunk)
                out_ref[:, cols] = gate_ref[:, cols] * project(parts, half, o_refs, w_ref, cols)


def split_dot(head_t, rows):
    dims = (((1,), (1,)), ((), ()))
    high = rows.astype(BF16)
    low = (rows - high.astype(F32)).astype(BF16)
    return lax.dot_general(head_t, high, dims, preferred_element_type=F32) + lax.dot_general(
        head_t, low, dims, preferred_element_type=F32
    )


def early_kernel(
    seq_count, scale_hbm, shift_hbm, head_hbm, owner_ref, steps_ref, out_ref, chosen_ref, weight_ref,
    scale_ref, shift_ref, head_ref, sems,
):
    copies = [
        pltpu.make_async_copy(source, target, sems.at[i])
        for i, (source, target) in enumerate(
            ((scale_hbm, scale_ref), (shift_hbm, shift_ref), (head_hbm, head_ref))
        )
    ]
    for copy in copies:
        copy.start()
    z = lax.axis_index("seq")
    for k in range(seq_count):
        for f in range(seq_count):
            here = jnp.where(owner_ref[0, f] == z ^ k, 1.0, 0.0)
            chosen_ref[k * seq_count + f : k * seq_count + f + 1, :] = jnp.full((1, LANES), here, F32)
    weight_ref[...] = plan_weight(jnp.full((SUBLANES, LANES), steps_ref[0], jnp.int32))
    for copy in copies:
        copy.wait()
    width = scale_ref.shape[1]
    which = lax.broadcasted_iota(jnp.int32, (LANES, width), 0)
    rows = jnp.where(which == 0, 1.0 + scale_ref[...], shift_ref[...])
    high = rows.astype(BF16)
    rest = rows - high.astype(F32)
    mid = rest.astype(BF16)
    low = (rest - mid.astype(F32)).astype(BF16)
    dims = (((1,), (1,)), ((), ()))
    total = None
    for part in (high, mid, low):
        term = lax.dot_general(head_ref[...], part, dims, preferred_element_type=F32)
        total = term if total is None else total + term
    out_ref[...] = total


def head_kernel(first, last, chunk, start, *refs):
    res_ref, hid_ref, got_ref, gate_ref, scale_ref, head_ref = refs[:6]
    if first:
        out_refs = refs[6:]
    else:
        prev_refs, out_refs = refs[6:9], refs[9:]
    channels = head_ref.shape[0]
    rows = hid_ref.shape[0]
    acc_one = jnp.zeros((rows, LANES), F32) if first else prev_refs[1][...]
    acc_two = jnp.zeros((rows, LANES), F32) if first else prev_refs[2][...]
    acc_head = jnp.zeros((channels, rows), F32) if first else prev_refs[0][...]
    for t in range(got_ref.shape[1] // chunk):
        cols = slice(start + t * chunk, start + (t + 1) * chunk)
        arrived = got_ref[:, t * chunk : (t + 1) * chunk].astype(F32)
        offset = cols.start - (hid_ref.shape[1] - res_ref.shape[1] if start else 0)
        here = slice(offset, offset + chunk)
        hidden = res_ref[:, here].astype(F32) + hid_ref[:, cols] + gate_ref[:, cols] * arrived
        for s in range(chunk // LANES):
            piece = hidden[:, s * LANES : (s + 1) * LANES]
            acc_one = acc_one + piece
            acc_two = acc_two + piece * piece
        acc_head = acc_head + split_dot(head_ref[:, cols], hidden * (1.0 + scale_ref[:, cols]))
    if last:
        out_ref = out_refs[0]
        out_ref[0:channels, :] = acc_head
        sum_one = jnp.sum(acc_one.T, axis=0, keepdims=True)
        sum_two = jnp.sum(acc_two.T, axis=0, keepdims=True)
        row = lax.broadcasted_iota(jnp.int32, (SUBLANES, rows), 0)
        out_ref[channels : channels + SUBLANES, :] = jnp.where(row == 0, sum_one, sum_two)
    else:
        out_refs[0][...] = acc_head
        out_refs[1][...] = acc_one
        out_refs[2][...] = acc_two


def norm_kernel(width_model, own_ref, got_ref, rows_own_ref, rows_got_ref, keep_ref, send_ref, eps_scr):
    channels = rows_own_ref.shape[0]
    half_channels = channels // 2
    guide = lax.axis_index("guide")
    head = own_ref[0:channels, :] + got_ref[0:channels, :]
    stats = own_ref[channels : channels + SUBLANES, :] + got_ref[channels : channels + SUBLANES, :]
    mean = stats[0:1] / width_model
    var = stats[1:2] / width_model - mean * mean
    inv_std = lax.rsqrt(var + norm_epsilon)
    scaled = rows_own_ref[:, 0:1] + rows_got_ref[:, 0:1]
    shifted = rows_own_ref[:, 1:2] + rows_got_ref[:, 1:2]
    eps_scr[...] = (head - mean * scaled) * inv_std + shifted
    keep_ref[...] = eps_scr[pl.ds(pl.multiple_of(guide * half_channels, SUBLANES), half_channels), :]
    send_ref[...] = eps_scr[pl.ds(pl.multiple_of((1 - guide) * half_channels, SUBLANES), half_channels), :]


def frame_kernel(seq_count, group, chosen_ref, keep_ref, got_ref, *out_refs):
    first = lax.axis_index("guide") == 0
    mine, other = keep_ref[...], got_ref[...]
    fold = LANES // group
    rows = mine.shape[0] // fold
    lane = lax.broadcasted_iota(jnp.int32, (rows, LANES), 1) // group
    for sub, block in enumerate((jnp.where(first, mine, other), jnp.where(first, other, mine))):
        packed = []
        for f in range(seq_count):
            frame = jnp.zeros((rows, LANES), F32)
            for j in range(fold):
                piece = block[j * rows : (j + 1) * rows]
                shift = (j - f) * group % LANES
                frame = jnp.where(lane == j, pltpu.roll(piece, shift, axis=1) if shift else piece, frame)
            packed.append(frame)
        for k in range(seq_count):
            frame = packed[0]
            for f in range(1, seq_count):
                frame = jnp.where(chosen_ref[k * seq_count + f : k * seq_count + f + 1, :] > 0.5, packed[f], frame)
            out_refs[k][sub * rows : (sub + 1) * rows, :] = frame


def final_kernel(seq_count, group, weight_ref, noise_ref, *refs):
    piece_refs, out_ref = refs[:seq_count], refs[seq_count]
    z = lax.axis_index("seq")
    parts = seq_count // 2
    fold = LANES // group
    rows = piece_refs[0].shape[0] // 2
    lane = lax.broadcasted_iota(jnp.int32, (rows, LANES), 1) // group
    for j in range(fold):
        eps_cond = jnp.zeros((rows, LANES), F32)
        eps_free = jnp.zeros((rows, LANES), F32)
        for k in range(seq_count):
            source = z ^ k
            branch, position = source // parts, lax.rem(source, parts)
            for sub in range(2):
                block = parts * sub + position
                shift = lax.rem((block - j) * group + LANES, LANES)
                rolled = pltpu.roll(piece_refs[k][sub * rows : (sub + 1) * rows], shift, axis=1)
                eps_cond = jnp.where((lane == block) & (branch == 0), rolled, eps_cond)
                eps_free = jnp.where((lane == block) & (branch == 1), rolled, eps_free)
        part = slice(j * rows, (j + 1) * rows)
        guided = eps_free + guidance_scale * (eps_cond - eps_free)
        out_ref[part, :] = weight_ref[0:1, :] * (guided - noise_ref[part, :])


def call(kernel, outs, args, specs=None, scratch=(), flops=0, moved=0, grant=16):
    shapes = [jax.ShapeDtypeStruct(s, d) for s, d in outs]
    return pl.pallas_call(
        kernel,
        out_shape=shapes,
        in_specs=specs or [VMEM_SPEC] * len(args),
        out_specs=[VMEM_SPEC] * len(outs),
        scratch_shapes=list(scratch),
        compiler_params=pltpu.CompilerParams(vmem_limit_bytes=grant << 20),
        cost_estimate=pl.CostEstimate(flops=flops, bytes_accessed=moved, transcendentals=0),
    )(*args)


def in_hbm(array):
    return pltpu.with_memory_space_constraint(array, pltpu.HBM)


def fast_plan(
    queries, key_vecs, value_vecs, residual, w_out, attn_gate, norm_shift, norm_scale, w_head, noise,
    timesteps, frame_owner,
):
    seq_count = lax.axis_size("seq")
    parts = seq_count // 2
    rows, width_local = queries.shape[2:]
    half = width_local // parts
    width_shard = residual.shape[3]
    channels = w_head.shape[1]
    group = rows // seq_count
    width_model = float(width_shard * lax.axis_size("shard"))
    both = [(0, 1), (1, 0)]
    axes = ("seq", "guide")

    crossed = [(x * 2 + c, x * 2 + (c + x) % 2) for x in range(2) for c in range(2)]
    straight = [(x * 2 + c, x * 2 + (c + x + 1) % 2) for x in range(2) for c in range(2)]

    def pack(*arrays):
        return call(
            functools.partial(pack_kernel, parts, half, len(arrays)),
            [((len(arrays), rows, half), BF16)] * parts,
            [in_hbm(array[0, 0]) for array in arrays],
            [HBM_SPEC] * len(arrays),
            [pltpu.SemaphoreType.DMA((parts * len(arrays),))],
            moved=4 * len(arrays) * rows * width_local,
        )

    kv_sent = pack(key_vecs, value_vecs)
    there = [
        [
            (z * 2 + c, (parts * c + (z + j) % parts) * 2 + z // parts)
            for z in range(seq_count)
            for c in range(2)
        ]
        for j in range(parts)
    ]
    inside = [[(z, z // parts * parts + (z - j) % parts) for z in range(seq_count)] for j in range(parts)]
    kv_own = [lax.ppermute(kv_sent[j], axes, there[j]) for j in range(parts)]
    q_sent = pack(queries)
    q_own = [lax.ppermute(q_sent[j], axes, there[j]) for j in range(parts)]
    near_w = lax.ppermute(w_out, ("shard", "guide"), crossed)
    far_w = lax.ppermute(w_out, ("shard", "guide"), straight)
    kv_other = [lax.ppermute(block, "guide", both) for block in kv_own]
    res_sent = call(
        split_kernel,
        [((rows, width_shard // 4), BF16), ((rows, width_shard - width_shard // 4), BF16)],
        [in_hbm(residual[0, 0])],
        [HBM_SPEC],
        [pltpu.SemaphoreType.DMA((2,))],
        moved=4 * rows * width_shard,
    )
    res_here = [lax.ppermute(block, axes, there[0]) for block in res_sent]

    head_t = w_head.T
    rows_own, chosen, weight = call(
        functools.partial(early_kernel, seq_count),
        [((channels, LANES), F32), ((seq_count * seq_count, LANES), F32), ((SUBLANES, LANES), F32)],
        [in_hbm(norm_scale), in_hbm(norm_shift), in_hbm(head_t), frame_owner, timesteps],
        [HBM_SPEC] * 3 + [SMEM_SPEC] * 2,
        [
            pltpu.VMEM(norm_scale.shape, F32),
            pltpu.VMEM(norm_shift.shape, F32),
            pltpu.VMEM(head_t.shape, BF16),
            pltpu.SemaphoreType.DMA((3,)),
        ],
        moved=4 * width_shard * LANES,
    )
    rows_got = lax.ppermute(rows_own, "shard", both)
    *q_own, rows_own = lax.optimization_barrier((*q_own, rows_own))

    mixed = call(
        functools.partial(attend_kernel, parts),
        [((rows, half), BF16)] * parts,
        q_own + kv_own + kv_other,
        scratch=[
            pltpu.VMEM((half // HEAD_DIM, rows * parts, 2 * parts * rows), F32),
            pltpu.VMEM((half // HEAD_DIM, rows * parts, HEAD_DIM), F32),
        ],
        flops=8 * rows * parts * rows * parts * half,
        moved=2 * rows * half * parts * 6,
    )
    mixed = [mixed[0]] + [lax.ppermute(mixed[j], "seq", inside[j]) for j in range(1, parts)]

    chunk = 128
    pieces = 4
    width_piece = width_shard // pieces
    got = []
    for i in range(pieces):
        partial = call(
            functools.partial(send_kernel, parts, half, chunk, i * width_piece),
            [((rows, width_piece), BF16)],
            mixed + [near_w, far_w],
            flops=2 * rows * width_local * width_piece,
            moved=2 * width_local * width_piece,
        )[0]
        got.append(lax.ppermute(partial, "shard", both))
    hidden = call(
        functools.partial(keep_kernel, parts, half, chunk),
        [((rows, width_shard), F32)],
        mixed + [near_w, far_w, attn_gate],
        flops=2 * rows * width_local * width_shard,
        moved=2 * width_local * width_shard,
    )[0]
    state = []
    for i in range(pieces):
        first, last = i == 0, i == pieces - 1
        state = call(
            functools.partial(head_kernel, first, last, chunk, i * width_piece),
            [((channels + SUBLANES, rows), F32)]
            if last
            else [((channels, rows), F32), ((rows, LANES), F32), ((rows, LANES), F32)],
            [res_here[0 if first else 1], hidden, got[i], attn_gate, norm_scale, head_t] + list(state),
            flops=4 * rows * channels * width_piece,
            moved=6 * rows * width_piece,
        )
    sums = state[0]
    sums_got = lax.ppermute(sums, "shard", both)
    keep, send = call(
        functools.partial(norm_kernel, width_model),
        [((channels // 2, rows), F32)] * 2,
        [sums, sums_got, rows_own, rows_got],
        scratch=[pltpu.VMEM((channels, rows), F32)],
    )
    eps_got = lax.ppermute(send, "guide", both)
    fold = LANES // group
    frames = call(
        functools.partial(frame_kernel, seq_count, group),
        [((channels // fold, LANES), F32)] * seq_count,
        [chosen, keep, eps_got],
    )
    arrived = [frames[0]] + [
        lax.ppermute(frames[k], "seq", [(z, z ^ k) for z in range(seq_count)])
        for k in range(1, seq_count)
    ]
    out = call(
        functools.partial(final_kernel, seq_count, group),
        [((channels // 2, rows), F32)],
        [weight, noise[0, 0].T] + arrived,
    )[0]
    return out.T[None, None]


def fast_fits(sizes, queries, residual, w_out, w_head):
    seq_count = sizes["seq"]
    step_count, rows, width_local = queries.shape[1:]
    channels = w_head.shape[1]
    if seq_count < 2 or sizes["guide"] != 2 or sizes["shard"] != 2 or seq_count & (seq_count - 1) or step_count != 1 or rows != LANES:
        return False
    if width_local % (seq_count // 2 * HEAD_DIM) or residual.shape[3] % (4 * LANES):
        return False
    if w_out.shape[1] != residual.shape[3] or channels % (2 * SUBLANES):
        return False
    group = rows // seq_count
    if rows % seq_count or LANES % group:
        return False
    fold = LANES // group
    return channels // 2 % (fold * SUBLANES) == 0


def solution(mesh):
    sizes = dict(mesh.shape)

    def on_device(queries, key_vecs, value_vecs, residual, w_out, attn_gate, norm_shift, norm_scale, w_head, *rest):
        fits = fast_fits(sizes, queries, residual, w_out, w_head)
        plan = fast_plan if fits else general_plan
        return plan(queries, key_vecs, value_vecs, residual, w_out, attn_gate, norm_shift, norm_scale, w_head, *rest)

    return jax.shard_map(
        on_device,
        mesh=mesh,
        in_specs=(
            P("guide", "group", "seq", "shard"),
            P("guide", "group", "seq", "shard"),
            P("guide", "group", "seq", "shard"),
            P("guide", "group", "seq", "shard"),
            P("shard", "guide"),
            P("group", "shard"),
            P("group", "shard"),
            P("group", "shard"),
            P("shard", None),
            P("group", "seq", None, "guide"),
            P("group"),
            P("group", None),
        ),
        out_specs=P("group", "seq", None, "guide"),
        check_vma=False,
    )
```
